32 devices in a mesh: cell: 4 (over x, core), head: 4 (over z), ctx: 2 (over y).
Axes of the slice: x: 2, y: 2, z: 4, core: 2. Of those that a mesh axis runs over, the one named last changes fastest.
Arguments:
- inputs: bfloat16 [4, 2048, 1120], P('cell', ('head', 'ctx')), may hold values from -6 to 6
- dataset_ids: int32 [4], P('cell'), may hold values from 0 to 19
- lengths: int32 [4], P('cell'), may hold values from 1024 to 2048, as said below
- dataset_table: bfloat16 [20, 1120], replicated, may hold values from -3 to 3
- attn_gain: float32 [1120], replicated, may hold values from 0.5 to 1.5
- attn_shift: float32 [1120], replicated, may hold values from -1.5 to 1.5
- qkv_weight: bfloat16 [1120, 3360], replicated, may hold values from -0.1875 to 0.1875
- query_bias: float32 [1120], replicated, may hold values from -1.5 to 1.5
- value_bias: float32 [1120], replicated, may hold values from -1.5 to 1.5
- out_weight: bfloat16 [1120, 1120], replicated, may hold values from -3 to 3
- out_bias: float32 [1120], replicated, may hold values from -1.5 to 1.5
- mlp_gain: float32 [1120], replicated, may hold values from 0.5 to 1.5
- mlp_shift: float32 [1120], replicated, may hold values from -1.5 to 1.5
- fc_weight: bfloat16 [1120, 4480], replicated, may hold values from -0.1875 to 0.1875
- fc_bias: float32 [4480], replicated, may hold values from -1.5 to 1.5
- proj_weight: bfloat16 [4480, 1120], replicated, may hold values from -0.09375 to 0.09375
- proj_bias: float32 [1120], replicated, may hold values from -1.5 to 1.5
- cotangent: bfloat16 [4, 2048, 1120], P('cell', ('head', 'ctx')), may hold values from -6 to 6
Outputs:
- block_out: bfloat16 [4, 2048, 1120], P('cell', ('head', 'ctx'))
- input_grad: bfloat16 [4, 2048, 1120], P('cell', ('head', 'ctx'))
- table_grad: float32 [20, 1120], P(None, 'cell')
- attn_gain_grad: float32 [1120], P('cell')
- attn_shift_grad: float32 [1120], P('cell')
- qkv_weight_grad: float32 [1120, 3360], P('cell', ('head', 'ctx'))
- query_bias_grad: float32 [1120], P('cell')
- value_bias_grad: float32 [1120], P('cell')
- out_weight_grad: float32 [1120, 1120], P('cell', ('head', 'ctx'))
- out_bias_grad: float32 [1120], P('cell')
- mlp_gain_grad: float32 [1120], P('cell')
- mlp_shift_grad: float32 [1120], P('cell')
- fc_weight_grad: float32 [1120, 4480], P('cell', ('head', 'ctx'))
- fc_bias_grad: float32 [4480], P('cell')
- proj_weight_grad: float32 [4480, 1120], P('cell', ('head', 'ctx'))
- proj_bias_grad: float32 [1120], P('cell')
The draws below stay inside these ranges and needn't reach their ends.
Inputs may be any that keep to these rules, and one draw needn't show every extreme that they name: `lengths`: each cell has 1024 to 2048 valid positions at the start of its 2048; some cell fills all 2048.
All inputs are finite; a program needn't handle non-finite values.
Results may differ from the reference program's by a relative error of at most 0.015.
Values may be sent and summed in bfloat16 or wider, within the bound.
No kernel may reach another device: no remote copies, remote signals or barrier semaphores. Data moves between devices by JAX's collectives and lax.ppermute only.
A program may use at most 192 MiB of HBM per device.

```python
import math
import jax
import jax.numpy as jnp
from jax import lax

D = 1120
HEADS = 20
HD = 56
FF = 4480
L = 2048
NDS = 20
CELLS = 4


def draw_lengths(key, part):
    drawn = jax.random.randint(key, (CELLS,), L // 2, L + 1, dtype=jnp.int32)
    first = jnp.arange(CELLS, dtype=jnp.int32) == 0
    return jnp.where(first, L, drawn).astype(jnp.int32)


def place_ends(values, stream_key, least, largest):
    longest = values.shape.index(max(values.shape))
    spots = []
    for shift in (0, 1):
        where = [jax.random.randint(jax.random.fold_in(stream_key, axis), (), 0, length) for axis, length in enumerate(values.shape)]
        where[longest] = (where[longest] + shift) % values.shape[longest]
        spots.append(tuple(where))
    return values.at[spots[0]].set(least).at[spots[1]].set(largest)


def shard_levels(stream_key, dims, split, smallest, high):
    loudness, own = 1.0, jax.random.fold_in(stream_key, 6)
    for dim, blocks in split:
        draws = jnp.exp(jax.random.uniform(jax.random.fold_in(own, dim), (blocks,), jnp.float32, smallest / len(split), high / len(split)))
        loudness = loudness * jnp.repeat(draws, dims[dim] // blocks).reshape([-1 if axis == dim else 1 for axis in range(len(dims))])
    return loudness


def centred(stream_key, shape, scale, bound, shards=(), kind=jnp.bfloat16):
    values = scale * jax.random.normal(stream_key, shape, jnp.float32)
    if shards:
        values = values * shard_levels(stream_key, shape, shards, -0.22, 0.18)
    return jnp.clip(values, -bound, bound).astype(kind)


def setup_inputs(seed: int = 0) -> dict:
    seeds = jax.random.split(jax.random.key(seed), 19)
    inputs = centred(seeds[0], (CELLS, L, D), 1.0, 6.0, ((0, 4), (1, 8)))
    dataset_ids = place_ends(jax.random.randint(seeds[1], (CELLS,), 0, NDS), jax.random.fold_in(seeds[1], 1), 0, NDS - 1).astype(jnp.int32)
    lengths = draw_lengths(jax.random.fold_in(seeds[18], 71), 0)
    dataset_table = centred(seeds[3], (NDS, D), 0.5, 3.0)
    attn_gain = jnp.clip(1.0 + 0.1 * jax.random.normal(seeds[4], (D,), jnp.float32), 0.5, 1.5)
    attn_shift = centred(seeds[5], (D,), 0.3, 1.5, (), jnp.float32)
    qkv_weight = centred(seeds[6], (D, 3 * D), D ** -0.5, 0.1875)
    query_bias = centred(seeds[7], (D,), 0.3, 1.5, (), jnp.float32)
    value_bias = centred(seeds[8], (D,), 0.3, 1.5, (), jnp.float32)
    out_weight = centred(seeds[9], (D, D), (max(D // 256, 1)) ** -0.5, 3.0)
    out_bias = centred(seeds[10], (D,), 0.3, 1.5, (), jnp.float32)
    mlp_gain = jnp.clip(1.0 + 0.1 * jax.random.normal(seeds[11], (D,), jnp.float32), 0.5, 1.5)
    mlp_shift = centred(seeds[12], (D,), 0.3, 1.5, (), jnp.float32)
    fc_weight = centred(seeds[13], (D, FF), D ** -0.5, 0.1875)
    fc_bias = centred(seeds[14], (FF,), 0.3, 1.5, (), jnp.float32)
    proj_weight = centred(seeds[15], (FF, D), FF ** -0.5, 0.09375)
    proj_bias = centred(seeds[16], (D,), 0.3, 1.5, (), jnp.float32)
    cotangent = centred(seeds[17], (CELLS, L, D), 1.0, 6.0, ((0, 4), (1, 8)))
    return dict(inputs=inputs, dataset_ids=dataset_ids, lengths=lengths, dataset_table=dataset_table, attn_gain=attn_gain, attn_shift=attn_shift, qkv_weight=qkv_weight, query_bias=query_bias, value_bias=value_bias, out_weight=out_weight, out_bias=out_bias, mlp_gain=mlp_gain, mlp_shift=mlp_shift, fc_weight=fc_weight, fc_bias=fc_bias, proj_weight=proj_weight, proj_bias=proj_bias, cotangent=cotangent)


@jax.custom_vjp
def low(v):
    return lax.optimization_barrier(v.astype(jnp.bfloat16)).astype(jnp.float32)

@jax.custom_vjp
def low_back(v):
    return v

def low_keep(v):
    return (low(v), None)

def low_pass(kept, grad):
    return (grad,)

def back_keep(v):
    return (v, None)

def back_low(kept, grad):
    return (low(grad),)
low.defvjp(low_keep, low_pass)
low_back.defvjp(back_keep, back_low)
epsilon = 1e-05
precise = lax.Precision.HIGHEST

def layer_norm(values, gain_row, shift_row):
    center = values - lax.optimization_barrier(jnp.mean(values, axis=-1, keepdims=True))
    spread = lax.optimization_barrier(jnp.mean(center * center, axis=-1, keepdims=True))
    return center * lax.rsqrt(spread + epsilon) * gain_row + shift_row

def cell_attention(cell_query, cell_keys, cell_values, seq_len):
    block_rows = min(512, L)
    positions = jnp.arange(L, dtype=jnp.int32)
    key_valid = positions < seq_len
    score_scale = 1.0 / math.sqrt(HD)

    def one_block(block_index):
        offset = block_index * block_rows
        queries = lax.dynamic_slice_in_dim(cell_query, offset, block_rows, 0)
        query_pos = offset + jnp.arange(block_rows, dtype=jnp.int32)
        scores = jnp.einsum('qhd,khd->hqk', queries, cell_keys, precision=precise) * score_scale
        scores = low_back(scores)
        allowed = (positions[None, :] <= query_pos[:, None]) & key_valid[None, :]
        scores = jnp.where(allowed[None], scores, -1e+30)
        row_max = lax.optimization_barrier(jnp.max(scores, axis=-1, keepdims=True))
        powers = jnp.exp(scores - row_max)
        weights = low(powers / lax.optimization_barrier(jnp.sum(powers, axis=-1, keepdims=True)))
        return jnp.einsum('hqk,khd->qhd', weights, cell_values, precision=precise)
    blocks = lax.map(jax.checkpoint(one_block), jnp.arange(L // block_rows, dtype=jnp.int32))
    return blocks.reshape(L, HEADS * HD)

def attend_items(cell_items):
    return cell_attention(cell_items[0], cell_items[1], cell_items[2], cell_items[3])

def forward(inputs, dataset_table, attn_gain, attn_shift, qkv_weight, query_bias, value_bias, out_weight, out_bias, mlp_gain, mlp_shift, fc_weight, fc_bias, proj_weight, proj_bias, dataset_ids, lengths):
    one_hot = (dataset_ids[:, None] == jnp.arange(NDS, dtype=jnp.int32)[None, :]).astype(jnp.float32)
    embedded = jnp.dot(one_hot, dataset_table, precision=precise)
    residual = inputs + embedded[:, None, :]
    normed = low(layer_norm(residual, attn_gain, attn_shift))
    mixed_qkv = jnp.einsum('cld,de->cle', normed, qkv_weight, precision=precise)
    bias_row = jnp.concatenate([query_bias, jnp.zeros_like(query_bias), value_bias])
    mixed_qkv = low(low_back(mixed_qkv + bias_row))
    shaped = mixed_qkv.reshape(CELLS, L, 3, HEADS, HD)
    attended = lax.map(jax.checkpoint(attend_items), (shaped[:, :, 0], shaped[:, :, 1], shaped[:, :, 2], lengths))
    attended = low(low_back(attended))
    attn_out = low_back(jnp.einsum('cld,de->cle', attended, out_weight, precision=precise) + out_bias)
    middle = residual + attn_out
    mlp_normed = low(layer_norm(middle, mlp_gain, mlp_shift))
    hidden = low_back(jnp.einsum('cld,df->clf', mlp_normed, fc_weight, precision=precise) + fc_bias)
    active = low(jax.nn.gelu(hidden, approximate=True))
    branch = low_back(jnp.einsum('clf,fd->cld', active, proj_weight, precision=precise) + proj_bias)
    return middle + branch

def reference(inputs, dataset_ids, lengths, dataset_table, attn_gain, attn_shift, qkv_weight, query_bias, value_bias, out_weight, out_bias, mlp_gain, mlp_shift, fc_weight, fc_bias, proj_weight, proj_bias, cotangent):
    floats = [array.astype(jnp.float32) for array in (inputs, dataset_table, attn_gain, attn_shift, qkv_weight, query_bias, value_bias, out_weight, out_bias, mlp_gain, mlp_shift, fc_weight, fc_bias, proj_weight, proj_bias)]

    def apply_layer(*params):
        return forward(*params, dataset_ids, lengths)
    block_out, pull_back = jax.vjp(apply_layer, *floats)
    grads = pull_back(cotangent.astype(jnp.float32))
    return (block_out.astype(jnp.bfloat16), grads[0].astype(jnp.bfloat16), grads[1], grads[2], grads[3], grads[4], grads[5], grads[6], grads[7], grads[8], grads[9], grads[10], grads[11], grads[12], grads[13], grads[14])
```

```python
import math

import jax
import jax.numpy as jnp
from jax import lax
from jax.experimental import pallas as pl
from jax.experimental.pallas import tpu as pltpu
from jax.sharding import PartitionSpec as P

HEADS = 20
HD = 56


epsilon = 1e-05
MASKED = -1e30
LOG2E = math.log2(math.e)


def layer_norm(values, gain_row, shift_row):
    center = values - jnp.mean(values, axis=-1, keepdims=True)
    spread = jnp.mean(center * center, axis=-1, keepdims=True)
    return center * lax.rsqrt(spread + epsilon) * gain_row + shift_row


def gelu_tanh(values):
    return jax.nn.gelu(values, approximate=True)


def swap(values, axis, bit):
    return lax.ppermute(values, axis, [(i, i ^ bit) for i in range(lax.axis_size(axis))])


def bits_of(axis):
    size, bit, found = lax.axis_size(axis), 1, []
    while bit < size:
        found.append((axis, bit))
        bit *= 2
    return found


def nn(a, b):
    return jnp.dot(a, b, preferred_element_type=jnp.float32)


def nt(a, b):
    return lax.dot_general(a, b, (((1,), (1,)), ((), ())), preferred_element_type=jnp.float32)


def weight_blocks(pairs, left_ids, right_ids):
    count = left_ids.shape[0]
    pair_count = len(pairs)
    rows = pairs[0][0].shape[1]
    cols = sum(r.shape[2] for _, r in pairs)

    def kernel(li, ri, *refs):
        i = pl.program_id(0)
        out = refs[-1]
        parts = []
        for p in range(pair_count):
            parts.append(nn(refs[2 * p][li[i]], refs[2 * p + 1][ri[i]]))
        whole = parts[0] if pair_count == 1 else jnp.concatenate(parts, axis=-1)
        out[0] = whole.astype(jnp.bfloat16)

    flat = [x for pair in pairs for x in pair]
    return pl.pallas_call(
        kernel,
        out_shape=jax.ShapeDtypeStruct((count, rows, cols), jnp.bfloat16),
        grid_spec=pltpu.PrefetchScalarGridSpec(
            num_scalar_prefetch=2,
            grid=(count,),
            in_specs=[
                pl.BlockSpec(x.shape, lambda i, li, ri: (0, 0, 0), pipeline_mode=pl.Buffered(1))
                for x in flat
            ],
            out_specs=pl.BlockSpec((1, rows, cols), lambda i, li, ri: (i, 0, 0)),
        ),
        name="weight_blocks",
    )(left_ids, right_ids, *flat)


def relative_ids(steps):
    count = 1
    for axis, _ in steps:
        count *= 2
    places = jnp.arange(count, dtype=jnp.int32)
    rel = {"cell": jnp.zeros_like(places), "head": jnp.zeros_like(places), "ctx": jnp.zeros_like(places)}
    for s, (axis, bit) in enumerate(steps):
        on = (places >> (len(steps) - 1 - s)) & 1
        rel[axis] = rel[axis] + on * bit
    cell_ids = rel["cell"] ^ lax.axis_index("cell")
    part_ids = (rel["head"] ^ lax.axis_index("head")) * lax.axis_size("ctx") + (
        rel["ctx"] ^ lax.axis_index("ctx")
    )
    return cell_ids, part_ids


def add_up(kept, got):
    return kept.astype(jnp.float32) + got.astype(jnp.float32)


def scatter_sum(kept, sent, steps):
    total = None
    for s, (axis, bit) in enumerate(steps):
        if s:
            total = total.astype(jnp.bfloat16)
            half = total.shape[0] // 2
            kept, sent = total[:half], total[half:]
        total = add_up(kept, swap(sent, axis, bit))
    return total[0]


def head_dims(qkv_ref):
    width = qkv_ref.shape[-1] // 3
    return width, width // HD


def chunk_mask(start, seq_len, query_start, rows, cols):
    key_pos = start + lax.broadcasted_iota(jnp.int32, (rows, cols), 0)
    if query_start is None:
        return key_pos < seq_len
    query_pos = query_start + lax.broadcasted_iota(jnp.int32, (rows, cols), 1)
    return (key_pos < seq_len) & (key_pos <= query_pos)


def sweep(i, half, seq_len, rows, visit, blocks):
    def own(j, carry):
        visit(j, (2 * j + half) * rows, False)
        return carry

    def other(j, carry):
        visit(blocks + j, (2 * j + 1 - half) * rows, False)
        return carry

    span = 2 * rows
    own_count = jnp.minimum(i, (seq_len - half * rows + span - 1) // span)
    other_count = jnp.minimum(i + half, (seq_len - (1 - half) * rows + span - 1) // span)
    lax.fori_loop(0, other_count, other, 0)
    lax.fori_loop(0, own_count, own, 0)
    visit(i, (2 * i + half) * rows, True)


def attend_kernel(info, qkv, kv_other, out, out_t, logs, q_t, k_n, v_t, acc, m_ref, l_ref):
    width, heads = head_dims(qkv)
    blocks, rows = q_t.shape[0], q_t.shape[-1]
    seq_len, half = info[0], info[1]
    factor = LOG2E / math.sqrt(HD)

    def prepare(b, carry):
        at = pl.ds(pl.multiple_of(b * rows, rows), rows)
        mine = qkv[at, :]
        mine_t = mine.astype(jnp.float32).T
        theirs = kv_other[at, :]
        theirs_t = theirs[:, width:].astype(jnp.float32).T
        for h in range(heads):
            lo, hi = h * HD, (h + 1) * HD
            q_t[b, h] = mine_t[lo:hi].astype(jnp.bfloat16)
            v_t[b, h] = mine_t[2 * width + lo : 2 * width + hi].astype(jnp.bfloat16)
            k_n[b, h] = mine[:, width + lo : width + hi]
            v_t[blocks + b, h] = theirs_t[lo:hi].astype(jnp.bfloat16)
            k_n[blocks + b, h] = theirs[:, lo:hi]
        return carry

    lax.fori_loop(0, blocks, prepare, 0)

    def block(i, carry):
        acc[...] = jnp.zeros_like(acc)
        m_ref[...] = jnp.full_like(m_ref, MASKED)
        l_ref[...] = jnp.zeros_like(l_ref)

        def visit(j, start, diagonal):
            query_start = (2 * i + half) * rows if diagonal else None
            allowed = chunk_mask(start, seq_len, query_start, rows, rows)
            for h in range(heads):
                s = nn(k_n[j, h], q_t[i, h]) * factor
                s = jnp.where(allowed, s, MASKED)
                old = m_ref[h]
                new = jnp.maximum(old, jnp.max(s, axis=0, keepdims=True))
                shrink = jnp.exp2(old - new)
                p = jnp.exp2(s - new)
                l_ref[h] = l_ref[h] * shrink + jnp.sum(p, axis=0, keepdims=True)
                acc[h] = acc[h] * shrink + nn(v_t[j, h], p.astype(jnp.bfloat16))
                m_ref[h] = new

        sweep(i, half, seq_len, rows, visit, blocks)
        at = pl.ds(pl.multiple_of(i * rows, rows), rows)
        for h in range(heads):
            out_t[i, h * HD : (h + 1) * HD, :] = acc[h] / l_ref[h]
            logs[i, h] = m_ref[h] + jnp.log2(l_ref[h])
        out[at, :] = out_t[i].T.astype(jnp.bfloat16)
        return carry

    lax.fori_loop(0, blocks, block, 0)


def vmem_specs(count):
    return [pl.BlockSpec(memory_space=pltpu.VMEM)] * count


def attend(info, qkv, kv_other, blocks):
    rows_all, wide = qkv.shape
    width = wide // 3
    heads, rows = width // HD, rows_all // blocks
    bf, f32 = jnp.bfloat16, jnp.float32
    pairs = blocks * rows * rows * (blocks + 1)
    return pl.pallas_call(
        attend_kernel,
        out_shape=(
            jax.ShapeDtypeStruct((rows_all, width), bf),
            jax.ShapeDtypeStruct((blocks, width, rows), f32),
            jax.ShapeDtypeStruct((blocks, heads, 1, rows), f32),
        ),
        in_specs=[pl.BlockSpec(memory_space=pltpu.SMEM)] + vmem_specs(2),
        out_specs=tuple(vmem_specs(3)),
        scratch_shapes=[
            pltpu.VMEM((blocks, heads, HD, rows), bf),
            pltpu.VMEM((2 * blocks, heads, rows, HD), bf),
            pltpu.VMEM((2 * blocks, heads, HD, rows), bf),
            pltpu.VMEM((heads, HD, rows), f32),
            pltpu.VMEM((heads, 1, rows), f32),
            pltpu.VMEM((heads, 1, rows), f32),
        ],
        cost_estimate=pl.CostEstimate(
            flops=20 * 1024 * 1024 * 1024, transcendentals=pairs * heads, bytes_accessed=8 * 1024 * 1024
        ),
        name="attend",
    )(info, qkv, kv_other)


def back_kernel(
    info, qkv, kv_other, grad, out_t, logs,
    dq, dkv, dkv_other,
    q_t, g_t, k_n, k_t, v_n, dq_t, dk_t, dv_t, delta,
):
    width, heads = head_dims(qkv)
    blocks, rows = q_t.shape[0], q_t.shape[-1]
    seq_len, half = info[0], info[1]
    scale = 1.0 / math.sqrt(HD)
    factor = LOG2E * scale

    def prepare(b, carry):
        at = pl.ds(pl.multiple_of(b * rows, rows), rows)
        mine = qkv[at, :]
        mine_t = mine[:, : 2 * width].astype(jnp.float32).T
        grad_t = grad[at, :].astype(jnp.float32).T
        theirs = kv_other[at, :]
        theirs_t = theirs[:, :width].astype(jnp.float32).T
        for h in range(heads):
            lo, hi = h * HD, (h + 1) * HD
            q_t[b, h] = mine_t[lo:hi].astype(jnp.bfloat16)
            g_t[b, h] = grad_t[lo:hi].astype(jnp.bfloat16)
            delta[b, h] = jnp.sum(grad_t[lo:hi] * out_t[b, lo:hi], axis=0, keepdims=True)
            k_t[b, h] = mine_t[width + lo : width + hi].astype(jnp.bfloat16)
            k_n[b, h] = mine[:, width + lo : width + hi]
            v_n[b, h] = mine[:, 2 * width + lo : 2 * width + hi]
            k_t[blocks + b, h] = theirs_t[lo:hi].astype(jnp.bfloat16)
            k_n[blocks + b, h] = theirs[:, lo:hi]
            v_n[blocks + b, h] = theirs[:, width + lo : width + hi]
        return carry

    lax.fori_loop(0, blocks, prepare, 0)
    dk_t[...] = jnp.zeros_like(dk_t)
    dv_t[...] = jnp.zeros_like(dv_t)

    def block(i, carry):
        dq_t[...] = jnp.zeros_like(dq_t)

        def visit(j, start, diagonal):
            query_start = (2 * i + half) * rows if diagonal else None
            allowed = chunk_mask(start, seq_len, query_start, rows, rows)
            for h in range(heads):
                at = slice(h * HD, (h + 1) * HD)
                s = nn(k_n[j, h], q_t[i, h]) * factor - logs[i, h]
                p = jnp.exp2(jnp.where(allowed, s, MASKED))
                dv_t[j, at] += nt(g_t[i, h], p.astype(jnp.bfloat16))
                dp = nn(v_n[j, h], g_t[i, h])
                ds = (p * (dp - delta[i, h])).astype(jnp.bfloat16)
                dq_t[at] += nn(k_t[j, h], ds)
                dk_t[j, at] += nt(q_t[i, h], ds)

        sweep(i, half, seq_len, rows, visit, blocks)
        at = pl.ds(pl.multiple_of(i * rows, rows), rows)
        dq[at, :] = (dq_t[...] * scale).T.astype(dq.dtype)
        return carry

    lax.fori_loop(0, blocks, block, 0)

    def finish(b, carry):
        at = pl.ds(pl.multiple_of(b * rows, rows), rows)
        dkv[at, :width] = (dk_t[b] * scale).T.astype(dkv.dtype)
        dkv[at, width:] = dv_t[b].T.astype(dkv.dtype)
        dkv_other[at, :width] = (dk_t[blocks + b] * scale).T.astype(dkv_other.dtype)
        dkv_other[at, width:] = dv_t[blocks + b].T.astype(dkv_other.dtype)
        return carry

    lax.fori_loop(0, blocks, finish, 0)


def attend_back(info, qkv, kv_other, grad, out_t, logs, blocks):
    rows_all, wide = qkv.shape
    width = wide // 3
    heads, rows = width // HD, rows_all // blocks
    bf, f32 = jnp.bfloat16, jnp.float32
    pairs = blocks * rows * rows * (blocks + 1)
    return pl.pallas_call(
        back_kernel,
        out_shape=(
            jax.ShapeDtypeStruct((rows_all, width), bf),
            jax.ShapeDtypeStruct((rows_all, 2 * width), bf),
            jax.ShapeDtypeStruct((rows_all, 2 * width), bf),
        ),
        in_specs=[pl.BlockSpec(memory_space=pltpu.SMEM)] + vmem_specs(5),
        out_specs=tuple(vmem_specs(3)),
        scratch_shapes=[
            pltpu.VMEM((blocks, heads, HD, rows), bf),
            pltpu.VMEM((blocks, heads, HD, rows), bf),
            pltpu.VMEM((2 * blocks, heads, rows, HD), bf),
            pltpu.VMEM((2 * blocks, heads, HD, rows), bf),
            pltpu.VMEM((2 * blocks, heads, rows, HD), bf),
            pltpu.VMEM((width, rows), f32),
            pltpu.VMEM((2 * blocks, width, rows), f32),
            pltpu.VMEM((2 * blocks, width, rows), f32),
            pltpu.VMEM((blocks, heads, 1, rows), f32),
        ],
        cost_estimate=pl.CostEstimate(
            flops=60 * 1024 * 1024 * 1024, transcendentals=pairs * heads, bytes_accessed=8 * 1024 * 1024
        ),
        name="attend_back",
    )(info, qkv, kv_other, grad, out_t, logs)


def column_blocks(values, count):
    return values.reshape(values.shape[0], count, -1).transpose(1, 0, 2)


def row_blocks(values, count):
    return values.reshape(values.shape[0], count, -1).transpose(1, 2, 0)


def block_sum(pairs, by_cell_left, steps):
    cell_ids, part_ids = relative_ids(steps)
    left, right = (cell_ids, part_ids) if by_cell_left else (part_ids, cell_ids)
    half = left.shape[0] // 2
    sent = weight_blocks(pairs, left[half:], right[half:])
    kept = weight_blocks(pairs, left[:half], right[:half])
    return kept, sent


def body(
    inputs,
    dataset_ids,
    lengths,
    dataset_table,
    attn_gain,
    attn_shift,
    qkv_weight,
    query_bias,
    value_bias,
    out_weight,
    out_bias,
    mlp_gain,
    mlp_shift,
    fc_weight,
    fc_bias,
    proj_weight,
    proj_bias,
    cotangent,
):
    cell_count, row_count, model_width = inputs.shape
    cells = lax.axis_size("cell")
    groups = lax.axis_size("head")
    halves = lax.axis_size("ctx")
    parts = groups * halves
    half_index = lax.axis_index("ctx")
    head_width = HEADS // groups * HD
    token_count = cell_count * row_count
    ctx_rows = groups * row_count
    cell_steps, ctx_steps, head_steps = bits_of("cell"), bits_of("ctx"), bits_of("head")[::-1]
    steps_x = cell_steps + ctx_steps + head_steps
    steps_y = cell_steps[:1] + ctx_steps + cell_steps[1:] + head_steps
    one_hot = (
        dataset_ids[:, None] == jnp.arange(dataset_table.shape[0], dtype=jnp.int32)[None, :]
    ).astype(jnp.bfloat16)
    embedded = jnp.dot(one_hot, dataset_table, preferred_element_type=jnp.float32)
    residual = (inputs.astype(jnp.float32) + embedded[:, None, :]).reshape(token_count, model_width)
    normed = layer_norm(residual, attn_gain, attn_shift).astype(jnp.bfloat16)
    mixed_qkv = jnp.dot(normed, qkv_weight, preferred_element_type=jnp.float32)
    bias_row = jnp.concatenate([query_bias, jnp.zeros_like(query_bias), value_bias])
    mixed_qkv = (mixed_qkv + bias_row).astype(jnp.bfloat16)

    def to_heads(values):
        sections = values.shape[1] // model_width
        values = values.reshape(cell_count, row_count, sections, groups, head_width)
        values = values.transpose(3, 0, 1, 2, 4).reshape(groups, cell_count, row_count, -1)
        values = lax.all_to_all(values, "head", split_axis=0, concat_axis=0, tiled=True)
        return values.transpose(1, 0, 2, 3).reshape(cell_count, ctx_rows, -1)

    def to_rows(values):
        sections = values.shape[-1] // head_width
        values = values.reshape(cell_count, groups, row_count, -1).transpose(1, 0, 2, 3)
        values = lax.all_to_all(values, "head", split_axis=0, concat_axis=0, tiled=True)
        values = values.reshape(groups, cell_count, row_count, sections, head_width)
        return values.transpose(1, 2, 3, 0, 4).reshape(token_count, sections * model_width)

    qkv_heads = to_heads(mixed_qkv)
    kv_other = swap(qkv_heads[:, :, head_width:], "ctx", 1)
    infos = [jnp.stack([lengths[n], half_index.astype(jnp.int32)]) for n in range(cell_count)]
    runs = [attend(infos[n], qkv_heads[n], kv_other[n], groups) for n in range(cell_count)]
    attended = jnp.stack([r[0] for r in runs])
    attended_rows = to_rows(attended)
    attn_out = jnp.dot(attended_rows, out_weight, preferred_element_type=jnp.float32) + out_bias
    middle = residual + attn_out
    mlp_normed = layer_norm(middle, mlp_gain, mlp_shift).astype(jnp.bfloat16)
    hidden = jnp.dot(mlp_normed, fc_weight, preferred_element_type=jnp.float32) + fc_bias
    active = gelu_tanh(hidden).astype(jnp.bfloat16)
    branch = jnp.dot(active, proj_weight, preferred_element_type=jnp.float32) + proj_bias
    block_out = (middle + branch).astype(jnp.bfloat16).reshape(cell_count, row_count, model_width)
    grad_low = cotangent.reshape(token_count, model_width)
    grad_top = grad_low.astype(jnp.float32)
    proj_bias_grad = jnp.sum(grad_top, axis=0)
    active_grad = jnp.einsum("nd,fd->nf", grad_low, proj_weight, preferred_element_type=jnp.float32)
    gelu_pull = jax.vjp(gelu_tanh, hidden)[1]
    hidden_grad = gelu_pull(active_grad)[0].astype(jnp.bfloat16)
    fc_bias_grad = jnp.sum(hidden_grad, axis=0, dtype=jnp.float32)
    normed_grad = jnp.einsum(
        "nf,df->nd", hidden_grad, fc_weight, preferred_element_type=jnp.float32
    )
    mlp_pull = jax.vjp(layer_norm, middle, mlp_gain, mlp_shift)[1]
    middle_part, mlp_gain_grad, mlp_shift_grad = mlp_pull(normed_grad)
    middle_grad = grad_top + middle_part
    middle_low = middle_grad.astype(jnp.bfloat16)
    out_bias_grad = jnp.sum(middle_low, axis=0, dtype=jnp.float32)
    attended_grad = jnp.einsum(
        "ne,de->nd", middle_low, out_weight, preferred_element_type=jnp.float32
    ).astype(jnp.bfloat16)
    grad_heads = to_heads(attended_grad)

    fc_kept, fc_sent = block_sum(
        [(row_blocks(mlp_normed, cells), column_blocks(hidden_grad, parts))], True, steps_x
    )
    po_kept, po_sent = block_sum(
        [
            (row_blocks(grad_low, parts), column_blocks(active, cells)),
            (row_blocks(middle_low, parts), column_blocks(attended_rows, cells)),
        ],
        False,
        steps_y,
    )
    grad_heads, fc_kept, fc_sent, po_kept, po_sent = lax.optimization_barrier(
        (grad_heads, fc_kept, fc_sent, po_kept, po_sent)
    )
    fc_weight_grad = scatter_sum(fc_kept, fc_sent, steps_x)
    po_grad = scatter_sum(po_kept, po_sent, steps_y)
    proj_rows = active.shape[1] // cells
    proj_weight_grad = po_grad[:, :proj_rows].T
    out_weight_grad = po_grad[:, proj_rows:].T

    backs = [
        attend_back(
            infos[n], qkv_heads[n], kv_other[n], grad_heads[n], runs[n][1], runs[n][2], groups
        )
        for n in range(cell_count)
    ]
    dq = jnp.stack([b[0] for b in backs])
    dkv = jnp.stack([b[1] for b in backs])
    dkv_got = swap(jnp.stack([b[2] for b in backs]), "ctx", 1)
    dkv = add_up(dkv, dkv_got).astype(jnp.bfloat16)
    qkv_grad = to_rows(jnp.concatenate([dq, dkv], axis=-1))
    qkv_kept, qkv_sent = block_sum(
        [(row_blocks(normed, cells), column_blocks(qkv_grad, parts))], True, steps_x
    )
    qkv_weight_grad = scatter_sum(qkv_kept, qkv_sent, steps_x)
    column_sums = jnp.sum(qkv_grad, axis=0, dtype=jnp.float32)
    query_bias_grad = column_sums[:model_width]
    value_bias_grad = column_sums[2 * model_width :]
    normed_back = jnp.einsum("ne,de->nd", qkv_grad, qkv_weight, preferred_element_type=jnp.float32)
    attn_pull = jax.vjp(layer_norm, residual, attn_gain, attn_shift)[1]
    residual_part, attn_gain_grad, attn_shift_grad = attn_pull(normed_back)
    residual_grad = middle_grad + residual_part
    input_grad = residual_grad.astype(jnp.bfloat16).reshape(cell_count, row_count, model_width)
    cell_totals = jnp.sum(residual_grad.reshape(cell_count, row_count, model_width), axis=1)
    table_grad = jnp.dot(
        one_hot.astype(jnp.float32).T, cell_totals, precision=lax.Precision.HIGHEST
    )

    width = model_width // cells
    vectors = [
        attn_gain_grad,
        attn_shift_grad,
        query_bias_grad,
        value_bias_grad,
        out_bias_grad,
        mlp_gain_grad,
        mlp_shift_grad,
        proj_bias_grad,
    ]
    fc_rows = fc_bias_grad.shape[0] // model_width
    packed = jnp.concatenate(
        [table_grad.reshape(-1, cells, width).transpose(1, 0, 2)]
        + [v.reshape(cells, 1, width) for v in vectors]
        + [fc_bias_grad.reshape(cells, fc_rows, width)],
        axis=1,
    )
    cell_index = lax.axis_index("cell")
    for axis, bit in cell_steps[::-1]:
        on = (cell_index // bit) % 2
        half = packed.shape[0] // 2
        kept = lax.dynamic_slice_in_dim(packed, on * half, half, 0)
        sent = lax.dynamic_slice_in_dim(packed, (1 - on) * half, half, 0)
        packed = kept + swap(sent, axis, bit)
    for axis, bit in ctx_steps + head_steps:
        packed = packed + swap(packed, axis, bit)
    packed = packed[0]
    datasets = dataset_table.shape[0]
    table_grad = packed[:datasets]
    (
        attn_gain_grad,
        attn_shift_grad,
        query_bias_grad,
        value_bias_grad,
        out_bias_grad,
        mlp_gain_grad,
        mlp_shift_grad,
        proj_bias_grad,
    ) = [packed[datasets + n] for n in range(len(vectors))]
    fc_bias_grad = packed[datasets + len(vectors) :].reshape(-1)
    return (
        block_out,
        input_grad,
        table_grad,
        attn_gain_grad,
        attn_shift_grad,
        qkv_weight_grad,
        query_bias_grad,
        value_bias_grad,
        out_weight_grad,
        out_bias_grad,
        mlp_gain_grad,
        mlp_shift_grad,
        fc_weight_grad,
        fc_bias_grad,
        proj_weight_grad,
        proj_bias_grad,
    )


def solution(mesh):
    in_specs = (
        P("cell", ("head", "ctx"), None),
        P("cell"),
        P("cell"),
        P(),
        P(),
        P(),
        P(),
        P(),
        P(),
        P(),
        P(),
        P(),
        P(),
        P(),
        P(),
        P(),
        P(),
        P("cell", ("head", "ctx"), None),
    )
    out_specs = (
        P("cell", ("head", "ctx"), None),
        P("cell", ("head", "ctx"), None),
        P(None, "cell"),
        P("cell"),
        P("cell"),
        P("cell", ("head", "ctx")),
        P("cell"),
        P("cell"),
        P("cell", ("head", "ctx")),
        P("cell"),
        P("cell"),
        P("cell"),
        P("cell", ("head", "ctx")),
        P("cell"),
        P("cell", ("head", "ctx")),
        P("cell"),
    )
    return jax.shard_map(body, mesh=mesh, in_specs=in_specs, out_specs=out_specs, check_vma=False)
```

```python
import math

import jax
import jax.numpy as jnp
from jax import lax
from jax.experimental import pallas as pl
from jax.experimental.pallas import tpu as pltpu
from jax.sharding import PartitionSpec as P
import numpy as np


HEADS = 20
HD = 56


epsilon = 1e-05
MASKED = -1e30
LOG2E = math.log2(math.e)


def layer_norm(values, gain_row, shift_row):
    center = values - jnp.mean(values, axis=-1, keepdims=True)
    spread = jnp.mean(center * center, axis=-1, keepdims=True)
    return center * lax.rsqrt(spread + epsilon) * gain_row + shift_row


def gelu_tanh(values):
    return jax.nn.gelu(values, approximate=True)


def swap(values, axis, bit):
    return lax.ppermute(values, axis, [(i, i ^ bit) for i in range(lax.axis_size(axis))])


def bits_of(axis):
    size, bit, found = lax.axis_size(axis), 1, []
    while bit < size:
        found.append((axis, bit))
        bit *= 2
    return found


def nn(a, b):
    return jnp.dot(a, b, preferred_element_type=jnp.float32)


def nt(a, b):
    return lax.dot_general(a, b, (((1,), (1,)), ((), ())), preferred_element_type=jnp.float32)


def weight_blocks(left, right, by_cell_left, y_first):
    cells, groups, halves = lax.axis_size("cell"), lax.axis_size("head"), lax.axis_size("ctx")
    parts, half_cells = groups * halves, cells // 2
    steps = bits_of("cell")
    rel = np.zeros((cells,), np.int32)
    for s, (_, bit) in enumerate(steps):
        rel += ((np.arange(cells) >> (len(steps) - 1 - s)) & 1).astype(np.int32) * bit
    cell_ids = jnp.asarray(rel) ^ lax.axis_index("cell")
    places = jnp.arange(parts, dtype=jnp.int32)
    part_ids = ((places % groups) ^ lax.axis_index("head")) * halves + (
        (places // groups) ^ lax.axis_index("ctx")
    )
    rows, cols = left.shape[1], right.shape[2]

    def kernel(ci, pi, left_ref, right_ref, kept, sent):
        part = pi[pl.program_id(0)]
        for n in range(cells):
            cell = ci[n]
            out, at = (kept, n) if n < half_cells else (sent, n - half_cells)
            if by_cell_left:
                block = nn(left_ref[cell], right_ref[part])
            else:
                block = nn(left_ref[part], right_ref[cell])
            if y_first:
                out[0, at, 0] = block.astype(jnp.bfloat16)
            else:
                out[at, 0] = block.astype(jnp.bfloat16)

    if y_first:
        shape = (halves, half_cells, groups, rows, cols)
        spec = pl.BlockSpec(
            (1, half_cells, 1, rows, cols), lambda i, ci, pi: (i // groups, 0, i % groups, 0, 0)
        )
    else:
        shape = (half_cells, parts, rows, cols)
        spec = pl.BlockSpec((half_cells, 1, rows, cols), lambda i, ci, pi: (0, i, 0, 0))
    whole = [
        pl.BlockSpec(x.shape, lambda i, ci, pi: (0, 0, 0), pipeline_mode=pl.Buffered(1))
        for x in (left, right)
    ]
    kept, sent = pl.pallas_call(
        kernel,
        out_shape=[jax.ShapeDtypeStruct(shape, jnp.bfloat16)] * 2,
        grid_spec=pltpu.PrefetchScalarGridSpec(
            num_scalar_prefetch=2, grid=(parts,), in_specs=whole, out_specs=[spec, spec]
        ),
        name="weight_blocks",
    )(cell_ids, part_ids, left, right)
    return kept.reshape(-1, rows, cols), sent.reshape(-1, rows, cols)


def add_up(kept, got):
    return kept.astype(jnp.float32) + got.astype(jnp.float32)


def scatter_sum(kept, sent, steps):
    total = None
    for s, (axis, bit) in enumerate(steps):
        if s:
            total = total.astype(jnp.bfloat16)
            half = total.shape[0] // 2
            kept, sent = total[:half], total[half:]
        got = swap(sent, axis, bit)
        total = add_up(kept, got)
    return total[0]


def head_dims(qkv_ref):
    width = qkv_ref.shape[-1] // 3
    return width, width // HD


def chunk_mask(start, seq_len, query_start, rows, cols):
    key_pos = start + lax.broadcasted_iota(jnp.int32, (rows, cols), 0)
    if query_start is None:
        return key_pos < seq_len
    query_pos = query_start + lax.broadcasted_iota(jnp.int32, (rows, cols), 1)
    return (key_pos < seq_len) & (key_pos <= query_pos)


def sweep(i, half, seq_len, rows, visit, blocks):
    def own(j, carry):
        visit(j, (2 * j + half) * rows, False)
        return carry

    def other(j, carry):
        visit(blocks + j, (2 * j + 1 - half) * rows, False)
        return carry

    span = 2 * rows
    own_count = jnp.minimum(i, (seq_len - half * rows + span - 1) // span)
    other_count = jnp.minimum(i + half, (seq_len - (1 - half) * rows + span - 1) // span)
    lax.fori_loop(0, other_count, other, 0)
    lax.fori_loop(0, own_count, own, 0)
    visit(i, (2 * i + half) * rows, True)


def attend_kernel(info, qkv, kv_other, out, out_t, logs, q_t, k_n, v_t, acc, m_ref, l_ref):
    width, heads = head_dims(qkv)
    blocks, rows = q_t.shape[0], q_t.shape[-1]
    seq_len, half = info[0], info[1]
    factor = LOG2E / math.sqrt(HD)

    def prepare(b, carry):
        at = pl.ds(pl.multiple_of(b * rows, rows), rows)
        mine = qkv[at, :]
        mine_t = mine.astype(jnp.float32).T
        theirs = kv_other[at, :]
        theirs_t = theirs[:, width:].astype(jnp.float32).T
        for h in range(heads):
            lo, hi = h * HD, (h + 1) * HD
            q_t[b, h] = mine_t[lo:hi].astype(jnp.bfloat16)
            v_t[b, h] = mine_t[2 * width + lo : 2 * width + hi].astype(jnp.bfloat16)
            k_n[b, h] = mine[:, width + lo : width + hi]
            v_t[blocks + b, h] = theirs_t[lo:hi].astype(jnp.bfloat16)
            k_n[blocks + b, h] = theirs[:, lo:hi]
        return carry

    lax.fori_loop(0, blocks, prepare, 0)

    def block(i, carry):
        acc[...] = jnp.zeros_like(acc)
        m_ref[...] = jnp.full_like(m_ref, MASKED)
        l_ref[...] = jnp.zeros_like(l_ref)

        def visit(j, start, diagonal):
            query_start = (2 * i + half) * rows if diagonal else None
            allowed = chunk_mask(start, seq_len, query_start, rows, rows)
            for h in range(heads):
                s = nn(k_n[j, h], q_t[i, h]) * factor
                s = jnp.where(allowed, s, MASKED)
                old = m_ref[h]
                new = jnp.maximum(old, jnp.max(s, axis=0, keepdims=True))
                shrink = jnp.exp2(old - new)
                p = jnp.exp2(s - new)
                l_ref[h] = l_ref[h] * shrink + jnp.sum(p, axis=0, keepdims=True)
                acc[h] = acc[h] * shrink + nn(v_t[j, h], p.astype(jnp.bfloat16))
                m_ref[h] = new

        sweep(i, half, seq_len, rows, visit, blocks)
        at = pl.ds(pl.multiple_of(i * rows, rows), rows)
        for h in range(heads):
            out_t[i, h * HD : (h + 1) * HD, :] = acc[h] / l_ref[h]
            logs[i, h] = m_ref[h] + jnp.log2(l_ref[h])
        out[at, :] = out_t[i].T.astype(jnp.bfloat16)
        return carry

    lax.fori_loop(0, blocks, block, 0)


def vmem_specs(count):
    return [pl.BlockSpec(memory_space=pltpu.VMEM)] * count


def attend(info, qkv, kv_other, blocks):
    rows_all, wide = qkv.shape
    width = wide // 3
    heads, rows = width // HD, rows_all // blocks
    bf, f32 = jnp.bfloat16, jnp.float32
    pairs = blocks * rows * rows * (blocks + 1)
    return pl.pallas_call(
        attend_kernel,
        out_shape=(
            jax.ShapeDtypeStruct((rows_all, width), bf),
            jax.ShapeDtypeStruct((blocks, width, rows), f32),
            jax.ShapeDtypeStruct((blocks, heads, 1, rows), f32),
        ),
        in_specs=[pl.BlockSpec(memory_space=pltpu.SMEM)] + vmem_specs(2),
        out_specs=tuple(vmem_specs(3)),
        scratch_shapes=[
            pltpu.VMEM((blocks, heads, HD, rows), bf),
            pltpu.VMEM((2 * blocks, heads, rows, HD), bf),
            pltpu.VMEM((2 * blocks, heads, HD, rows), bf),
            pltpu.VMEM((heads, HD, rows), f32),
            pltpu.VMEM((heads, 1, rows), f32),
            pltpu.VMEM((heads, 1, rows), f32),
        ],
        cost_estimate=pl.CostEstimate(
            flops=20 * 1024 * 1024 * 1024, transcendentals=pairs * heads, bytes_accessed=8 * 1024 * 1024
        ),
        name="attend",
    )(info, qkv, kv_other)


def back_kernel(
    info, qkv, kv_other, grad, out_t, logs,
    dq, dkv, dkv_other,
    q_t, g_t, k_n, k_t, v_n, dq_t, dk_t, dv_t, delta,
):
    width, heads = head_dims(qkv)
    blocks, rows = q_t.shape[0], q_t.shape[-1]
    seq_len, half = info[0], info[1]
    scale = 1.0 / math.sqrt(HD)
    factor = LOG2E * scale

    def prepare(b, carry):
        at = pl.ds(pl.multiple_of(b * rows, rows), rows)
        mine = qkv[at, :]
        mine_t = mine[:, : 2 * width].astype(jnp.float32).T
        grad_t = grad[at, :].astype(jnp.float32).T
        theirs = kv_other[at, :]
        theirs_t = theirs[:, :width].astype(jnp.float32).T
        for h in range(heads):
            lo, hi = h * HD, (h + 1) * HD
            q_t[b, h] = mine_t[lo:hi].astype(jnp.bfloat16)
            g_t[b, h] = grad_t[lo:hi].astype(jnp.bfloat16)
            delta[b, h] = jnp.sum(grad_t[lo:hi] * out_t[b, lo:hi], axis=0, keepdims=True)
            k_t[b, h] = mine_t[width + lo : width + hi].astype(jnp.bfloat16)
            k_n[b, h] = mine[:, width + lo : width + hi]
            v_n[b, h] = mine[:, 2 * width + lo : 2 * width + hi]
            k_t[blocks + b, h] = theirs_t[lo:hi].astype(jnp.bfloat16)
            k_n[blocks + b, h] = theirs[:, lo:hi]
            v_n[blocks + b, h] = theirs[:, width + lo : width + hi]
        return carry

    lax.fori_loop(0, blocks, prepare, 0)
    dk_t[...] = jnp.zeros_like(dk_t)
    dv_t[...] = jnp.zeros_like(dv_t)

    def block(i, carry):
        dq_t[...] = jnp.zeros_like(dq_t)

        def visit(j, start, diagonal):
            query_start = (2 * i + half) * rows if diagonal else None
            allowed = chunk_mask(start, seq_len, query_start, rows, rows)
            for h in range(heads):
                at = slice(h * HD, (h + 1) * HD)
                s = nn(k_n[j, h], q_t[i, h]) * factor - logs[i, h]
                p = jnp.exp2(jnp.where(allowed, s, MASKED))
                dv_t[j, at] += nt(g_t[i, h], p.astype(jnp.bfloat16))
                dp = nn(v_n[j, h], g_t[i, h])
                ds = (p * (dp - delta[i, h])).astype(jnp.bfloat16)
                dq_t[at] += nn(k_t[j, h], ds)
                dk_t[j, at] += nt(q_t[i, h], ds)

        sweep(i, half, seq_len, rows, visit, blocks)
        at = pl.ds(pl.multiple_of(i * rows, rows), rows)
        dq[at, :] = (dq_t[...] * scale).T.astype(dq.dtype)
        return carry

    lax.fori_loop(0, blocks, block, 0)

    def finish(b, carry):
        at = pl.ds(pl.multiple_of(b * rows, rows), rows)
        dkv[at, :width] = (dk_t[b] * scale).T.astype(dkv.dtype)
        dkv[at, width:] = dv_t[b].T.astype(dkv.dtype)
        dkv_other[at, :width] = (dk_t[blocks + b] * scale).T.astype(dkv_other.dtype)
        dkv_other[at, width:] = dv_t[blocks + b].T.astype(dkv_other.dtype)
        return carry

    lax.fori_loop(0, blocks, finish, 0)


def attend_back(info, qkv, kv_other, grad, out_t, logs, blocks):
    rows_all, wide = qkv.shape
    width = wide // 3
    heads, rows = width // HD, rows_all // blocks
    bf, f32 = jnp.bfloat16, jnp.float32
    pairs = blocks * rows * rows * (blocks + 1)
    return pl.pallas_call(
        back_kernel,
        out_shape=(
            jax.ShapeDtypeStruct((rows_all, width), bf),
            jax.ShapeDtypeStruct((rows_all, 2 * width), bf),
            jax.ShapeDtypeStruct((rows_all, 2 * width), bf),
        ),
        in_specs=[pl.BlockSpec(memory_space=pltpu.SMEM)] + vmem_specs(5),
        out_specs=tuple(vmem_specs(3)),
        scratch_shapes=[
            pltpu.VMEM((blocks, heads, HD, rows), bf),
            pltpu.VMEM((blocks, heads, HD, rows), bf),
            pltpu.VMEM((2 * blocks, heads, rows, HD), bf),
            pltpu.VMEM((2 * blocks, heads, HD, rows), bf),
            pltpu.VMEM((2 * blocks, heads, rows, HD), bf),
            pltpu.VMEM((width, rows), f32),
            pltpu.VMEM((2 * blocks, width, rows), f32),
            pltpu.VMEM((2 * blocks, width, rows), f32),
            pltpu.VMEM((blocks, heads, 1, rows), f32),
        ],
        cost_estimate=pl.CostEstimate(
            flops=60 * 1024 * 1024 * 1024, transcendentals=pairs * heads, bytes_accessed=8 * 1024 * 1024
        ),
        name="attend_back",
    )(info, qkv, kv_other, grad, out_t, logs)


def column_blocks(values, count):
    return values.reshape(values.shape[0], count, -1).transpose(1, 0, 2)


def row_blocks(values, count):
    return values.reshape(values.shape[0], count, -1).transpose(1, 2, 0)


def head_columns(groups, halves, sections, units):
    local, owned = units // groups, sections * units // (groups * halves)
    send = [[[[] for _ in range(groups)] for _ in range(halves)] for _ in range(groups)]
    take = np.zeros((groups, halves, owned, 2), np.int32)
    for u in range(sections * units):
        section, inside = divmod(u, units)
        source, offset = divmod(inside, local)
        owner, place = divmod(u, owned)
        head, ctx = divmod(owner, halves)
        slots = send[source][ctx][head]
        take[head, ctx, place] = (source, len(slots))
        slots.append(section * local + offset)
    width = max(len(x) for a in send for b in a for x in b)
    table = np.zeros((groups, halves, groups, width), np.int32)
    for a in range(groups):
        for b in range(halves):
            for c in range(groups):
                table[a, b, c, : len(send[a][b][c])] = send[a][b][c]
    return table, take


def body(
    inputs,
    dataset_ids,
    lengths,
    dataset_table,
    attn_gain,
    attn_shift,
    qkv_weight,
    query_bias,
    value_bias,
    out_weight,
    out_bias,
    mlp_gain,
    mlp_shift,
    fc_weight,
    fc_bias,
    proj_weight,
    proj_bias,
    cotangent,
):
    cell_count, row_count, model_width = inputs.shape
    cells = lax.axis_size("cell")
    groups = lax.axis_size("head")
    halves = lax.axis_size("ctx")
    parts = groups * halves
    half_index = lax.axis_index("ctx")
    head_width = HEADS // groups * HD
    token_count = cell_count * row_count
    ctx_rows = groups * row_count
    cell_steps, ctx_steps, head_steps = bits_of("cell"), bits_of("ctx"), bits_of("head")[::-1]
    steps_x = cell_steps + ctx_steps + head_steps
    steps_y = cell_steps[:1] + ctx_steps + cell_steps[1:] + head_steps
    one_hot = (
        dataset_ids[:, None] == jnp.arange(dataset_table.shape[0], dtype=jnp.int32)[None, :]
    ).astype(jnp.bfloat16)
    embedded = jnp.dot(one_hot, dataset_table, preferred_element_type=jnp.float32)
    residual = (inputs.astype(jnp.float32) + embedded[:, None, :]).reshape(token_count, model_width)
    normed = layer_norm(residual, attn_gain, attn_shift).astype(jnp.bfloat16)
    mixed_qkv = jnp.dot(normed, qkv_weight, preferred_element_type=jnp.float32)
    bias_row = jnp.concatenate([query_bias, jnp.zeros_like(query_bias), value_bias])
    mixed_qkv = (mixed_qkv + bias_row).astype(jnp.bfloat16)

    def to_heads(values):
        sections = values.shape[1] // model_width
        values = values.reshape(cell_count, row_count, sections, groups, head_width)
        values = values.transpose(3, 0, 1, 2, 4).reshape(groups, cell_count, row_count, -1)
        values = lax.all_to_all(values, "head", split_axis=0, concat_axis=0, tiled=True)
        return values.transpose(1, 0, 2, 3).reshape(cell_count, ctx_rows, -1)

    def to_rows(values):
        sections = values.shape[-1] // head_width
        values = values.reshape(cell_count, groups, row_count, -1).transpose(1, 0, 2, 3)
        values = lax.all_to_all(values, "head", split_axis=0, concat_axis=0, tiled=True)
        values = values.reshape(groups, cell_count, row_count, sections, head_width)
        return values.transpose(1, 2, 3, 0, 4).reshape(token_count, sections * model_width)

    qkv_heads = to_heads(mixed_qkv)
    kv_other = swap(qkv_heads[:, :, head_width:], "ctx", 1)
    normed_near = normed.reshape(cell_count, 1, row_count, model_width)
    normed_near = lax.all_gather(normed_near, "head", axis=1, tiled=True)
    normed_near = normed_near.reshape(cell_count * ctx_rows, model_width)
    normed_far = swap(normed_near, "ctx", 1)
    infos = [jnp.stack([lengths[n], half_index.astype(jnp.int32)]) for n in range(cell_count)]
    runs = [attend(infos[n], qkv_heads[n], kv_other[n], groups) for n in range(cell_count)]
    attended = jnp.stack([r[0] for r in runs])
    attended_rows = to_rows(attended)
    attn_out = jnp.dot(attended_rows, out_weight, preferred_element_type=jnp.float32) + out_bias
    middle = residual + attn_out
    mlp_normed = layer_norm(middle, mlp_gain, mlp_shift).astype(jnp.bfloat16)
    hidden = jnp.dot(mlp_normed, fc_weight, preferred_element_type=jnp.float32) + fc_bias
    active = gelu_tanh(hidden).astype(jnp.bfloat16)
    branch = jnp.dot(active, proj_weight, preferred_element_type=jnp.float32) + proj_bias
    block_out = (middle + branch).astype(jnp.bfloat16).reshape(cell_count, row_count, model_width)
    grad_low = cotangent.reshape(token_count, model_width)
    proj_kept, proj_sent = weight_blocks(
        row_blocks(grad_low, parts), column_blocks(active, cells), False, False
    )
    grad_low, proj_kept, proj_sent = lax.optimization_barrier((grad_low, proj_kept, proj_sent))
    proj_weight_grad = scatter_sum(proj_kept, proj_sent, steps_x).T
    grad_top = grad_low.astype(jnp.float32)
    proj_bias_grad = jnp.sum(grad_top, axis=0)
    active_grad = jnp.einsum("nd,fd->nf", grad_low, proj_weight, preferred_element_type=jnp.float32)
    gelu_pull = jax.vjp(gelu_tanh, hidden)[1]
    hidden_grad = gelu_pull(active_grad)[0].astype(jnp.bfloat16)
    fc_bias_grad = jnp.sum(hidden_grad, axis=0, dtype=jnp.float32)
    normed_grad = jnp.einsum(
        "nf,df->nd", hidden_grad, fc_weight, preferred_element_type=jnp.float32
    )
    mlp_pull = jax.vjp(layer_norm, middle, mlp_gain, mlp_shift)[1]
    middle_part, mlp_gain_grad, mlp_shift_grad = mlp_pull(normed_grad)
    middle_grad = grad_top + middle_part
    middle_low = middle_grad.astype(jnp.bfloat16)
    out_bias_grad = jnp.sum(middle_low, axis=0, dtype=jnp.float32)
    attended_grad = jnp.einsum(
        "ne,de->nd", middle_low, out_weight, preferred_element_type=jnp.float32
    ).astype(jnp.bfloat16)
    grad_heads = to_heads(attended_grad)

    fc_kept, fc_sent = weight_blocks(
        row_blocks(mlp_normed, cells), column_blocks(hidden_grad, parts), True, False
    )
    out_kept, out_sent = weight_blocks(
        row_blocks(middle_low, parts), column_blocks(attended_rows, cells), False, True
    )
    grad_heads, fc_kept, fc_sent, out_kept, out_sent = lax.optimization_barrier(
        (grad_heads, fc_kept, fc_sent, out_kept, out_sent)
    )
    fc_weight_grad = scatter_sum(fc_kept, fc_sent, steps_x)
    out_weight_grad = scatter_sum(out_kept, out_sent, steps_y).T

    backs = [
      attend_back(
        infos[n], qkv_heads[n], kv_other[n], grad_heads[n], runs[n][1], runs[n][2], groups
      )
      for n in range(cell_count)
    ]
    dq = jnp.stack([b[0] for b in backs])
    dkv = jnp.stack([b[1] for b in backs])
    dkv_far = jnp.stack([b[2] for b in backs])

    def tall(values):
        return values.reshape(cell_count * ctx_rows, -1)

    def over_tokens(a, b):
        return jnp.einsum("nd,ne->de", a, b, preferred_element_type=jnp.float32)

    qkv_part = jnp.concatenate(
        [
            over_tokens(normed_near, tall(dq)),
            over_tokens(normed_near, tall(dkv)) + over_tokens(normed_far, tall(dkv_far)),
        ],
        axis=1,
    ).astype(jnp.bfloat16)
    units = 2 * groups
    local_units = 3 * units // groups
    qkv_part = qkv_part.reshape(cells, model_width // cells, local_units, -1).transpose(0, 2, 1, 3)
    cell_index = lax.axis_index("cell")
    for axis, bit in cell_steps[::-1]:
        on = (cell_index // bit) % 2
        half = qkv_part.shape[0] // 2
        kept = lax.dynamic_slice_in_dim(qkv_part, on * half, half, 0)
        sent = lax.dynamic_slice_in_dim(qkv_part, (1 - on) * half, half, 0)
        qkv_part = add_up(kept, swap(sent, axis, bit)).astype(jnp.bfloat16)
    qkv_part = add_up(qkv_part, swap(qkv_part, "ctx", 1)).astype(jnp.bfloat16)[0]
    send_table, take_table = head_columns(groups, halves, 3, units)
    head_index = lax.axis_index("head")
    sent = qkv_part[jnp.asarray(send_table)[head_index, half_index]]
    got = lax.all_to_all(sent, "head", split_axis=0, concat_axis=0, tiled=True)
    taken = jnp.asarray(take_table)[head_index, half_index]
    qkv_weight_grad = jnp.concatenate(
        [got[taken[n, 0], taken[n, 1]] for n in range(take_table.shape[2])], axis=-1
    ).astype(jnp.float32)

    dkv_got = swap(dkv_far, "ctx", 1)
    dkv = add_up(dkv, dkv_got).astype(jnp.bfloat16)
    qkv_grad = to_rows(jnp.concatenate([dq, dkv], axis=-1))
    column_sums = jnp.sum(qkv_grad, axis=0, dtype=jnp.float32)
    query_bias_grad = column_sums[:model_width]
    value_bias_grad = column_sums[2 * model_width :]
    normed_back = jnp.einsum("ne,de->nd", qkv_grad, qkv_weight, preferred_element_type=jnp.float32)
    attn_pull = jax.vjp(layer_norm, residual, attn_gain, attn_shift)[1]
    residual_part, attn_gain_grad, attn_shift_grad = attn_pull(normed_back)
    residual_grad = middle_grad + residual_part
    input_grad = residual_grad.astype(jnp.bfloat16).reshape(cell_count, row_count, model_width)
    cell_totals = jnp.sum(residual_grad.reshape(cell_count, row_count, model_width), axis=1)
    table_grad = jnp.dot(
        one_hot.astype(jnp.float32).T, cell_totals, precision=lax.Precision.HIGHEST
    )

    width = model_width // cells
    vectors = [
        attn_gain_grad,
        attn_shift_grad,
        query_bias_grad,
        value_bias_grad,
        out_bias_grad,
        mlp_gain_grad,
        mlp_shift_grad,
        proj_bias_grad,
    ]
    fc_rows = fc_bias_grad.shape[0] // model_width
    packed = jnp.concatenate(
        [table_grad.reshape(-1, cells, width).transpose(1, 0, 2)]
        + [v.reshape(cells, 1, width) for v in vectors]
        + [fc_bias_grad.reshape(cells, fc_rows, width)],
        axis=1,
    )
    for axis, bit in cell_steps[::-1]:
        on = (cell_index // bit) % 2
        half = packed.shape[0] // 2
        kept = lax.dynamic_slice_in_dim(packed, on * half, half, 0)
        sent = lax.dynamic_slice_in_dim(packed, (1 - on) * half, half, 0)
        packed = kept + swap(sent, axis, bit)
    for axis, bit in ctx_steps + head_steps:
        packed = packed + swap(packed, axis, bit)
    packed = packed[0]
    datasets = dataset_table.shape[0]
    table_grad = packed[:datasets]
    (
        attn_gain_grad,
        attn_shift_grad,
        query_bias_grad,
        value_bias_grad,
        out_bias_grad,
        mlp_gain_grad,
        mlp_shift_grad,
        proj_bias_grad,
    ) = [packed[datasets + n] for n in range(len(vectors))]
    fc_bias_grad = packed[datasets + len(vectors) :].reshape(-1)
    return (
        block_out,
        input_grad,
        table_grad,
        attn_gain_grad,
        attn_shift_grad,
        qkv_weight_grad,
        query_bias_grad,
        value_bias_grad,
        out_weight_grad,
        out_bias_grad,
        mlp_gain_grad,
        mlp_shift_grad,
        fc_weight_grad,
        fc_bias_grad,
        proj_weight_grad,
        proj_bias_grad,
    )


def solution(mesh):
    in_specs = (
        P("cell", ("head", "ctx"), None),
        P("cell"),
        P("cell"),
        P(),
        P(),
        P(),
        P(),
        P(),
        P(),
        P(),
        P(),
        P(),
        P(),
        P(),
        P(),
        P(),
        P(),
        P("cell", ("head", "ctx"), None),
    )
    out_specs = (
        P("cell", ("head", "ctx"), None),
        P("cell", ("head", "ctx"), None),
        P(None, "cell"),
        P("cell"),
        P("cell"),
        P("cell", ("head", "ctx")),
        P("cell"),
        P("cell"),
        P("cell", ("head", "ctx")),
        P("cell"),
        P("cell"),
        P("cell"),
        P("cell", ("head", "ctx")),
        P("cell"),
        P("cell", ("head", "ctx")),
        P("cell"),
    )
    return jax.shard_map(body, mesh=mesh, in_specs=in_specs, out_specs=out_specs, check_vma=False)
```

```python
import math

import jax
import jax.numpy as jnp
from jax import lax
from jax.experimental import pallas as pl
from jax.experimental.pallas import tpu as pltpu
from jax.sharding import PartitionSpec as P
import numpy as np


HEADS = 20
HD = 56


epsilon = 1e-05
MASKED = -1e30
LOG2E = math.log2(math.e)


def layer_norm(values, gain_row, shift_row):
    center = values - jnp.mean(values, axis=-1, keepdims=True)
    spread = jnp.mean(center * center, axis=-1, keepdims=True)
    return center * lax.rsqrt(spread + epsilon) * gain_row + shift_row


def gelu_tanh(values):
    return jax.nn.gelu(values, approximate=True)


def swap(values, axis, bit):
    return lax.ppermute(values, axis, [(i, i ^ bit) for i in range(lax.axis_size(axis))])


def bits_of(axis):
    size, bit, found = lax.axis_size(axis), 1, []
    while bit < size:
        found.append((axis, bit))
        bit *= 2
    return found


def nn(a, b):
    return jnp.dot(a, b, preferred_element_type=jnp.float32)


def nt(a, b):
    return lax.dot_general(a, b, (((1,), (1,)), ((), ())), preferred_element_type=jnp.float32)


def relative_order(count, axis_bits):
    rel = np.zeros((count,), np.int32)
    for s, bit in enumerate(axis_bits):
        rel += ((np.arange(count) >> (len(axis_bits) - 1 - s)) & 1).astype(np.int32) * bit
    return jnp.asarray(rel)


def padded_rows(values, multiple=16):
    extra = -values.shape[1] % multiple
    return jnp.pad(values, ((0, 0), (0, extra), (0, 0))) if extra else values


def weight_blocks(left, right, by_cell_left, y_first):
    cells, groups, halves = lax.axis_size("cell"), lax.axis_size("head"), lax.axis_size("ctx")
    parts, half_cells = groups * halves, cells // 2
    cell_ids = relative_order(cells, [b for _, b in bits_of("cell")]) ^ lax.axis_index("cell")
    places = jnp.arange(parts, dtype=jnp.int32)
    part_ids = ((places % groups) ^ lax.axis_index("head")) * halves + (
        (places // groups) ^ lax.axis_index("ctx")
    )
    left_ids, right_ids = (cell_ids, part_ids) if by_cell_left else (part_ids, cell_ids)
    left = padded_rows(left[left_ids])
    rows, cols = left.shape[1], right.shape[2]
    tall = left.reshape(-1, left.shape[2])
    right_count = right.shape[0]

    def put(out, index, values):
        out[index] = values.astype(jnp.bfloat16)

    def kernel(ids, left_ref, right_ref, kept, sent):
        i = pl.program_id(0)
        if by_cell_left:
            block = nn(left_ref[...], right_ref[ids[i]])
            for n in range(cells):
                out, at = (kept, n) if n < half_cells else (sent, n - half_cells)
                put(out, (at, 0), block[n * rows : (n + 1) * rows])
        else:
            block = nn(left_ref[...], right_ref[ids[(i + half_cells) % cells]])

            def fill(out):
                for n in range(parts):
                    at = (n // groups, 0, n % groups) if y_first else (0, n)
                    put(out, at, block[n * rows : (n + 1) * rows])

            pl.when(i < half_cells)(lambda: fill(sent))
            pl.when(i >= half_cells)(lambda: fill(kept))

    last = half_cells - 1
    if by_cell_left:
        shape = (half_cells, parts, rows, cols)
        specs = [pl.BlockSpec((half_cells, 1, rows, cols), lambda i, ids: (0, i, 0, 0))] * 2
    elif y_first:
        shape = (halves, half_cells, groups, rows, cols)
        block_shape = (halves, 1, groups, rows, cols)
        specs = [
            pl.BlockSpec(block_shape, lambda i, ids: (0, jnp.maximum(i - last - 1, 0), 0, 0, 0)),
            pl.BlockSpec(block_shape, lambda i, ids: (0, jnp.minimum(i, last), 0, 0, 0)),
        ]
    else:
        shape = (half_cells, parts, rows, cols)
        block_shape = (1, parts, rows, cols)
        specs = [
            pl.BlockSpec(block_shape, lambda i, ids: (jnp.maximum(i - last - 1, 0), 0, 0, 0)),
            pl.BlockSpec(block_shape, lambda i, ids: (jnp.minimum(i, last), 0, 0, 0)),
        ]
    kept, sent = pl.pallas_call(
        kernel,
        out_shape=[jax.ShapeDtypeStruct(shape, jnp.bfloat16)] * 2,
        grid_spec=pltpu.PrefetchScalarGridSpec(
            num_scalar_prefetch=1,
            grid=(right_count,),
            in_specs=[
                pl.BlockSpec(tall.shape, lambda i, ids: (0, 0), pipeline_mode=pl.Buffered(1)),
                pl.BlockSpec(right.shape, lambda i, ids: (0, 0, 0), pipeline_mode=pl.Buffered(1)),
            ],
            out_specs=specs,
        ),
        name="weight_blocks",
    )(right_ids, tall, right)
    return kept.reshape(-1, rows, cols), sent.reshape(-1, rows, cols)


def line_gather(values):
    groups, halves = lax.axis_size("head"), lax.axis_size("ctx")
    index = lax.axis_index("head")

    def across(piece, heads):
        pairs = [(h * halves + c, h * halves + (c ^ 1)) for h in heads for c in range(halves)]
        return lax.ppermute(piece, ("head", "ctx"), pairs)

    near, far = {0: values}, {0: across(values, range(groups))}
    rising = falling = values
    for k in range(1, groups):
        rising = lax.ppermute(rising, "head", [(i, i + 1) for i in range(k - 1, groups - 1)])
        falling = lax.ppermute(falling, "head", [(i + 1, i) for i in range(groups - k)])
        near[-k], near[k] = rising, falling
        far[-k], far[k] = across(rising, range(k, groups)), across(falling, range(groups - k))

    def ordered(found):
        line = jnp.stack([found[k] for k in range(1 - groups, groups)])
        return lax.dynamic_slice_in_dim(line, groups - 1 - index, groups, 0)

    return ordered(near), ordered(far)


def add_up(kept, got):
    return kept.astype(jnp.float32) + got.astype(jnp.float32)


def scatter_sum(kept, sent, steps):
    total = None
    for s, (axis, bit) in enumerate(steps):
        if s:
            total = total.astype(jnp.bfloat16)
            half = total.shape[0] // 2
            kept, sent = total[:half], total[half:]
        got = swap(sent, axis, bit)
        total = add_up(kept, got)
    return total[0]


def head_dims(qkv_ref):
    width = qkv_ref.shape[-1] // 3
    return width, width // HD


def chunk_mask(start, seq_len, query_start, rows, cols):
    key_pos = start + lax.broadcasted_iota(jnp.int32, (rows, cols), 0)
    if query_start is None:
        return key_pos < seq_len
    query_pos = query_start + lax.broadcasted_iota(jnp.int32, (rows, cols), 1)
    return (key_pos < seq_len) & (key_pos <= query_pos)


def sweep(i, half, seq_len, rows, visit, blocks):
    def own(j, carry):
        visit(j, (2 * j + half) * rows, False)
        return carry

    def other(j, carry):
        visit(blocks + j, (2 * j + 1 - half) * rows, False)
        return carry

    span = 2 * rows
    own_count = jnp.minimum(i, (seq_len - half * rows + span - 1) // span)
    other_count = jnp.minimum(i + half, (seq_len - (1 - half) * rows + span - 1) // span)
    lax.fori_loop(0, other_count, other, 0)
    lax.fori_loop(0, own_count, own, 0)
    visit(i, (2 * i + half) * rows, True)


def attend_kernel(info, qkv, kv_other, out, out_t, logs, q_t, k_n, v_t, acc, m_ref, l_ref):
    width, heads = head_dims(qkv)
    blocks, rows = q_t.shape[0], q_t.shape[-1]
    seq_len, half = info[0], info[1]
    factor = LOG2E / math.sqrt(HD)

    def prepare(b, carry):
        at = pl.ds(pl.multiple_of(b * rows, rows), rows)
        mine = qkv[at, :]
        mine_t = mine.astype(jnp.float32).T
        theirs = kv_other[at, :]
        theirs_t = theirs[:, width:].astype(jnp.float32).T
        for h in range(heads):
            lo, hi = h * HD, (h + 1) * HD
            q_t[b, h] = mine_t[lo:hi].astype(jnp.bfloat16)
            v_t[b, h] = mine_t[2 * width + lo : 2 * width + hi].astype(jnp.bfloat16)
            k_n[b, h] = mine[:, width + lo : width + hi]
            v_t[blocks + b, h] = theirs_t[lo:hi].astype(jnp.bfloat16)
            k_n[blocks + b, h] = theirs[:, lo:hi]
        return carry

    lax.fori_loop(0, blocks, prepare, 0)

    def block(i, carry):
        acc[...] = jnp.zeros_like(acc)
        m_ref[...] = jnp.full_like(m_ref, MASKED)
        l_ref[...] = jnp.zeros_like(l_ref)

        def visit(j, start, diagonal):
            query_start = (2 * i + half) * rows if diagonal else None
            allowed = chunk_mask(start, seq_len, query_start, rows, rows)
            for h in range(heads):
                s = nn(k_n[j, h], q_t[i, h]) * factor
                s = jnp.where(allowed, s, MASKED)
                old = m_ref[h]
                new = jnp.maximum(old, jnp.max(s, axis=0, keepdims=True))
                shrink = jnp.exp2(old - new)
                p = jnp.exp2(s - new)
                l_ref[h] = l_ref[h] * shrink + jnp.sum(p, axis=0, keepdims=True)
                acc[h] = acc[h] * shrink + nn(v_t[j, h], p.astype(jnp.bfloat16))
                m_ref[h] = new

        sweep(i, half, seq_len, rows, visit, blocks)
        at = pl.ds(pl.multiple_of(i * rows, rows), rows)
        for h in range(heads):
            out_t[i, h * HD : (h + 1) * HD, :] = acc[h] / l_ref[h]
            logs[i, h] = m_ref[h] + jnp.log2(l_ref[h])
        out[at, :] = out_t[i].T.astype(jnp.bfloat16)
        return carry

    lax.fori_loop(0, blocks, block, 0)


def vmem_specs(count):
    return [pl.BlockSpec(memory_space=pltpu.VMEM)] * count


def attend(info, qkv, kv_other, blocks):
    rows_all, wide = qkv.shape
    width = wide // 3
    heads, rows = width // HD, rows_all // blocks
    bf, f32 = jnp.bfloat16, jnp.float32
    pairs = blocks * rows * rows * (blocks + 1)
    return pl.pallas_call(
        attend_kernel,
        out_shape=(
            jax.ShapeDtypeStruct((rows_all, width), bf),
            jax.ShapeDtypeStruct((blocks, width, rows), f32),
            jax.ShapeDtypeStruct((blocks, heads, 1, rows), f32),
        ),
        in_specs=[pl.BlockSpec(memory_space=pltpu.SMEM)] + vmem_specs(2),
        out_specs=tuple(vmem_specs(3)),
        scratch_shapes=[
            pltpu.VMEM((blocks, heads, HD, rows), bf),
            pltpu.VMEM((2 * blocks, heads, rows, HD), bf),
            pltpu.VMEM((2 * blocks, heads, HD, rows), bf),
            pltpu.VMEM((heads, HD, rows), f32),
            pltpu.VMEM((heads, 1, rows), f32),
            pltpu.VMEM((heads, 1, rows), f32),
        ],
        cost_estimate=pl.CostEstimate(
            flops=20 * 1024 * 1024 * 1024, transcendentals=pairs * heads, bytes_accessed=8 * 1024 * 1024
        ),
        name="attend",
    )(info, qkv, kv_other)


def back_kernel(
    info, qkv, kv_other, grad, out_t, logs,
    dq, dkv, dkv_other,
    q_t, g_t, k_n, k_t, v_n, dq_t, dk_t, dv_t, delta,
):
    width, heads = head_dims(qkv)
    blocks, rows = q_t.shape[0], q_t.shape[-1]
    seq_len, half = info[0], info[1]
    scale = 1.0 / math.sqrt(HD)
    factor = LOG2E * scale

    def prepare(b, carry):
        at = pl.ds(pl.multiple_of(b * rows, rows), rows)
        mine = qkv[at, :]
        mine_t = mine[:, : 2 * width].astype(jnp.float32).T
        grad_t = grad[at, :].astype(jnp.float32).T
        theirs = kv_other[at, :]
        theirs_t = theirs[:, :width].astype(jnp.float32).T
        for h in range(heads):
            lo, hi = h * HD, (h + 1) * HD
            q_t[b, h] = mine_t[lo:hi].astype(jnp.bfloat16)
            g_t[b, h] = grad_t[lo:hi].astype(jnp.bfloat16)
            delta[b, h] = jnp.sum(grad_t[lo:hi] * out_t[b, lo:hi], axis=0, keepdims=True)
            k_t[b, h] = mine_t[width + lo : width + hi].astype(jnp.bfloat16)
            k_n[b, h] = mine[:, width + lo : width + hi]
            v_n[b, h] = mine[:, 2 * width + lo : 2 * width + hi]
            k_t[blocks + b, h] = theirs_t[lo:hi].astype(jnp.bfloat16)
            k_n[blocks + b, h] = theirs[:, lo:hi]
            v_n[blocks + b, h] = theirs[:, width + lo : width + hi]
        return carry

    lax.fori_loop(0, blocks, prepare, 0)
    dk_t[...] = jnp.zeros_like(dk_t)
    dv_t[...] = jnp.zeros_like(dv_t)

    def block(i, carry):
        dq_t[...] = jnp.zeros_like(dq_t)

        def visit(j, start, diagonal):
            query_start = (2 * i + half) * rows if diagonal else None
            allowed = chunk_mask(start, seq_len, query_start, rows, rows)
            for h in range(heads):
                at = slice(h * HD, (h + 1) * HD)
                s = nn(k_n[j, h], q_t[i, h]) * factor - logs[i, h]
                p = jnp.exp2(jnp.where(allowed, s, MASKED))
                dv_t[j, at] += nt(g_t[i, h], p.astype(jnp.bfloat16))
                dp = nn(v_n[j, h], g_t[i, h])
                ds = (p * (dp - delta[i, h])).astype(jnp.bfloat16)
                dq_t[at] += nn(k_t[j, h], ds)
                dk_t[j, at] += nt(q_t[i, h], ds)

        sweep(i, half, seq_len, rows, visit, blocks)
        at = pl.ds(pl.multiple_of(i * rows, rows), rows)
        dq[at, :] = (dq_t[...] * scale).T.astype(dq.dtype)
        return carry

    lax.fori_loop(0, blocks, block, 0)

    def finish(b, carry):
        at = pl.ds(pl.multiple_of(b * rows, rows), rows)
        dkv[at, :width] = (dk_t[b] * scale).T.astype(dkv.dtype)
        dkv[at, width:] = dv_t[b].T.astype(dkv.dtype)
        dkv_other[at, :width] = (dk_t[blocks + b] * scale).T.astype(dkv_other.dtype)
        dkv_other[at, width:] = dv_t[blocks + b].T.astype(dkv_other.dtype)
        return carry

    lax.fori_loop(0, blocks, finish, 0)


def attend_back(info, qkv, kv_other, grad, out_t, logs, blocks):
    rows_all, wide = qkv.shape
    width = wide // 3
    heads, rows = width // HD, rows_all // blocks
    bf, f32 = jnp.bfloat16, jnp.float32
    pairs = blocks * rows * rows * (blocks + 1)
    return pl.pallas_call(
        back_kernel,
        out_shape=(
            jax.ShapeDtypeStruct((rows_all, width), bf),
            jax.ShapeDtypeStruct((rows_all, 2 * width), bf),
            jax.ShapeDtypeStruct((rows_all, 2 * width), bf),
        ),
        in_specs=[pl.BlockSpec(memory_space=pltpu.SMEM)] + vmem_specs(5),
        out_specs=tuple(vmem_specs(3)),
        scratch_shapes=[
            pltpu.VMEM((blocks, heads, HD, rows), bf),
            pltpu.VMEM((blocks, heads, HD, rows), bf),
            pltpu.VMEM((2 * blocks, heads, rows, HD), bf),
            pltpu.VMEM((2 * blocks, heads, HD, rows), bf),
            pltpu.VMEM((2 * blocks, heads, rows, HD), bf),
            pltpu.VMEM((width, rows), f32),
            pltpu.VMEM((2 * blocks, width, rows), f32),
            pltpu.VMEM((2 * blocks, width, rows), f32),
            pltpu.VMEM((blocks, heads, 1, rows), f32),
        ],
        cost_estimate=pl.CostEstimate(
            flops=60 * 1024 * 1024 * 1024, transcendentals=pairs * heads, bytes_accessed=8 * 1024 * 1024
        ),
        name="attend_back",
    )(info, qkv, kv_other, grad, out_t, logs)


def column_blocks(values, count):
    return values.reshape(values.shape[0], count, -1).transpose(1, 0, 2)


def row_blocks(values, count):
    return values.reshape(values.shape[0], count, -1).transpose(1, 2, 0)


def head_columns(groups, halves, sections, units):
    local, owned = units // groups, sections * units // (groups * halves)
    send = [[[[] for _ in range(groups)] for _ in range(halves)] for _ in range(groups)]
    take = np.zeros((groups, halves, owned, 2), np.int32)
    for u in range(sections * units):
        section, inside = divmod(u, units)
        source, offset = divmod(inside, local)
        owner, place = divmod(u, owned)
        head, ctx = divmod(owner, halves)
        slots = send[source][ctx][head]
        take[head, ctx, place] = (source, len(slots))
        slots.append(section * local + offset)
    width = max(len(x) for a in send for b in a for x in b)
    table = np.zeros((groups, halves, groups, width), np.int32)
    for a in range(groups):
        for b in range(halves):
            for c in range(groups):
                table[a, b, c, : len(send[a][b][c])] = send[a][b][c]
    return table, take


def body(
    inputs,
    dataset_ids,
    lengths,
    dataset_table,
    attn_gain,
    attn_shift,
    qkv_weight,
    query_bias,
    value_bias,
    out_weight,
    out_bias,
    mlp_gain,
    mlp_shift,
    fc_weight,
    fc_bias,
    proj_weight,
    proj_bias,
    cotangent,
):
    cell_count, row_count, model_width = inputs.shape
    cells = lax.axis_size("cell")
    groups = lax.axis_size("head")
    halves = lax.axis_size("ctx")
    parts = groups * halves
    half_index = lax.axis_index("ctx")
    head_width = HEADS // groups * HD
    token_count = cell_count * row_count
    ctx_rows = groups * row_count
    cell_steps, ctx_steps, head_steps = bits_of("cell"), bits_of("ctx"), bits_of("head")[::-1]
    steps_x = cell_steps + ctx_steps + head_steps
    steps_y = cell_steps[:1] + ctx_steps + cell_steps[1:] + head_steps
    one_hot = (
        dataset_ids[:, None] == jnp.arange(dataset_table.shape[0], dtype=jnp.int32)[None, :]
    ).astype(jnp.bfloat16)
    embedded = jnp.dot(one_hot, dataset_table, preferred_element_type=jnp.float32)
    residual = (inputs.astype(jnp.float32) + embedded[:, None, :]).reshape(token_count, model_width)
    normed = layer_norm(residual, attn_gain, attn_shift).astype(jnp.bfloat16)
    normed_near, normed_far = line_gather(normed.reshape(cell_count, row_count, model_width))
    normed_near = normed_near.transpose(1, 0, 2, 3).reshape(cell_count * ctx_rows, model_width)
    normed_far = normed_far.transpose(1, 0, 2, 3).reshape(cell_count * ctx_rows, model_width)
    head_index = lax.axis_index("head")

    def own_columns(values):
        values = values.reshape(values.shape[0], 3, groups, head_width)
        values = lax.dynamic_index_in_dim(values, head_index, 2, keepdims=False)
        return values.reshape(values.shape[0], 3 * head_width)

    own_weight = own_columns(qkv_weight)
    bias_row = jnp.concatenate([query_bias, jnp.zeros_like(query_bias), value_bias])
    own_bias = own_columns(bias_row[None])
    qkv_heads = (nn(normed_near, own_weight) + own_bias).astype(jnp.bfloat16)
    qkv_heads = qkv_heads.reshape(cell_count, ctx_rows, -1)
    kv_other = nn(normed_far, own_weight[:, head_width:]) + own_bias[:, head_width:]
    kv_other = kv_other.astype(jnp.bfloat16).reshape(cell_count, ctx_rows, -1)

    def to_heads(values):
        sections = values.shape[1] // model_width
        values = values.reshape(cell_count, row_count, sections, groups, head_width)
        values = values.transpose(3, 0, 1, 2, 4).reshape(groups, cell_count, row_count, -1)
        values = lax.all_to_all(values, "head", split_axis=0, concat_axis=0, tiled=True)
        return values.transpose(1, 0, 2, 3).reshape(cell_count, ctx_rows, -1)

    def to_rows(values):
        sections = values.shape[-1] // head_width
        values = values.reshape(cell_count, groups, row_count, -1).transpose(1, 0, 2, 3)
        values = lax.all_to_all(values, "head", split_axis=0, concat_axis=0, tiled=True)
        values = values.reshape(groups, cell_count, row_count, sections, head_width)
        return values.transpose(1, 2, 3, 0, 4).reshape(token_count, sections * model_width)

    infos = [jnp.stack([lengths[n], half_index.astype(jnp.int32)]) for n in range(cell_count)]
    runs = [attend(infos[n], qkv_heads[n], kv_other[n], groups) for n in range(cell_count)]
    attended = jnp.stack([r[0] for r in runs])
    attended_rows = to_rows(attended)
    attn_out = jnp.dot(attended_rows, out_weight, preferred_element_type=jnp.float32) + out_bias
    middle = residual + attn_out
    mlp_normed = layer_norm(middle, mlp_gain, mlp_shift).astype(jnp.bfloat16)
    hidden = jnp.dot(mlp_normed, fc_weight, preferred_element_type=jnp.float32) + fc_bias
    active = gelu_tanh(hidden).astype(jnp.bfloat16)
    branch = jnp.dot(active, proj_weight, preferred_element_type=jnp.float32) + proj_bias
    block_out = (middle + branch).astype(jnp.bfloat16).reshape(cell_count, row_count, model_width)
    grad_low = cotangent.reshape(token_count, model_width)
    proj_kept, proj_sent = weight_blocks(
        row_blocks(grad_low, parts), column_blocks(active, cells), False, False
    )
    part_columns = model_width // parts
    proj_weight_grad = scatter_sum(proj_kept, proj_sent, steps_x)[:part_columns].T
    grad_top = grad_low.astype(jnp.float32)
    proj_bias_grad = jnp.sum(grad_top, axis=0)
    active_grad = jnp.einsum("nd,fd->nf", grad_low, proj_weight, preferred_element_type=jnp.float32)
    gelu_pull = jax.vjp(gelu_tanh, hidden)[1]
    hidden_grad = gelu_pull(active_grad)[0].astype(jnp.bfloat16)
    fc_bias_grad = jnp.sum(hidden_grad, axis=0, dtype=jnp.float32)
    normed_grad = jnp.einsum(
        "nf,df->nd", hidden_grad, fc_weight, preferred_element_type=jnp.float32
    )
    mlp_pull = jax.vjp(layer_norm, middle, mlp_gain, mlp_shift)[1]
    middle_part, mlp_gain_grad, mlp_shift_grad = mlp_pull(normed_grad)
    middle_grad = grad_top + middle_part
    middle_low = middle_grad.astype(jnp.bfloat16)
    out_bias_grad = jnp.sum(middle_low, axis=0, dtype=jnp.float32)
    attended_grad = jnp.einsum(
        "ne,de->nd", middle_low, out_weight, preferred_element_type=jnp.float32
    ).astype(jnp.bfloat16)
    grad_heads = to_heads(attended_grad)

    fc_kept, fc_sent = weight_blocks(
        row_blocks(mlp_normed, cells), column_blocks(hidden_grad, parts), True, False
    )
    out_kept, out_sent = weight_blocks(
        row_blocks(middle_low, parts), column_blocks(attended_rows, cells), False, True
    )
    cell_rows = model_width // cells
    fc_weight_grad = scatter_sum(fc_kept, fc_sent, steps_x)[:cell_rows]
    out_weight_grad = scatter_sum(out_kept, out_sent, steps_y)[:part_columns].T

    backs = [
      attend_back(
        infos[n], qkv_heads[n], kv_other[n], grad_heads[n], runs[n][1], runs[n][2], groups
      )
      for n in range(cell_count)
    ]
    dq = jnp.stack([b[0] for b in backs])
    dkv = jnp.stack([b[1] for b in backs])
    dkv_far = jnp.stack([b[2] for b in backs])

    def tall(values):
        return values.reshape(cell_count * ctx_rows, -1)

    def over_tokens(a, b):
        return jnp.einsum("nd,ne->de", a, b, preferred_element_type=jnp.float32)

    dkv_got = swap(dkv_far, "ctx", 1)
    dq_rows = to_rows(dq)
    qkv_part = jnp.concatenate(
        [
            over_tokens(normed_near, tall(dq)),
            over_tokens(normed_near, tall(dkv)) + over_tokens(normed_far, tall(dkv_far)),
        ],
        axis=1,
    ).astype(jnp.bfloat16)
    units = 2 * groups
    local_units = 3 * units // groups
    qkv_part = qkv_part.reshape(cells, model_width // cells, local_units, -1).transpose(0, 2, 1, 3)
    cell_index = lax.axis_index("cell")
    for axis, bit in cell_steps[::-1]:
        on = (cell_index // bit) % 2
        half = qkv_part.shape[0] // 2
        kept = lax.dynamic_slice_in_dim(qkv_part, on * half, half, 0)
        sent = lax.dynamic_slice_in_dim(qkv_part, (1 - on) * half, half, 0)
        qkv_part = add_up(kept, swap(sent, axis, bit)).astype(jnp.bfloat16)
    qkv_part = add_up(qkv_part, swap(qkv_part, "ctx", 1)).astype(jnp.bfloat16)[0]
    send_table, take_table = head_columns(groups, halves, 3, units)
    sent = qkv_part[jnp.asarray(send_table)[head_index, half_index]]
    got = lax.all_to_all(sent, "head", split_axis=0, concat_axis=0, tiled=True)
    taken = jnp.asarray(take_table)[head_index, half_index]
    qkv_weight_grad = jnp.concatenate(
        [got[taken[n, 0], taken[n, 1]] for n in range(take_table.shape[2])], axis=-1
    ).astype(jnp.float32)

    dkv = add_up(dkv, dkv_got).astype(jnp.bfloat16)
    dkv, dq_rows = lax.optimization_barrier((dkv, dq_rows))
    qkv_grad = jnp.concatenate([dq_rows, to_rows(dkv)], axis=-1)
    column_sums = jnp.sum(qkv_grad, axis=0, dtype=jnp.float32)
    query_bias_grad = column_sums[:model_width]
    value_bias_grad = column_sums[2 * model_width :]
    normed_back = jnp.einsum("ne,de->nd", qkv_grad, qkv_weight, preferred_element_type=jnp.float32)
    attn_pull = jax.vjp(layer_norm, residual, attn_gain, attn_shift)[1]
    residual_part, attn_gain_grad, attn_shift_grad = attn_pull(normed_back)
    residual_grad = middle_grad + residual_part
    input_grad = residual_grad.astype(jnp.bfloat16).reshape(cell_count, row_count, model_width)
    cell_totals = jnp.sum(residual_grad.reshape(cell_count, row_count, model_width), axis=1)
    table_grad = jnp.dot(
        one_hot.astype(jnp.float32).T, cell_totals, precision=lax.Precision.HIGHEST
    )

    width = model_width // cells
    vectors = [
        attn_gain_grad,
        attn_shift_grad,
        query_bias_grad,
        value_bias_grad,
        out_bias_grad,
        mlp_gain_grad,
        mlp_shift_grad,
        proj_bias_grad,
    ]
    fc_rows = fc_bias_grad.shape[0] // model_width
    packed = jnp.concatenate(
        [table_grad.reshape(-1, cells, width).transpose(1, 0, 2)]
        + [v.reshape(cells, 1, width) for v in vectors]
        + [fc_bias_grad.reshape(cells, fc_rows, width)],
        axis=1,
    )
    for axis, bit in cell_steps[::-1]:
        on = (cell_index // bit) % 2
        half = packed.shape[0] // 2
        kept = lax.dynamic_slice_in_dim(packed, on * half, half, 0)
        sent = lax.dynamic_slice_in_dim(packed, (1 - on) * half, half, 0)
        packed = kept + swap(sent, axis, bit)
    for axis, bit in ctx_steps + head_steps:
        packed = packed + swap(packed, axis, bit)
    packed = packed[0]
    datasets = dataset_table.shape[0]
    table_grad = packed[:datasets]
    (
        attn_gain_grad,
        attn_shift_grad,
        query_bias_grad,
        value_bias_grad,
        out_bias_grad,
        mlp_gain_grad,
        mlp_shift_grad,
        proj_bias_grad,
    ) = [packed[datasets + n] for n in range(len(vectors))]
    fc_bias_grad = packed[datasets + len(vectors) :].reshape(-1)
    return (
        block_out,
        input_grad,
        table_grad,
        attn_gain_grad,
        attn_shift_grad,
        qkv_weight_grad,
        query_bias_grad,
        value_bias_grad,
        out_weight_grad,
        out_bias_grad,
        mlp_gain_grad,
        mlp_shift_grad,
        fc_weight_grad,
        fc_bias_grad,
        proj_weight_grad,
        proj_bias_grad,
    )


def solution(mesh):
    in_specs = (
        P("cell", ("head", "ctx"), None),
        P("cell"),
        P("cell"),
        P(),
        P(),
        P(),
        P(),
        P(),
        P(),
        P(),
        P(),
        P(),
        P(),
        P(),
        P(),
        P(),
        P(),
        P("cell", ("head", "ctx"), None),
    )
    out_specs = (
        P("cell", ("head", "ctx"), None),
        P("cell", ("head", "ctx"), None),
        P(None, "cell"),
        P("cell"),
        P("cell"),
        P("cell", ("head", "ctx")),
        P("cell"),
        P("cell"),
        P("cell", ("head", "ctx")),
        P("cell"),
        P("cell"),
        P("cell"),
        P("cell", ("head", "ctx")),
        P("cell"),
        P("cell", ("head", "ctx")),
        P("cell"),
    )
    return jax.shard_map(body, mesh=mesh, in_specs=in_specs, out_specs=out_specs, check_vma=False)
```

```python
import math

import jax
import jax.numpy as jnp
from jax import lax
from jax.experimental import pallas as pl
from jax.experimental.pallas import tpu as pltpu
from jax.sharding import PartitionSpec as P
import numpy as np


HEADS = 20
HD = 56


epsilon = 1e-05
MASKED = -1e30
LOG2E = math.log2(math.e)


def layer_norm(values, gain_row, shift_row):
    center = values - jnp.mean(values, axis=-1, keepdims=True)
    spread = jnp.mean(center * center, axis=-1, keepdims=True)
    return center * lax.rsqrt(spread + epsilon) * gain_row + shift_row


def gelu_tanh(values):
    return jax.nn.gelu(values, approximate=True)


def swap(values, axis, bit):
    return lax.ppermute(values, axis, [(i, i ^ bit) for i in range(lax.axis_size(axis))])


def bits_of(axis):
    size, bit, found = lax.axis_size(axis), 1, []
    while bit < size:
        found.append((axis, bit))
        bit *= 2
    return found


def nn(a, b):
    return jnp.dot(a, b, preferred_element_type=jnp.float32)


def nt(a, b):
    return lax.dot_general(a, b, (((1,), (1,)), ((), ())), preferred_element_type=jnp.float32)


def relative_order(count, axis_bits):
    rel = np.zeros((count,), np.int32)
    for s, bit in enumerate(axis_bits):
        rel += ((np.arange(count) >> (len(axis_bits) - 1 - s)) & 1).astype(np.int32) * bit
    return jnp.asarray(rel)


def weight_blocks(pairs, by_cell_left):
    cells, groups, halves = lax.axis_size("cell"), lax.axis_size("head"), lax.axis_size("ctx")
    parts, half_cells = groups * halves, cells // 2
    cell_ids = relative_order(cells, [b for _, b in bits_of("cell")]) ^ lax.axis_index("cell")
    places = jnp.arange(parts, dtype=jnp.int32)
    part_ids = ((places % groups) ^ lax.axis_index("head")) * halves + (
        (places // groups) ^ lax.axis_index("ctx")
    )
    left_ids, right_ids = (cell_ids, part_ids) if by_cell_left else (part_ids, cell_ids)
    left_count, right_count = (cells, parts) if by_cell_left else (parts, cells)
    tokens = pairs[0][0].shape[0]
    left_rows = pairs[0][0].shape[1] // left_count
    rows = left_rows + -left_rows % 16
    widths = [right.shape[1] // right_count for _, right in pairs]
    cols = sum(widths)
    count = len(pairs)

    def kernel(left_at, right_at, *refs):
        sources, (kept, sent), scratch = refs[: 2 * count], refs[2 * count : 2 * count + 2], refs[2 * count + 2 :]
        step = pl.program_id(0)

        @pl.when(step == 0)
        def _():
            turned = scratch[-1]
            turned[...] = jnp.zeros_like(turned)
            for p in range(count):
                left_t = sources[2 * p][...].astype(jnp.float32).T.astype(jnp.bfloat16)
                for n in range(left_count):
                    turned[n, :left_rows] = left_t[n * left_rows : (n + 1) * left_rows]
                for n in range(left_count):
                    scratch[2 * p][n * rows : (n + 1) * rows, :] = turned[left_at[n]]
                width = widths[p]
                for n in range(right_count):
                    scratch[2 * p + 1][n] = sources[2 * p + 1][:, n * width : (n + 1) * width]

        index = step if by_cell_left else (step + half_cells) % cells
        offset = 0
        for p in range(count):
            block = nn(scratch[2 * p][...], scratch[2 * p + 1][right_at[index]])
            at = slice(offset, offset + widths[p])
            offset += widths[p]
            if by_cell_left:
                for n in range(cells):
                    out, place = (kept, n) if n < half_cells else (sent, n - half_cells)
                    out[place, 0, :, at] = block[n * rows : (n + 1) * rows].astype(jnp.bfloat16)
            else:

                def fill(out, block=block, at=at):
                    for n in range(parts):
                        out[0, n, :, at] = block[n * rows : (n + 1) * rows].astype(jnp.bfloat16)

                pl.when(step < half_cells)(lambda: fill(sent))
                pl.when(step >= half_cells)(lambda: fill(kept))

    last = half_cells - 1
    shape = (half_cells, parts, rows, cols)
    if by_cell_left:
        specs = [pl.BlockSpec((half_cells, 1, rows, cols), lambda i, a, b: (0, i, 0, 0))] * 2
    else:
        block_shape = (1, parts, rows, cols)
        specs = [
            pl.BlockSpec(block_shape, lambda i, a, b: (jnp.maximum(i - last - 1, 0), 0, 0, 0)),
            pl.BlockSpec(block_shape, lambda i, a, b: (jnp.minimum(i, last), 0, 0, 0)),
        ]
    scratch = []
    for width in widths:
        scratch.append(pltpu.VMEM((left_count * rows, tokens), jnp.bfloat16))
        scratch.append(pltpu.VMEM((right_count, tokens, width), jnp.bfloat16))
    scratch.append(pltpu.VMEM((left_count, rows, tokens), jnp.bfloat16))
    flat = [x for pair in pairs for x in pair]
    kept, sent = pl.pallas_call(
        kernel,
        out_shape=[jax.ShapeDtypeStruct(shape, jnp.bfloat16)] * 2,
        grid_spec=pltpu.PrefetchScalarGridSpec(
            num_scalar_prefetch=2,
            grid=(right_count,),
            in_specs=[
                pl.BlockSpec(x.shape, lambda i, a, b: (0, 0), pipeline_mode=pl.Buffered(1))
                for x in flat
            ],
            out_specs=specs,
            scratch_shapes=scratch,
        ),
        name="weight_blocks",
    )(left_ids, right_ids, *flat)
    return kept.reshape(-1, rows, cols), sent.reshape(-1, rows, cols)


def add_up(kept, got):
    return kept.astype(jnp.float32) + got.astype(jnp.float32)


def scatter_sum(kept, sent, steps):
    total = None
    for s, (axis, bit) in enumerate(steps):
        if s:
            total = total.astype(jnp.bfloat16)
            half = total.shape[0] // 2
            kept, sent = total[:half], total[half:]
        got = swap(sent, axis, bit)
        total = add_up(kept, got)
    return total[0]


def head_dims(qkv_ref):
    width = qkv_ref.shape[-1] // 3
    return width, width // HD


def chunk_mask(start, seq_len, query_start, rows, cols):
    key_pos = start + lax.broadcasted_iota(jnp.int32, (rows, cols), 0)
    if query_start is None:
        return key_pos < seq_len
    query_pos = query_start + lax.broadcasted_iota(jnp.int32, (rows, cols), 1)
    return (key_pos < seq_len) & (key_pos <= query_pos)


def sweep(i, half, seq_len, rows, visit, blocks):
    def own(j, carry):
        visit(j, (2 * j + half) * rows, False)
        return carry

    def other(j, carry):
        visit(blocks + j, (2 * j + 1 - half) * rows, False)
        return carry

    span = 2 * rows
    own_count = jnp.minimum(i, (seq_len - half * rows + span - 1) // span)
    other_count = jnp.minimum(i + half, (seq_len - (1 - half) * rows + span - 1) // span)
    lax.fori_loop(0, other_count, other, 0)
    lax.fori_loop(0, own_count, own, 0)
    visit(i, (2 * i + half) * rows, True)


def attend_kernel(info, qkv, kv_other, out, out_t, logs, q_t, k_n, v_t, acc, m_ref, l_ref):
    width, heads = head_dims(qkv)
    blocks, rows = q_t.shape[0], q_t.shape[-1]
    seq_len, half = info[0], info[1]
    factor = LOG2E / math.sqrt(HD)

    def prepare(b, carry):
        at = pl.ds(pl.multiple_of(b * rows, rows), rows)
        mine = qkv[at, :]
        mine_t = mine.astype(jnp.float32).T
        theirs = kv_other[at, :]
        theirs_t = theirs[:, width:].astype(jnp.float32).T
        for h in range(heads):
            lo, hi = h * HD, (h + 1) * HD
            q_t[b, h] = mine_t[lo:hi].astype(jnp.bfloat16)
            v_t[b, h] = mine_t[2 * width + lo : 2 * width + hi].astype(jnp.bfloat16)
            k_n[b, h] = mine[:, width + lo : width + hi]
            v_t[blocks + b, h] = theirs_t[lo:hi].astype(jnp.bfloat16)
            k_n[blocks + b, h] = theirs[:, lo:hi]
        return carry

    lax.fori_loop(0, blocks, prepare, 0)

    def block(i, carry):
        acc[...] = jnp.zeros_like(acc)
        m_ref[...] = jnp.full_like(m_ref, MASKED)
        l_ref[...] = jnp.zeros_like(l_ref)

        def visit(j, start, diagonal):
            query_start = (2 * i + half) * rows if diagonal else None
            allowed = chunk_mask(start, seq_len, query_start, rows, rows)
            for h in range(heads):
                s = nn(k_n[j, h], q_t[i, h]) * factor
                s = jnp.where(allowed, s, MASKED)
                old = m_ref[h]
                new = jnp.maximum(old, jnp.max(s, axis=0, keepdims=True))
                shrink = jnp.exp2(old - new)
                p = jnp.exp2(s - new)
                l_ref[h] = l_ref[h] * shrink + jnp.sum(p, axis=0, keepdims=True)
                acc[h] = acc[h] * shrink + nn(v_t[j, h], p.astype(jnp.bfloat16))
                m_ref[h] = new

        sweep(i, half, seq_len, rows, visit, blocks)
        at = pl.ds(pl.multiple_of(i * rows, rows), rows)
        for h in range(heads):
            out_t[i, h * HD : (h + 1) * HD, :] = acc[h] / l_ref[h]
            logs[i, h] = m_ref[h] + jnp.log2(l_ref[h])
        out[at, :] = out_t[i].T.astype(jnp.bfloat16)
        return carry

    lax.fori_loop(0, blocks, block, 0)


def vmem_specs(count):
    return [pl.BlockSpec(memory_space=pltpu.VMEM)] * count


def attend(info, qkv, kv_other, blocks):
    rows_all, wide = qkv.shape
    width = wide // 3
    heads, rows = width // HD, rows_all // blocks
    bf, f32 = jnp.bfloat16, jnp.float32
    pairs = blocks * rows * rows * (blocks + 1)
    return pl.pallas_call(
        attend_kernel,
        out_shape=(
            jax.ShapeDtypeStruct((rows_all, width), bf),
            jax.ShapeDtypeStruct((blocks, width, rows), f32),
            jax.ShapeDtypeStruct((blocks, heads, 1, rows), f32),
        ),
        in_specs=[pl.BlockSpec(memory_space=pltpu.SMEM)] + vmem_specs(2),
        out_specs=tuple(vmem_specs(3)),
        scratch_shapes=[
            pltpu.VMEM((blocks, heads, HD, rows), bf),
            pltpu.VMEM((2 * blocks, heads, rows, HD), bf),
            pltpu.VMEM((2 * blocks, heads, HD, rows), bf),
            pltpu.VMEM((heads, HD, rows), f32),
            pltpu.VMEM((heads, 1, rows), f32),
            pltpu.VMEM((heads, 1, rows), f32),
        ],
        cost_estimate=pl.CostEstimate(
            flops=20 * 1024 * 1024 * 1024, transcendentals=pairs * heads, bytes_accessed=8 * 1024 * 1024
        ),
        name="attend",
    )(info, qkv, kv_other)


def back_kernel(
    info, qkv, kv_other, grad, out_t, logs,
    dq, dkv, dkv_other,
    q_t, g_t, k_n, k_t, v_n, dq_t, dk_t, dv_t, delta,
):
    width, heads = head_dims(qkv)
    blocks, rows = q_t.shape[0], q_t.shape[-1]
    seq_len, half = info[0], info[1]
    scale = 1.0 / math.sqrt(HD)
    factor = LOG2E * scale

    def prepare(b, carry):
        at = pl.ds(pl.multiple_of(b * rows, rows), rows)
        mine = qkv[at, :]
        mine_t = mine[:, : 2 * width].astype(jnp.float32).T
        grad_t = grad[at, :].astype(jnp.float32).T
        theirs = kv_other[at, :]
        theirs_t = theirs[:, :width].astype(jnp.float32).T
        for h in range(heads):
            lo, hi = h * HD, (h + 1) * HD
            q_t[b, h] = mine_t[lo:hi].astype(jnp.bfloat16)
            g_t[b, h] = grad_t[lo:hi].astype(jnp.bfloat16)
            delta[b, h] = jnp.sum(grad_t[lo:hi] * out_t[b, lo:hi], axis=0, keepdims=True)
            k_t[b, h] = mine_t[width + lo : width + hi].astype(jnp.bfloat16)
            k_n[b, h] = mine[:, width + lo : width + hi]
            v_n[b, h] = mine[:, 2 * width + lo : 2 * width + hi]
            k_t[blocks + b, h] = theirs_t[lo:hi].astype(jnp.bfloat16)
            k_n[blocks + b, h] = theirs[:, lo:hi]
            v_n[blocks + b, h] = theirs[:, width + lo : width + hi]
        return carry

    lax.fori_loop(0, blocks, prepare, 0)
    dk_t[...] = jnp.zeros_like(dk_t)
    dv_t[...] = jnp.zeros_like(dv_t)

    def block(i, carry):
        dq_t[...] = jnp.zeros_like(dq_t)

        def visit(j, start, diagonal):
            query_start = (2 * i + half) * rows if diagonal else None
            allowed = chunk_mask(start, seq_len, query_start, rows, rows)
            for h in range(heads):
                at = slice(h * HD, (h + 1) * HD)
                s = nn(k_n[j, h], q_t[i, h]) * factor - logs[i, h]
                p = jnp.exp2(jnp.where(allowed, s, MASKED))
                dv_t[j, at] += nt(g_t[i, h], p.astype(jnp.bfloat16))
                dp = nn(v_n[j, h], g_t[i, h])
                ds = (p * (dp - delta[i, h])).astype(jnp.bfloat16)
                dq_t[at] += nn(k_t[j, h], ds)
                dk_t[j, at] += nt(q_t[i, h], ds)

        sweep(i, half, seq_len, rows, visit, blocks)
        at = pl.ds(pl.multiple_of(i * rows, rows), rows)
        dq[at, :] = (dq_t[...] * scale).T.astype(dq.dtype)
        return carry

    lax.fori_loop(0, blocks, block, 0)

    def finish(b, carry):
        at = pl.ds(pl.multiple_of(b * rows, rows), rows)
        dkv[at, :width] = (dk_t[b] * scale).T.astype(dkv.dtype)
        dkv[at, width:] = dv_t[b].T.astype(dkv.dtype)
        dkv_other[at, :width] = (dk_t[blocks + b] * scale).T.astype(dkv_other.dtype)
        dkv_other[at, width:] = dv_t[blocks + b].T.astype(dkv_other.dtype)
        return carry

    lax.fori_loop(0, blocks, finish, 0)


def attend_back(info, qkv, kv_other, grad, out_t, logs, blocks):
    rows_all, wide = qkv.shape
    width = wide // 3
    heads, rows = width // HD, rows_all // blocks
    bf, f32 = jnp.bfloat16, jnp.float32
    pairs = blocks * rows * rows * (blocks + 1)
    return pl.pallas_call(
        back_kernel,
        out_shape=(
            jax.ShapeDtypeStruct((rows_all, width), bf),
            jax.ShapeDtypeStruct((rows_all, 2 * width), bf),
            jax.ShapeDtypeStruct((rows_all, 2 * width), bf),
        ),
        in_specs=[pl.BlockSpec(memory_space=pltpu.SMEM)] + vmem_specs(5),
        out_specs=tuple(vmem_specs(3)),
        scratch_shapes=[
            pltpu.VMEM((blocks, heads, HD, rows), bf),
            pltpu.VMEM((blocks, heads, HD, rows), bf),
            pltpu.VMEM((2 * blocks, heads, rows, HD), bf),
            pltpu.VMEM((2 * blocks, heads, HD, rows), bf),
            pltpu.VMEM((2 * blocks, heads, rows, HD), bf),
            pltpu.VMEM((width, rows), f32),
            pltpu.VMEM((2 * blocks, width, rows), f32),
            pltpu.VMEM((2 * blocks, width, rows), f32),
            pltpu.VMEM((blocks, heads, 1, rows), f32),
        ],
        cost_estimate=pl.CostEstimate(
            flops=60 * 1024 * 1024 * 1024, transcendentals=pairs * heads, bytes_accessed=8 * 1024 * 1024
        ),
        name="attend_back",
    )(info, qkv, kv_other, grad, out_t, logs)


def head_columns(groups, halves, sections, units):
    local, owned = units // groups, sections * units // (groups * halves)
    send = [[[[] for _ in range(groups)] for _ in range(halves)] for _ in range(groups)]
    take = np.zeros((groups, halves, owned, 2), np.int32)
    for u in range(sections * units):
        section, inside = divmod(u, units)
        source, offset = divmod(inside, local)
        owner, place = divmod(u, owned)
        head, ctx = divmod(owner, halves)
        slots = send[source][ctx][head]
        take[head, ctx, place] = (source, len(slots))
        slots.append(section * local + offset)
    width = max(len(x) for a in send for b in a for x in b)
    table = np.zeros((groups, halves, groups, width), np.int32)
    for a in range(groups):
        for b in range(halves):
            for c in range(groups):
                table[a, b, c, : len(send[a][b][c])] = send[a][b][c]
    return table, take


def body(
    inputs,
    dataset_ids,
    lengths,
    dataset_table,
    attn_gain,
    attn_shift,
    qkv_weight,
    query_bias,
    value_bias,
    out_weight,
    out_bias,
    mlp_gain,
    mlp_shift,
    fc_weight,
    fc_bias,
    proj_weight,
    proj_bias,
    cotangent,
):
    cell_count, row_count, model_width = inputs.shape
    cells = lax.axis_size("cell")
    groups = lax.axis_size("head")
    halves = lax.axis_size("ctx")
    parts = groups * halves
    half_index = lax.axis_index("ctx")
    head_width = HEADS // groups * HD
    token_count = cell_count * row_count
    ctx_rows = groups * row_count
    cell_steps, ctx_steps, head_steps = bits_of("cell"), bits_of("ctx"), bits_of("head")[::-1]
    steps_x = cell_steps + ctx_steps + head_steps
    one_hot = (
        dataset_ids[:, None] == jnp.arange(dataset_table.shape[0], dtype=jnp.int32)[None, :]
    ).astype(jnp.bfloat16)
    embedded = jnp.dot(one_hot, dataset_table, preferred_element_type=jnp.float32)
    residual = (inputs.astype(jnp.float32) + embedded[:, None, :]).reshape(token_count, model_width)
    normed = layer_norm(residual, attn_gain, attn_shift).astype(jnp.bfloat16)
    mixed_qkv = jnp.dot(normed, qkv_weight, preferred_element_type=jnp.float32)
    bias_row = jnp.concatenate([query_bias, jnp.zeros_like(query_bias), value_bias])
    mixed_qkv = (mixed_qkv + bias_row).astype(jnp.bfloat16)
    head_index = lax.axis_index("head")

    def to_heads(values):
        sections = values.shape[1] // model_width
        values = values.reshape(cell_count, row_count, sections, groups, head_width)
        values = values.transpose(3, 0, 1, 2, 4).reshape(groups, cell_count, row_count, -1)
        values = lax.all_to_all(values, "head", split_axis=0, concat_axis=0, tiled=True)
        return values.transpose(1, 0, 2, 3).reshape(cell_count, ctx_rows, -1)

    def to_rows(values):
        sections = values.shape[-1] // head_width
        values = values.reshape(cell_count, groups, row_count, -1).transpose(1, 0, 2, 3)
        values = lax.all_to_all(values, "head", split_axis=0, concat_axis=0, tiled=True)
        values = values.reshape(groups, cell_count, row_count, sections, head_width)
        return values.transpose(1, 2, 3, 0, 4).reshape(token_count, sections * model_width)

    qkv_heads = to_heads(mixed_qkv)
    kv_other = swap(qkv_heads[:, :, head_width:], "ctx", 1)
    normed_near = normed.reshape(cell_count, 1, row_count, model_width)
    normed_near = lax.all_gather(normed_near, "head", axis=1, tiled=True)
    normed_near = normed_near.reshape(cell_count * ctx_rows, model_width)
    normed_far = swap(normed_near, "ctx", 1)
    infos = [jnp.stack([lengths[n], half_index.astype(jnp.int32)]) for n in range(cell_count)]
    runs = [attend(infos[n], qkv_heads[n], kv_other[n], groups) for n in range(cell_count)]
    attended = jnp.stack([r[0] for r in runs])
    attended_rows = to_rows(attended)
    attn_out = jnp.dot(attended_rows, out_weight, preferred_element_type=jnp.float32) + out_bias
    middle = residual + attn_out
    mlp_normed = layer_norm(middle, mlp_gain, mlp_shift).astype(jnp.bfloat16)
    hidden = jnp.dot(mlp_normed, fc_weight, preferred_element_type=jnp.float32) + fc_bias
    active = gelu_tanh(hidden).astype(jnp.bfloat16)
    branch = jnp.dot(active, proj_weight, preferred_element_type=jnp.float32) + proj_bias
    block_out = (middle + branch).astype(jnp.bfloat16).reshape(cell_count, row_count, model_width)
    grad_low = cotangent.reshape(token_count, model_width)
    proj_kept, proj_sent = weight_blocks([(grad_low, active)], False)
    part_columns = model_width // parts
    proj_weight_grad = scatter_sum(proj_kept, proj_sent, steps_x)[:part_columns].T
    grad_top = grad_low.astype(jnp.float32)
    proj_bias_grad = jnp.sum(grad_top, axis=0)
    active_grad = jnp.einsum("nd,fd->nf", grad_low, proj_weight, preferred_element_type=jnp.float32)
    gelu_pull = jax.vjp(gelu_tanh, hidden)[1]
    hidden_grad = gelu_pull(active_grad)[0].astype(jnp.bfloat16)
    fc_bias_grad = jnp.sum(hidden_grad, axis=0, dtype=jnp.float32)
    normed_grad = jnp.einsum(
        "nf,df->nd", hidden_grad, fc_weight, preferred_element_type=jnp.float32
    )
    mlp_pull = jax.vjp(layer_norm, middle, mlp_gain, mlp_shift)[1]
    middle_part, mlp_gain_grad, mlp_shift_grad = mlp_pull(normed_grad)
    middle_grad = grad_top + middle_part
    middle_low = middle_grad.astype(jnp.bfloat16)
    out_bias_grad = jnp.sum(middle_low, axis=0, dtype=jnp.float32)
    attended_grad = jnp.einsum(
        "ne,de->nd", middle_low, out_weight, preferred_element_type=jnp.float32
    ).astype(jnp.bfloat16)
    grad_heads = to_heads(attended_grad)

    fc_kept, fc_sent = weight_blocks([(mlp_normed, hidden_grad), (attended_rows, middle_low)], True)
    fc_out_grad = scatter_sum(fc_kept, fc_sent, steps_x)[: model_width // cells]
    fc_columns = fc_weight.shape[1] // parts
    fc_weight_grad = fc_out_grad[:, :fc_columns]
    out_weight_grad = fc_out_grad[:, fc_columns:]

    backs = [
      attend_back(
        infos[n], qkv_heads[n], kv_other[n], grad_heads[n], runs[n][1], runs[n][2], groups
      )
      for n in range(cell_count)
    ]
    dq = jnp.stack([b[0] for b in backs])
    dkv = jnp.stack([b[1] for b in backs])
    dkv_far = jnp.stack([b[2] for b in backs])

    def tall(values):
        return values.reshape(cell_count * ctx_rows, -1)

    def over_tokens(a, b):
        return jnp.einsum("nd,ne->de", a, b, preferred_element_type=jnp.float32)

    dkv_got = swap(dkv_far, "ctx", 1)
    dq_rows = to_rows(dq)
    qkv_part = jnp.concatenate(
        [
            over_tokens(normed_near, tall(dq)),
            over_tokens(normed_near, tall(dkv)) + over_tokens(normed_far, tall(dkv_far)),
        ],
        axis=1,
    ).astype(jnp.bfloat16)
    units = 2 * groups
    local_units = 3 * units // groups
    qkv_part = qkv_part.reshape(cells, model_width // cells, local_units, -1).transpose(0, 2, 1, 3)
    cell_index = lax.axis_index("cell")
    for axis, bit in cell_steps[::-1]:
        on = (cell_index // bit) % 2
        half = qkv_part.shape[0] // 2
        kept = lax.dynamic_slice_in_dim(qkv_part, on * half, half, 0)
        sent = lax.dynamic_slice_in_dim(qkv_part, (1 - on) * half, half, 0)
        qkv_part = add_up(kept, swap(sent, axis, bit)).astype(jnp.bfloat16)
    qkv_part = add_up(qkv_part, swap(qkv_part, "ctx", 1)).astype(jnp.bfloat16)[0]
    send_table, take_table = head_columns(groups, halves, 3, units)
    sent = qkv_part[jnp.asarray(send_table)[head_index, half_index]]
    got = lax.all_to_all(sent, "head", split_axis=0, concat_axis=0, tiled=True)
    taken = jnp.asarray(take_table)[head_index, half_index]
    qkv_weight_grad = jnp.concatenate(
        [got[taken[n, 0], taken[n, 1]] for n in range(take_table.shape[2])], axis=-1
    ).astype(jnp.float32)

    dkv = add_up(dkv, dkv_got).astype(jnp.bfloat16)
    dkv, dq_rows = lax.optimization_barrier((dkv, dq_rows))
    dkv_rows = to_rows(dkv)
    qkv_grad = jnp.concatenate([dq_rows, dkv_rows], axis=-1)
    column_sums = jnp.sum(qkv_grad, axis=0, dtype=jnp.float32)
    query_bias_grad = column_sums[:model_width]
    value_bias_grad = column_sums[2 * model_width :]
    normed_back = jnp.einsum("ne,de->nd", qkv_grad, qkv_weight, preferred_element_type=jnp.float32)
    attn_pull = jax.vjp(layer_norm, residual, attn_gain, attn_shift)[1]
    residual_part, attn_gain_grad, attn_shift_grad = attn_pull(normed_back)
    residual_grad = middle_grad + residual_part
    input_grad = residual_grad.astype(jnp.bfloat16).reshape(cell_count, row_count, model_width)
    cell_totals = jnp.sum(residual_grad.reshape(cell_count, row_count, model_width), axis=1)
    table_grad = jnp.dot(
        one_hot.astype(jnp.float32).T, cell_totals, precision=lax.Precision.HIGHEST
    )

    width = model_width // cells
    vectors = [
        attn_gain_grad,
        attn_shift_grad,
        query_bias_grad,
        value_bias_grad,
        out_bias_grad,
        mlp_gain_grad,
        mlp_shift_grad,
        proj_bias_grad,
    ]
    fc_rows = fc_bias_grad.shape[0] // model_width
    packed = jnp.concatenate(
        [table_grad.reshape(-1, cells, width).transpose(1, 0, 2)]
        + [v.reshape(cells, 1, width) for v in vectors]
        + [fc_bias_grad.reshape(cells, fc_rows, width)],
        axis=1,
    )
    for axis, bit in cell_steps[::-1]:
        on = (cell_index // bit) % 2
        half = packed.shape[0] // 2
        kept = lax.dynamic_slice_in_dim(packed, on * half, half, 0)
        sent = lax.dynamic_slice_in_dim(packed, (1 - on) * half, half, 0)
        packed = kept + swap(sent, axis, bit)
    for axis, bit in ctx_steps + head_steps:
        packed = packed + swap(packed, axis, bit)
    packed = packed[0]
    datasets = dataset_table.shape[0]
    table_grad = packed[:datasets]
    (
        attn_gain_grad,
        attn_shift_grad,
        query_bias_grad,
        value_bias_grad,
        out_bias_grad,
        mlp_gain_grad,
        mlp_shift_grad,
        proj_bias_grad,
    ) = [packed[datasets + n] for n in range(len(vectors))]
    fc_bias_grad = packed[datasets + len(vectors) :].reshape(-1)
    return (
        block_out,
        input_grad,
        table_grad,
        attn_gain_grad,
        attn_shift_grad,
        qkv_weight_grad,
        query_bias_grad,
        value_bias_grad,
        out_weight_grad,
        out_bias_grad,
        mlp_gain_grad,
        mlp_shift_grad,
        fc_weight_grad,
        fc_bias_grad,
        proj_weight_grad,
        proj_bias_grad,
    )


def solution(mesh):
    in_specs = (
        P("cell", ("head", "ctx"), None),
        P("cell"),
        P("cell"),
        P(),
        P(),
        P(),
        P(),
        P(),
        P(),
        P(),
        P(),
        P(),
        P(),
        P(),
        P(),
        P(),
        P(),
        P("cell", ("head", "ctx"), None),
    )
    out_specs = (
        P("cell", ("head", "ctx"), None),
        P("cell", ("head", "ctx"), None),
        P(None, "cell"),
        P("cell"),
        P("cell"),
        P("cell", ("head", "ctx")),
        P("cell"),
        P("cell"),
        P("cell", ("head", "ctx")),
        P("cell"),
        P("cell"),
        P("cell"),
        P("cell", ("head", "ctx")),
        P("cell"),
        P("cell", ("head", "ctx")),
        P("cell"),
    )
    return jax.shard_map(body, mesh=mesh, in_specs=in_specs, out_specs=out_specs, check_vma=False)
```

```python
import math

import jax
import jax.numpy as jnp
from jax import lax
from jax.experimental import pallas as pl
from jax.experimental.pallas import tpu as pltpu
from jax.sharding import PartitionSpec as P
import numpy as np


HEADS = 20
HD = 56


epsilon = 1e-05
MASKED = -1e30
LOG2E = math.log2(math.e)


def layer_norm(values, gain_row, shift_row):
    center = values - jnp.mean(values, axis=-1, keepdims=True)
    spread = jnp.mean(center * center, axis=-1, keepdims=True)
    return center * lax.rsqrt(spread + epsilon) * gain_row + shift_row


def gelu_tanh(values):
    return jax.nn.gelu(values, approximate=True)


def swap(values, axis, bit):
    return lax.ppermute(values, axis, [(i, i ^ bit) for i in range(lax.axis_size(axis))])


def bits_of(axis):
    size, bit, found = lax.axis_size(axis), 1, []
    while bit < size:
        found.append((axis, bit))
        bit *= 2
    return found


def nn(a, b):
    return jnp.dot(a, b, preferred_element_type=jnp.float32)


def nt(a, b):
    return lax.dot_general(a, b, (((1,), (1,)), ((), ())), preferred_element_type=jnp.float32)


def relative_order(count, axis_bits):
    rel = np.zeros((count,), np.int32)
    for s, bit in enumerate(axis_bits):
        rel += ((np.arange(count) >> (len(axis_bits) - 1 - s)) & 1).astype(np.int32) * bit
    return jnp.asarray(rel)


def weight_blocks(pairs, by_cell_left):
    cells, groups, halves = lax.axis_size("cell"), lax.axis_size("head"), lax.axis_size("ctx")
    parts, half_cells = groups * halves, cells // 2
    cell_ids = relative_order(cells, [b for _, b in bits_of("cell")]) ^ lax.axis_index("cell")
    places = jnp.arange(parts, dtype=jnp.int32)
    part_ids = ((places % groups) ^ lax.axis_index("head")) * halves + (
        (places // groups) ^ lax.axis_index("ctx")
    )
    left_ids, right_ids = (cell_ids, part_ids) if by_cell_left else (part_ids, cell_ids)
    left_count, right_count = (cells, parts) if by_cell_left else (parts, cells)
    tokens = pairs[0][0].shape[0]
    left_rows = pairs[0][0].shape[1] // left_count
    rows = left_rows + -left_rows % 16
    widths = [right.shape[1] // right_count for _, right in pairs]
    cols = sum(widths)
    count = len(pairs)

    def kernel(left_at, right_at, *refs):
        sources, (kept, sent), scratch = refs[: 2 * count], refs[2 * count : 2 * count + 2], refs[2 * count + 2 :]
        step = pl.program_id(0)

        @pl.when(step == 0)
        def _():
            turned = scratch[-1]
            turned[...] = jnp.zeros_like(turned)
            for p in range(count):
                left_t = sources[2 * p][...].astype(jnp.float32).T.astype(jnp.bfloat16)
                for n in range(left_count):
                    turned[n, :left_rows] = left_t[n * left_rows : (n + 1) * left_rows]
                for n in range(left_count):
                    scratch[2 * p][n * rows : (n + 1) * rows, :] = turned[left_at[n]]
                width = widths[p]
                for n in range(right_count):
                    scratch[2 * p + 1][n] = sources[2 * p + 1][:, n * width : (n + 1) * width]

        index = step if by_cell_left else (step + half_cells) % cells
        offset = 0
        for p in range(count):
            block = nn(scratch[2 * p][...], scratch[2 * p + 1][right_at[index]])
            at = slice(offset, offset + widths[p])
            offset += widths[p]
            if by_cell_left:
                for n in range(cells):
                    out, place = (kept, n) if n < half_cells else (sent, n - half_cells)
                    out[place, 0, :, at] = block[n * rows : (n + 1) * rows].astype(jnp.bfloat16)
            else:

                def fill(out, block=block, at=at):
                    for n in range(parts):
                        out[0, n, :, at] = block[n * rows : (n + 1) * rows].astype(jnp.bfloat16)

                pl.when(step < half_cells)(lambda: fill(sent))
                pl.when(step >= half_cells)(lambda: fill(kept))

    last = half_cells - 1
    shape = (half_cells, parts, rows, cols)
    if by_cell_left:
        specs = [pl.BlockSpec((half_cells, 1, rows, cols), lambda i, a, b: (0, i, 0, 0))] * 2
    else:
        block_shape = (1, parts, rows, cols)
        specs = [
            pl.BlockSpec(block_shape, lambda i, a, b: (jnp.maximum(i - last - 1, 0), 0, 0, 0)),
            pl.BlockSpec(block_shape, lambda i, a, b: (jnp.minimum(i, last), 0, 0, 0)),
        ]
    scratch = []
    for width in widths:
        scratch.append(pltpu.VMEM((left_count * rows, tokens), jnp.bfloat16))
        scratch.append(pltpu.VMEM((right_count, tokens, width), jnp.bfloat16))
    scratch.append(pltpu.VMEM((left_count, rows, tokens), jnp.bfloat16))
    flat = [x for pair in pairs for x in pair]
    kept, sent = pl.pallas_call(
        kernel,
        out_shape=[jax.ShapeDtypeStruct(shape, jnp.bfloat16)] * 2,
        grid_spec=pltpu.PrefetchScalarGridSpec(
            num_scalar_prefetch=2,
            grid=(right_count,),
            in_specs=[
                pl.BlockSpec(x.shape, lambda i, a, b: (0, 0), pipeline_mode=pl.Buffered(1))
                for x in flat
            ],
            out_specs=specs,
            scratch_shapes=scratch,
        ),
        name="weight_blocks",
    )(left_ids, right_ids, *flat)
    return kept.reshape(-1, rows, cols), sent.reshape(-1, rows, cols)


def qkv_blocks(near, far, dq, dkv, dkv_far):
    cells = lax.axis_size("cell")
    steps = [b for _, b in bits_of("cell")]
    rel = np.zeros((cells,), np.int32)
    for s, bit in enumerate(steps):
        rel += ((np.arange(cells) >> (len(steps) - 1 - s)) & 1).astype(np.int32) * bit
    place_at = jnp.asarray(np.argsort(rel).astype(np.int32))[
        jnp.arange(cells, dtype=jnp.int32) ^ lax.axis_index("cell")
    ]
    pieces, wide, tokens = near.shape
    rows = wide // cells
    width = dq.shape[1]
    row_at = (jnp.arange(pieces, dtype=jnp.int32) ^ lax.axis_index("head")) * tokens

    def kernel(place, row, near_ref, far_ref, dq_ref, dkv_ref, far_grad, out, tall, q, kv):
        for p in range(pieces):
            at = pl.ds(pl.multiple_of(row[p], tokens), tokens)
            here, there = slice(p * tokens, (p + 1) * tokens), slice(
                (pieces + p) * tokens, (pieces + p + 1) * tokens
            )
            tall[:, here] = near_ref[p]
            tall[:, there] = far_ref[p]
            q[here, :] = dq_ref[at, :]
            kv[here, :] = dkv_ref[at, :]
            kv[there, :] = far_grad[at, :]
        for a in range(cells):
            left = tall[a * rows : (a + 1) * rows, :]
            out[place[a], :, :width] = nn(left[:, : pieces * tokens], q[...]).astype(jnp.bfloat16)
            out[place[a], :, width:] = nn(left, kv[...]).astype(jnp.bfloat16)

    smem = pl.BlockSpec(memory_space=pltpu.SMEM)
    return pl.pallas_call(
        kernel,
        out_shape=jax.ShapeDtypeStruct((cells, rows, 3 * width), jnp.bfloat16),
        in_specs=[smem, smem] + vmem_specs(5),
        out_specs=vmem_specs(1)[0],
        scratch_shapes=[
            pltpu.VMEM((wide, 2 * pieces * tokens), jnp.bfloat16),
            pltpu.VMEM((pieces * tokens, width), jnp.bfloat16),
            pltpu.VMEM((2 * pieces * tokens, 2 * width), jnp.bfloat16),
        ],
        name="qkv_blocks",
    )(place_at, row_at, near, far, dq, dkv, dkv_far)


def add_up(*terms):
    total = terms[0].astype(jnp.float32)
    for term in terms[1:]:
        total = total + term.astype(jnp.float32)
    return total


def scatter_sum(kept, sent, steps, ties=None):
    ties = ties or {}
    terms = [kept]
    for s, (axis, bit) in enumerate(steps):
        if s:
            half = terms[0].shape[0] // 2
            sent = add_up(*[t[half:] for t in terms]).astype(jnp.bfloat16)
            terms = [t[:half] for t in terms]
        if s in ties:
            sent, ties[s][0] = lax.optimization_barrier((sent, ties[s][0]))
        terms.append(swap(sent, axis, bit))
    return add_up(*terms)[0]


def head_dims(qkv_ref):
    width = qkv_ref.shape[-1] // 3
    return width, width // HD


def chunk_mask(start, seq_len, query_start, rows, cols):
    key_pos = start + lax.broadcasted_iota(jnp.int32, (rows, cols), 0)
    if query_start is None:
        return key_pos < seq_len
    query_pos = query_start + lax.broadcasted_iota(jnp.int32, (rows, cols), 1)
    return (key_pos < seq_len) & (key_pos <= query_pos)


def sweep(i, half, seq_len, rows, visit, blocks):
    def own(j, carry):
        visit(j, (2 * j + half) * rows, False)
        return carry

    def other(j, carry):
        visit(blocks + j, (2 * j + 1 - half) * rows, False)
        return carry

    span = 2 * rows
    own_count = jnp.minimum(i, (seq_len - half * rows + span - 1) // span)
    other_count = jnp.minimum(i + half, (seq_len - (1 - half) * rows + span - 1) // span)
    lax.fori_loop(0, other_count, other, 0)
    lax.fori_loop(0, own_count, own, 0)
    visit(i, (2 * i + half) * rows, True)


def attend_kernel(info, qkv, kv_other, out, out_t, logs, q_t, k_n, v_t, acc, m_ref, l_ref):
    width, heads = head_dims(qkv)
    blocks, rows = q_t.shape[0], q_t.shape[-1]
    seq_len, half = info[0], info[1]
    factor = LOG2E / math.sqrt(HD)

    def prepare(b, carry):
        at = pl.ds(pl.multiple_of(b * rows, rows), rows)
        mine = qkv[at, :]
        mine_t = mine.astype(jnp.float32).T
        theirs = kv_other[at, :]
        theirs_t = theirs[:, width:].astype(jnp.float32).T
        for h in range(heads):
            lo, hi = h * HD, (h + 1) * HD
            q_t[b, h] = mine_t[lo:hi].astype(jnp.bfloat16)
            v_t[b, h] = mine_t[2 * width + lo : 2 * width + hi].astype(jnp.bfloat16)
            k_n[b, h] = mine[:, width + lo : width + hi]
            v_t[blocks + b, h] = theirs_t[lo:hi].astype(jnp.bfloat16)
            k_n[blocks + b, h] = theirs[:, lo:hi]
        return carry

    lax.fori_loop(0, blocks, prepare, 0)

    def block(i, carry):
        acc[...] = jnp.zeros_like(acc)
        m_ref[...] = jnp.full_like(m_ref, MASKED)
        l_ref[...] = jnp.zeros_like(l_ref)

        def visit(j, start, diagonal):
            query_start = (2 * i + half) * rows if diagonal else None
            allowed = chunk_mask(start, seq_len, query_start, rows, rows)
            for h in range(heads):
                s = nn(k_n[j, h], q_t[i, h]) * factor
                s = jnp.where(allowed, s, MASKED)
                old = m_ref[h]
                new = jnp.maximum(old, jnp.max(s, axis=0, keepdims=True))
                shrink = jnp.exp2(old - new)
                p = jnp.exp2(s - new)
                l_ref[h] = l_ref[h] * shrink + jnp.sum(p, axis=0, keepdims=True)
                acc[h] = acc[h] * shrink + nn(v_t[j, h], p.astype(jnp.bfloat16))
                m_ref[h] = new

        sweep(i, half, seq_len, rows, visit, blocks)
        at = pl.ds(pl.multiple_of(i * rows, rows), rows)
        for h in range(heads):
            out_t[i, h * HD : (h + 1) * HD, :] = acc[h] / l_ref[h]
            logs[i, h] = m_ref[h] + jnp.log2(l_ref[h])
        out[at, :] = out_t[i].T.astype(jnp.bfloat16)
        return carry

    lax.fori_loop(0, blocks, block, 0)


def vmem_specs(count):
    return [pl.BlockSpec(memory_space=pltpu.VMEM)] * count


def attend(info, qkv, kv_other, blocks):
    rows_all, wide = qkv.shape
    width = wide // 3
    heads, rows = width // HD, rows_all // blocks
    bf, f32 = jnp.bfloat16, jnp.float32
    pairs = blocks * rows * rows * (blocks + 1)
    return pl.pallas_call(
        attend_kernel,
        out_shape=(
            jax.ShapeDtypeStruct((rows_all, width), bf),
            jax.ShapeDtypeStruct((blocks, width, rows), f32),
            jax.ShapeDtypeStruct((blocks, heads, 1, rows), f32),
        ),
        in_specs=[pl.BlockSpec(memory_space=pltpu.SMEM)] + vmem_specs(2),
        out_specs=tuple(vmem_specs(3)),
        scratch_shapes=[
            pltpu.VMEM((blocks, heads, HD, rows), bf),
            pltpu.VMEM((2 * blocks, heads, rows, HD), bf),
            pltpu.VMEM((2 * blocks, heads, HD, rows), bf),
            pltpu.VMEM((heads, HD, rows), f32),
            pltpu.VMEM((heads, 1, rows), f32),
            pltpu.VMEM((heads, 1, rows), f32),
        ],
        cost_estimate=pl.CostEstimate(
            flops=20 * 1024 * 1024 * 1024, transcendentals=pairs * heads, bytes_accessed=8 * 1024 * 1024
        ),
        name="attend",
    )(info, qkv, kv_other)


def back_kernel(
    info, qkv, kv_other, grad, out_t, logs,
    dq, dkv, dkv_other,
    q_t, g_t, k_n, k_t, v_n, dq_t, dk_t, dv_t, delta,
):
    width, heads = head_dims(qkv)
    blocks, rows = q_t.shape[0], q_t.shape[-1]
    seq_len, half = info[0], info[1]
    scale = 1.0 / math.sqrt(HD)
    factor = LOG2E * scale

    def prepare(b, carry):
        at = pl.ds(pl.multiple_of(b * rows, rows), rows)
        mine = qkv[at, :]
        mine_t = mine[:, : 2 * width].astype(jnp.float32).T
        grad_t = grad[at, :].astype(jnp.float32).T
        theirs = kv_other[at, :]
        theirs_t = theirs[:, :width].astype(jnp.float32).T
        for h in range(heads):
            lo, hi = h * HD, (h + 1) * HD
            q_t[b, h] = mine_t[lo:hi].astype(jnp.bfloat16)
            g_t[b, h] = grad_t[lo:hi].astype(jnp.bfloat16)
            delta[b, h] = jnp.sum(grad_t[lo:hi] * out_t[b, lo:hi], axis=0, keepdims=True)
            k_t[b, h] = mine_t[width + lo : width + hi].astype(jnp.bfloat16)
            k_n[b, h] = mine[:, width + lo : width + hi]
            v_n[b, h] = mine[:, 2 * width + lo : 2 * width + hi]
            k_t[blocks + b, h] = theirs_t[lo:hi].astype(jnp.bfloat16)
            k_n[blocks + b, h] = theirs[:, lo:hi]
            v_n[blocks + b, h] = theirs[:, width + lo : width + hi]
        return carry

    lax.fori_loop(0, blocks, prepare, 0)
    dk_t[...] = jnp.zeros_like(dk_t)
    dv_t[...] = jnp.zeros_like(dv_t)

    def block(i, carry):
        dq_t[...] = jnp.zeros_like(dq_t)

        def visit(j, start, diagonal):
            query_start = (2 * i + half) * rows if diagonal else None
            allowed = chunk_mask(start, seq_len, query_start, rows, rows)
            for h in range(heads):
                at = slice(h * HD, (h + 1) * HD)
                s = nn(k_n[j, h], q_t[i, h]) * factor - logs[i, h]
                p = jnp.exp2(jnp.where(allowed, s, MASKED))
                dv_t[j, at] += nt(g_t[i, h], p.astype(jnp.bfloat16))
                dp = nn(v_n[j, h], g_t[i, h])
                ds = (p * (dp - delta[i, h])).astype(jnp.bfloat16)
                dq_t[at] += nn(k_t[j, h], ds)
                dk_t[j, at] += nt(q_t[i, h], ds)

        sweep(i, half, seq_len, rows, visit, blocks)
        at = pl.ds(pl.multiple_of(i * rows, rows), rows)
        dq[at, :] = (dq_t[...] * scale).T.astype(dq.dtype)
        return carry

    lax.fori_loop(0, blocks, block, 0)

    def finish(b, carry):
        at = pl.ds(pl.multiple_of(b * rows, rows), rows)
        dkv[at, :width] = (dk_t[b] * scale).T.astype(dkv.dtype)
        dkv[at, width:] = dv_t[b].T.astype(dkv.dtype)
        dkv_other[at, :width] = (dk_t[blocks + b] * scale).T.astype(dkv_other.dtype)
        dkv_other[at, width:] = dv_t[blocks + b].T.astype(dkv_other.dtype)
        return carry

    lax.fori_loop(0, blocks, finish, 0)


def attend_back(info, qkv, kv_other, grad, out_t, logs, blocks):
    rows_all, wide = qkv.shape
    width = wide // 3
    heads, rows = width // HD, rows_all // blocks
    bf, f32 = jnp.bfloat16, jnp.float32
    pairs = blocks * rows * rows * (blocks + 1)
    return pl.pallas_call(
        back_kernel,
        out_shape=(
            jax.ShapeDtypeStruct((rows_all, width), bf),
            jax.ShapeDtypeStruct((rows_all, 2 * width), bf),
            jax.ShapeDtypeStruct((rows_all, 2 * width), bf),
        ),
        in_specs=[pl.BlockSpec(memory_space=pltpu.SMEM)] + vmem_specs(5),
        out_specs=tuple(vmem_specs(3)),
        scratch_shapes=[
            pltpu.VMEM((blocks, heads, HD, rows), bf),
            pltpu.VMEM((blocks, heads, HD, rows), bf),
            pltpu.VMEM((2 * blocks, heads, rows, HD), bf),
            pltpu.VMEM((2 * blocks, heads, HD, rows), bf),
            pltpu.VMEM((2 * blocks, heads, rows, HD), bf),
            pltpu.VMEM((width, rows), f32),
            pltpu.VMEM((2 * blocks, width, rows), f32),
            pltpu.VMEM((2 * blocks, width, rows), f32),
            pltpu.VMEM((blocks, heads, 1, rows), f32),
        ],
        cost_estimate=pl.CostEstimate(
            flops=60 * 1024 * 1024 * 1024, transcendentals=pairs * heads, bytes_accessed=8 * 1024 * 1024
        ),
        name="attend_back",
    )(info, qkv, kv_other, grad, out_t, logs)


def head_columns(groups, halves, sections, units):
    local, owned = units // groups, sections * units // (groups * halves)
    send = [[[[] for _ in range(groups)] for _ in range(halves)] for _ in range(groups)]
    take = np.zeros((groups, halves, owned, 2), np.int32)
    for u in range(sections * units):
        section, inside = divmod(u, units)
        source, offset = divmod(inside, local)
        owner, place = divmod(u, owned)
        head, ctx = divmod(owner, halves)
        slots = send[source][ctx][head]
        take[head, ctx, place] = (source, len(slots))
        slots.append(section * local + offset)
    width = max(len(x) for a in send for b in a for x in b)
    table = np.zeros((groups, halves, groups, width), np.int32)
    for a in range(groups):
        for b in range(halves):
            for c in range(groups):
                table[a, b, c, : len(send[a][b][c])] = send[a][b][c]
    return table, take


def body(
    inputs,
    dataset_ids,
    lengths,
    dataset_table,
    attn_gain,
    attn_shift,
    qkv_weight,
    query_bias,
    value_bias,
    out_weight,
    out_bias,
    mlp_gain,
    mlp_shift,
    fc_weight,
    fc_bias,
    proj_weight,
    proj_bias,
    cotangent,
):
    cell_count, row_count, model_width = inputs.shape
    cells = lax.axis_size("cell")
    groups = lax.axis_size("head")
    halves = lax.axis_size("ctx")
    parts = groups * halves
    half_index = lax.axis_index("ctx")
    head_width = HEADS // groups * HD
    token_count = cell_count * row_count
    ctx_rows = groups * row_count
    cell_steps, ctx_steps, head_steps = bits_of("cell"), bits_of("ctx"), bits_of("head")[::-1]
    steps_x = cell_steps + ctx_steps + head_steps
    one_hot = (
        dataset_ids[:, None] == jnp.arange(dataset_table.shape[0], dtype=jnp.int32)[None, :]
    ).astype(jnp.bfloat16)
    embedded = jnp.dot(one_hot, dataset_table, preferred_element_type=jnp.float32)
    residual = (inputs.astype(jnp.float32) + embedded[:, None, :]).reshape(token_count, model_width)
    normed = layer_norm(residual, attn_gain, attn_shift).astype(jnp.bfloat16)
    mixed_qkv = jnp.dot(normed, qkv_weight, preferred_element_type=jnp.float32)
    bias_row = jnp.concatenate([query_bias, jnp.zeros_like(query_bias), value_bias])
    mixed_qkv = (mixed_qkv + bias_row).astype(jnp.bfloat16)
    head_index = lax.axis_index("head")

    def to_heads(values):
        sections = values.shape[1] // model_width
        values = values.reshape(cell_count, row_count, sections, groups, head_width)
        values = values.transpose(3, 0, 1, 2, 4).reshape(groups, cell_count, row_count, -1)
        values = lax.all_to_all(values, "head", split_axis=0, concat_axis=0, tiled=True)
        return values.transpose(1, 0, 2, 3).reshape(cell_count, ctx_rows, -1)

    def to_rows(values):
        sections = values.shape[-1] // head_width
        values = values.reshape(cell_count, groups, row_count, -1).transpose(1, 0, 2, 3)
        values = lax.all_to_all(values, "head", split_axis=0, concat_axis=0, tiled=True)
        values = values.reshape(groups, cell_count, row_count, sections, head_width)
        return values.transpose(1, 2, 3, 0, 4).reshape(token_count, sections * model_width)

    qkv_heads = to_heads(mixed_qkv)
    kv_other = swap(qkv_heads[:, :, head_width:], "ctx", 1)
    normed_t = normed.T.reshape(cells, model_width // cells, token_count)
    normed_t = jnp.pad(normed_t, ((0, 0), (0, -normed_t.shape[1] % 16), (0, 0)))
    normed_t, kv_other = lax.optimization_barrier((normed_t.reshape(-1, token_count), kv_other))
    pieces = [normed_t]
    for p in range(1, groups):
        pieces.append(swap(normed_t, "head", p))
    normed_near = jnp.stack(pieces)
    normed_far = swap(normed_near, "ctx", 1)
    infos = [jnp.stack([lengths[n], half_index.astype(jnp.int32)]) for n in range(cell_count)]
    runs = [attend(infos[n], qkv_heads[n], kv_other[n], groups) for n in range(cell_count)]
    attended = jnp.stack([r[0] for r in runs])
    attended_rows = to_rows(attended)
    attn_out = jnp.dot(attended_rows, out_weight, preferred_element_type=jnp.float32) + out_bias
    middle = residual + attn_out
    mlp_normed = layer_norm(middle, mlp_gain, mlp_shift).astype(jnp.bfloat16)
    hidden = jnp.dot(mlp_normed, fc_weight, preferred_element_type=jnp.float32) + fc_bias
    active = gelu_tanh(hidden).astype(jnp.bfloat16)
    branch = jnp.dot(active, proj_weight, preferred_element_type=jnp.float32) + proj_bias
    block_out = (middle + branch).astype(jnp.bfloat16).reshape(cell_count, row_count, model_width)
    grad_low = cotangent.reshape(token_count, model_width)
    proj_kept, proj_sent = weight_blocks([(grad_low, active)], False)
    part_columns = model_width // parts
    grad_top = grad_low.astype(jnp.float32)
    proj_bias_grad = jnp.sum(grad_top, axis=0)
    active_grad = jnp.einsum("nd,fd->nf", grad_low, proj_weight, preferred_element_type=jnp.float32)
    gelu_pull = jax.vjp(gelu_tanh, hidden)[1]
    hidden_grad = gelu_pull(active_grad)[0].astype(jnp.bfloat16)
    fc_bias_grad = jnp.sum(hidden_grad, axis=0, dtype=jnp.float32)
    hidden_tie = [hidden_grad]
    proj_total = scatter_sum(proj_kept, proj_sent, steps_x, {1: hidden_tie})
    proj_weight_grad = proj_total[:part_columns].T
    hidden_grad = hidden_tie[0]
    normed_grad = jnp.einsum(
        "nf,df->nd", hidden_grad, fc_weight, preferred_element_type=jnp.float32
    )
    mlp_pull = jax.vjp(layer_norm, middle, mlp_gain, mlp_shift)[1]
    middle_part, mlp_gain_grad, mlp_shift_grad = mlp_pull(normed_grad)
    middle_grad = grad_top + middle_part
    middle_low = middle_grad.astype(jnp.bfloat16)
    out_bias_grad = jnp.sum(middle_low, axis=0, dtype=jnp.float32)
    attended_grad = jnp.einsum(
        "ne,de->nd", middle_low, out_weight, preferred_element_type=jnp.float32
    ).astype(jnp.bfloat16)
    grad_heads = to_heads(attended_grad)

    fc_kept, fc_sent = weight_blocks([(mlp_normed, hidden_grad), (attended_rows, middle_low)], True)
    back_tie = [grad_heads]
    fc_out_grad = scatter_sum(fc_kept, fc_sent, steps_x, {1: back_tie})
    grad_heads = back_tie[0]
    fc_out_grad = fc_out_grad[: model_width // cells]
    fc_columns = fc_weight.shape[1] // parts
    fc_weight_grad = fc_out_grad[:, :fc_columns]
    out_weight_grad = fc_out_grad[:, fc_columns:]

    backs = [
      attend_back(
        infos[n], qkv_heads[n], kv_other[n], grad_heads[n], runs[n][1], runs[n][2], groups
      )
      for n in range(cell_count)
    ]
    dq = jnp.stack([b[0] for b in backs])
    dkv = jnp.stack([b[1] for b in backs])
    dkv_far = jnp.stack([b[2] for b in backs])

    dkv_got = swap(dkv_far, "ctx", 1)
    dq_rows = to_rows(dq)
    qkv_part = qkv_blocks(normed_near, normed_far, dq[0], dkv[0], dkv_far[0])
    half_cells = cells // 2
    qkv_part = scatter_sum(qkv_part[:half_cells], qkv_part[half_cells:], cell_steps)
    qkv_part = qkv_part[: model_width // cells].astype(jnp.bfloat16)
    qkv_part = add_up(qkv_part, swap(qkv_part, "ctx", 1)).astype(jnp.bfloat16)
    units = 2 * groups
    qkv_part = qkv_part.reshape(qkv_part.shape[0], 3 * units // groups, -1).transpose(1, 0, 2)
    send_table, take_table = head_columns(groups, halves, 3, units)
    sent = qkv_part[jnp.asarray(send_table)[head_index, half_index]]
    got = lax.all_to_all(sent, "head", split_axis=0, concat_axis=0, tiled=True)
    taken = jnp.asarray(take_table)[head_index, half_index]
    qkv_weight_grad = jnp.concatenate(
        [got[taken[n, 0], taken[n, 1]] for n in range(take_table.shape[2])], axis=-1
    ).astype(jnp.float32)

    dkv = add_up(dkv, dkv_got).astype(jnp.bfloat16)
    dkv, dq_rows = lax.optimization_barrier((dkv, dq_rows))
    dkv_rows = to_rows(dkv)
    qkv_grad = jnp.concatenate([dq_rows, dkv_rows], axis=-1)
    column_sums = jnp.sum(qkv_grad, axis=0, dtype=jnp.float32)
    query_bias_grad = column_sums[:model_width]
    value_bias_grad = column_sums[2 * model_width :]
    normed_back = jnp.einsum("ne,de->nd", qkv_grad, qkv_weight, preferred_element_type=jnp.float32)
    attn_pull = jax.vjp(layer_norm, residual, attn_gain, attn_shift)[1]
    residual_part, attn_gain_grad, attn_shift_grad = attn_pull(normed_back)
    residual_grad = middle_grad + residual_part
    input_grad = residual_grad.astype(jnp.bfloat16).reshape(cell_count, row_count, model_width)
    cell_totals = jnp.sum(residual_grad.reshape(cell_count, row_count, model_width), axis=1)
    table_grad = jnp.dot(
        one_hot.astype(jnp.float32).T, cell_totals, precision=lax.Precision.HIGHEST
    )

    width = model_width // cells
    vectors = [
        attn_gain_grad,
        attn_shift_grad,
        query_bias_grad,
        value_bias_grad,
        out_bias_grad,
        mlp_gain_grad,
        mlp_shift_grad,
        proj_bias_grad,
    ]
    fc_rows = fc_bias_grad.shape[0] // model_width
    packed = jnp.concatenate(
        [table_grad.reshape(-1, cells, width).transpose(1, 0, 2)]
        + [v.reshape(cells, 1, width) for v in vectors]
        + [fc_bias_grad.reshape(cells, fc_rows, width)],
        axis=1,
    )
    cell_index = lax.axis_index("cell")
    for axis, bit in cell_steps[::-1]:
        on = (cell_index // bit) % 2
        half = packed.shape[0] // 2
        kept = lax.dynamic_slice_in_dim(packed, on * half, half, 0)
        sent = lax.dynamic_slice_in_dim(packed, (1 - on) * half, half, 0)
        packed = kept + swap(sent, axis, bit)
    for axis, bit in ctx_steps + head_steps:
        packed = packed + swap(packed, axis, bit)
    packed = packed[0]
    datasets = dataset_table.shape[0]
    table_grad = packed[:datasets]
    (
        attn_gain_grad,
        attn_shift_grad,
        query_bias_grad,
        value_bias_grad,
        out_bias_grad,
        mlp_gain_grad,
        mlp_shift_grad,
        proj_bias_grad,
    ) = [packed[datasets + n] for n in range(len(vectors))]
    fc_bias_grad = packed[datasets + len(vectors) :].reshape(-1)
    return (
        block_out,
        input_grad,
        table_grad,
        attn_gain_grad,
        attn_shift_grad,
        qkv_weight_grad,
        query_bias_grad,
        value_bias_grad,
        out_weight_grad,
        out_bias_grad,
        mlp_gain_grad,
        mlp_shift_grad,
        fc_weight_grad,
        fc_bias_grad,
        proj_weight_grad,
        proj_bias_grad,
    )


def solution(mesh):
    in_specs = (
        P("cell", ("head", "ctx"), None),
        P("cell"),
        P("cell"),
        P(),
        P(),
        P(),
        P(),
        P(),
        P(),
        P(),
        P(),
        P(),
        P(),
        P(),
        P(),
        P(),
        P(),
        P("cell", ("head", "ctx"), None),
    )
    out_specs = (
        P("cell", ("head", "ctx"), None),
        P("cell", ("head", "ctx"), None),
        P(None, "cell"),
        P("cell"),
        P("cell"),
        P("cell", ("head", "ctx")),
        P("cell"),
        P("cell"),
        P("cell", ("head", "ctx")),
        P("cell"),
        P("cell"),
        P("cell"),
        P("cell", ("head", "ctx")),
        P("cell"),
        P("cell", ("head", "ctx")),
        P("cell"),
    )
    return jax.shard_map(body, mesh=mesh, in_specs=in_specs, out_specs=out_specs, check_vma=False)
```

```python
import math

import jax
import jax.numpy as jnp
from jax import lax
from jax.experimental import pallas as pl
from jax.experimental.pallas import tpu as pltpu
from jax.sharding import PartitionSpec as P
import numpy as np


HEADS = 20
HD = 56


epsilon = 1e-05
MASKED = -1e30
LOG2E = math.log2(math.e)


CELL, HEAD, CTX = "cell", "head", "ctx"


def layer_norm(values, gain_row, shift_row):
    center = values - jnp.mean(values, axis=-1, keepdims=True)
    spread = jnp.mean(center * center, axis=-1, keepdims=True)
    return center * lax.rsqrt(spread + epsilon) * gain_row + shift_row


def gelu_tanh(values):
    return jax.nn.gelu(values, approximate=True)


def swap(values, axis, bit):
    return lax.ppermute(values, axis, [(i, i ^ bit) for i in range(lax.axis_size(axis))])


def bits_of(axis):
    size, bit, found = lax.axis_size(axis), 1, []
    while bit < size:
        found.append((axis, bit))
        bit *= 2
    return found


def nn(a, b):
    return jnp.dot(a, b, preferred_element_type=jnp.float32)


def nt(a, b):
    return lax.dot_general(a, b, (((1,), (1,)), ((), ())), preferred_element_type=jnp.float32)


def relative_order(count, axis_bits):
    rel = np.zeros((count,), np.int32)
    for s, bit in enumerate(axis_bits):
        rel += ((np.arange(count) >> (len(axis_bits) - 1 - s)) & 1).astype(np.int32) * bit
    return jnp.asarray(rel)


def weight_blocks(pairs, by_cell_left):
    cells, groups, halves = lax.axis_size(CELL), lax.axis_size(HEAD), lax.axis_size(CTX)
    parts, half_cells = groups * halves, cells // 2
    cell_ids = relative_order(cells, [b for _, b in bits_of(CELL)]) ^ lax.axis_index(CELL)
    places = jnp.arange(parts, dtype=jnp.int32)
    part_ids = ((places % groups) ^ lax.axis_index(HEAD)) * halves + (
        (places // groups) ^ lax.axis_index(CTX)
    )
    left_ids, right_ids = (cell_ids, part_ids) if by_cell_left else (part_ids, cell_ids)
    left_count, right_count = (cells, parts) if by_cell_left else (parts, cells)
    tokens = pairs[0][0].shape[0]
    left_rows = pairs[0][0].shape[1] // left_count
    rows = left_rows + -left_rows % 16
    widths = [right.shape[1] // right_count for _, right in pairs]
    cols = sum(widths)
    count = len(pairs)

    def kernel(left_at, right_at, *refs):
        sources, (kept, sent), scratch = refs[: 2 * count], refs[2 * count : 2 * count + 2], refs[2 * count + 2 :]
        step = pl.program_id(0)

        @pl.when(step == 0)
        def _():
            turned = scratch[-1]
            turned[...] = jnp.zeros_like(turned)
            for p in range(count):
                left_t = sources[2 * p][...].astype(jnp.float32).T.astype(jnp.bfloat16)
                for n in range(left_count):
                    turned[n, :left_rows] = left_t[n * left_rows : (n + 1) * left_rows]
                for n in range(left_count):
                    scratch[2 * p][n * rows : (n + 1) * rows, :] = turned[left_at[n]]
                width = widths[p]
                for n in range(right_count):
                    scratch[2 * p + 1][n] = sources[2 * p + 1][:, n * width : (n + 1) * width]

        index = step if by_cell_left else (step + half_cells) % cells
        offset = 0
        for p in range(count):
            block = nn(scratch[2 * p][...], scratch[2 * p + 1][right_at[index]])
            at = slice(offset, offset + widths[p])
            offset += widths[p]
            if by_cell_left:
                for n in range(cells):
                    out, place = (kept, n) if n < half_cells else (sent, n - half_cells)
                    out[place, 0, :, at] = block[n * rows : (n + 1) * rows].astype(jnp.bfloat16)
            else:

                def fill(out, block=block, at=at):
                    for n in range(parts):
                        out[0, n, :, at] = block[n * rows : (n + 1) * rows].astype(jnp.bfloat16)

                pl.when(step < half_cells)(lambda: fill(sent))
                pl.when(step >= half_cells)(lambda: fill(kept))

    last = half_cells - 1
    shape = (half_cells, parts, rows, cols)
    if by_cell_left:
        specs = [pl.BlockSpec((half_cells, 1, rows, cols), lambda i, a, b: (0, i, 0, 0))] * 2
    else:
        block_shape = (1, parts, rows, cols)
        specs = [
            pl.BlockSpec(block_shape, lambda i, a, b: (jnp.maximum(i - last - 1, 0), 0, 0, 0)),
            pl.BlockSpec(block_shape, lambda i, a, b: (jnp.minimum(i, last), 0, 0, 0)),
        ]
    scratch = []
    for width in widths:
        scratch.append(pltpu.VMEM((left_count * rows, tokens), jnp.bfloat16))
        scratch.append(pltpu.VMEM((right_count, tokens, width), jnp.bfloat16))
    scratch.append(pltpu.VMEM((left_count, rows, tokens), jnp.bfloat16))
    flat = [x for pair in pairs for x in pair]
    kept, sent = pl.pallas_call(
        kernel,
        out_shape=[jax.ShapeDtypeStruct(shape, jnp.bfloat16)] * 2,
        grid_spec=pltpu.PrefetchScalarGridSpec(
            num_scalar_prefetch=2,
            grid=(right_count,),
            in_specs=[
                pl.BlockSpec(x.shape, lambda i, a, b: (0, 0), pipeline_mode=pl.Buffered(1))
                for x in flat
            ],
            out_specs=specs,
            scratch_shapes=scratch,
        ),
        name="wb",
    )(left_ids, right_ids, *flat)
    return kept.reshape(-1, rows, cols), sent.reshape(-1, rows, cols)


def qkv_blocks(near, far, dq, dkv, dkv_far):
    cells = lax.axis_size(CELL)
    steps = [b for _, b in bits_of(CELL)]
    rel = np.zeros((cells,), np.int32)
    for s, bit in enumerate(steps):
        rel += ((np.arange(cells) >> (len(steps) - 1 - s)) & 1).astype(np.int32) * bit
    place_at = jnp.asarray(np.argsort(rel).astype(np.int32))[
        jnp.arange(cells, dtype=jnp.int32) ^ lax.axis_index(CELL)
    ]
    pieces, wide, tokens = near.shape
    rows = wide // cells
    width = dq.shape[1]
    row_at = (jnp.arange(pieces, dtype=jnp.int32) ^ lax.axis_index(HEAD)) * tokens

    def kernel(place, row, near_ref, far_ref, dq_ref, dkv_ref, far_grad, out, tall, q, kv):
        for p in range(pieces):
            at = pl.ds(pl.multiple_of(row[p], tokens), tokens)
            here, there = slice(p * tokens, (p + 1) * tokens), slice(
                (pieces + p) * tokens, (pieces + p + 1) * tokens
            )
            tall[:, here] = near_ref[p]
            tall[:, there] = far_ref[p]
            q[here, :] = dq_ref[at, :]
            kv[here, :] = dkv_ref[at, :]
            kv[there, :] = far_grad[at, :]
        for a in range(cells):
            left = tall[a * rows : (a + 1) * rows, :]
            out[place[a], :, :width] = nn(left[:, : pieces * tokens], q[...]).astype(jnp.bfloat16)
            out[place[a], :, width:] = nn(left, kv[...]).astype(jnp.bfloat16)

    smem = pl.BlockSpec(memory_space=pltpu.SMEM)
    return pl.pallas_call(
        kernel,
        out_shape=jax.ShapeDtypeStruct((cells, rows, 3 * width), jnp.bfloat16),
        in_specs=[smem, smem] + vmem_specs(5),
        out_specs=vmem_specs(1)[0],
        scratch_shapes=[
            pltpu.VMEM((wide, 2 * pieces * tokens), jnp.bfloat16),
            pltpu.VMEM((pieces * tokens, width), jnp.bfloat16),
            pltpu.VMEM((2 * pieces * tokens, 2 * width), jnp.bfloat16),
        ],
        name="qb",
    )(place_at, row_at, near, far, dq, dkv, dkv_far)


def add_up(*terms):
    total = terms[0].astype(jnp.float32)
    for term in terms[1:]:
        total = total + term.astype(jnp.float32)
    return total


def scatter_sum(kept, sent, steps, ties=None):
    ties = ties or {}
    terms = [kept]
    for s, (axis, bit) in enumerate(steps):
        if s:
            half = terms[0].shape[0] // 2
            sent = add_up(*[t[half:] for t in terms]).astype(jnp.bfloat16)
            terms = [t[:half] for t in terms]
        if s in ties:
            sent, ties[s][0] = lax.optimization_barrier((sent, ties[s][0]))
        terms.append(swap(sent, axis, bit))
    return add_up(*terms)[0]


def head_dims(query):
    width = query.shape[-1]
    return width, width // HD


def chunk_mask(start, seq_len, query_start, rows, cols):
    key_pos = start + lax.broadcasted_iota(jnp.int32, (rows, cols), 0)
    if query_start is None:
        return key_pos < seq_len
    query_pos = query_start + lax.broadcasted_iota(jnp.int32, (rows, cols), 1)
    return (key_pos < seq_len) & (key_pos <= query_pos)


def sweep(i, half, seq_len, rows, visit, blocks):
    def own(j, carry):
        visit(j, (2 * j + half) * rows, False)
        return carry

    def other(j, carry):
        visit(blocks + j, (2 * j + 1 - half) * rows, False)
        return carry

    span = 2 * rows
    own_count = jnp.minimum(i, (seq_len - half * rows + span - 1) // span)
    other_count = jnp.minimum(i + half, (seq_len - (1 - half) * rows + span - 1) // span)
    lax.fori_loop(0, other_count, other, 0)
    lax.fori_loop(0, own_count, own, 0)
    visit(i, (2 * i + half) * rows, True)


def attend_kernel(info, query, kv_near, kv_other, out, out_t, logs, q_t, k_n, v_t, acc, m_ref, l_ref):
    width, heads = head_dims(query)
    blocks, rows = q_t.shape[0], q_t.shape[-1]
    seq_len, half = info[0], info[1]
    factor = LOG2E / math.sqrt(HD)

    def prepare(b, carry):
        at = pl.ds(pl.multiple_of(b * rows, rows), rows)
        query_t = query[at, :].astype(jnp.float32).T
        mine = kv_near[at, :]
        mine_t = mine[:, width:].astype(jnp.float32).T
        theirs = kv_other[at, :]
        theirs_t = theirs[:, width:].astype(jnp.float32).T
        for h in range(heads):
            lo, hi = h * HD, (h + 1) * HD
            q_t[b, h] = query_t[lo:hi].astype(jnp.bfloat16)
            v_t[b, h] = mine_t[lo:hi].astype(jnp.bfloat16)
            k_n[b, h] = mine[:, lo:hi]
            v_t[blocks + b, h] = theirs_t[lo:hi].astype(jnp.bfloat16)
            k_n[blocks + b, h] = theirs[:, lo:hi]
        return carry

    lax.fori_loop(0, blocks, prepare, 0)

    def block(i, carry):
        acc[...] = jnp.zeros_like(acc)
        m_ref[...] = jnp.full_like(m_ref, MASKED)
        l_ref[...] = jnp.zeros_like(l_ref)

        def visit(j, start, diagonal):
            query_start = (2 * i + half) * rows if diagonal else None
            allowed = chunk_mask(start, seq_len, query_start, rows, rows)
            for h in range(heads):
                s = nn(k_n[j, h], q_t[i, h]) * factor
                s = jnp.where(allowed, s, MASKED)
                old = m_ref[h]
                new = jnp.maximum(old, jnp.max(s, axis=0, keepdims=True))
                shrink = jnp.exp2(old - new)
                p = jnp.exp2(s - new)
                l_ref[h] = l_ref[h] * shrink + jnp.sum(p, axis=0, keepdims=True)
                acc[h] = acc[h] * shrink + nn(v_t[j, h], p.astype(jnp.bfloat16))
                m_ref[h] = new

        sweep(i, half, seq_len, rows, visit, blocks)
        at = pl.ds(pl.multiple_of(i * rows, rows), rows)
        for h in range(heads):
            out_t[i, h * HD : (h + 1) * HD, :] = acc[h] / l_ref[h]
            logs[i, h] = m_ref[h] + jnp.log2(l_ref[h])
        out[at, :] = out_t[i].T.astype(jnp.bfloat16)
        return carry

    lax.fori_loop(0, blocks, block, 0)


def vmem_specs(count):
    return [pl.BlockSpec(memory_space=pltpu.VMEM)] * count


def attend(info, query, kv_near, kv_other, blocks):
    rows_all, width = query.shape
    heads, rows = width // HD, rows_all // blocks
    bf, f32 = jnp.bfloat16, jnp.float32
    pairs = blocks * rows * rows * (blocks + 1)
    return pl.pallas_call(
        attend_kernel,
        out_shape=(
            jax.ShapeDtypeStruct((rows_all, width), bf),
            jax.ShapeDtypeStruct((blocks, width, rows), f32),
            jax.ShapeDtypeStruct((blocks, heads, 1, rows), f32),
        ),
        in_specs=[pl.BlockSpec(memory_space=pltpu.SMEM)] + vmem_specs(3),
        out_specs=tuple(vmem_specs(3)),
        scratch_shapes=[
            pltpu.VMEM((blocks, heads, HD, rows), bf),
            pltpu.VMEM((2 * blocks, heads, rows, HD), bf),
            pltpu.VMEM((2 * blocks, heads, HD, rows), bf),
            pltpu.VMEM((heads, HD, rows), f32),
            pltpu.VMEM((heads, 1, rows), f32),
            pltpu.VMEM((heads, 1, rows), f32),
        ],
        cost_estimate=pl.CostEstimate(
            flops=20 * 1024 * 1024 * 1024, transcendentals=pairs * heads, bytes_accessed=8 * 1024 * 1024
        ),
        name="attend",
    )(info, query, kv_near, kv_other)


def back_kernel(
    info, query, kv_near, kv_other, grad, out_t, logs,
    dq, dkv, dkv_other,
    q_t, g_t, k_n, k_t, v_n, dq_t, dk_t, dv_t, delta,
):
    width, heads = head_dims(query)
    blocks, rows = q_t.shape[0], q_t.shape[-1]
    seq_len, half = info[0], info[1]
    scale = 1.0 / math.sqrt(HD)
    factor = LOG2E * scale

    def prepare(b, carry):
        at = pl.ds(pl.multiple_of(b * rows, rows), rows)
        query_t = query[at, :].astype(jnp.float32).T
        mine = kv_near[at, :]
        mine_t = mine[:, :width].astype(jnp.float32).T
        grad_t = grad[at, :].astype(jnp.float32).T
        theirs = kv_other[at, :]
        theirs_t = theirs[:, :width].astype(jnp.float32).T
        for h in range(heads):
            lo, hi = h * HD, (h + 1) * HD
            q_t[b, h] = query_t[lo:hi].astype(jnp.bfloat16)
            g_t[b, h] = grad_t[lo:hi].astype(jnp.bfloat16)
            delta[b, h] = jnp.sum(grad_t[lo:hi] * out_t[b, lo:hi], axis=0, keepdims=True)
            k_t[b, h] = mine_t[lo:hi].astype(jnp.bfloat16)
            k_n[b, h] = mine[:, lo:hi]
            v_n[b, h] = mine[:, width + lo : width + hi]
            k_t[blocks + b, h] = theirs_t[lo:hi].astype(jnp.bfloat16)
            k_n[blocks + b, h] = theirs[:, lo:hi]
            v_n[blocks + b, h] = theirs[:, width + lo : width + hi]
        return carry

    lax.fori_loop(0, blocks, prepare, 0)
    dk_t[...] = jnp.zeros_like(dk_t)
    dv_t[...] = jnp.zeros_like(dv_t)

    def block(i, carry):
        dq_t[...] = jnp.zeros_like(dq_t)

        def visit(j, start, diagonal):
            query_start = (2 * i + half) * rows if diagonal else None
            allowed = chunk_mask(start, seq_len, query_start, rows, rows)
            for h in range(heads):
                at = slice(h * HD, (h + 1) * HD)
                s = nn(k_n[j, h], q_t[i, h]) * factor - logs[i, h]
                p = jnp.exp2(jnp.where(allowed, s, MASKED))
                dv_t[j, at] += nt(g_t[i, h], p.astype(jnp.bfloat16))
                dp = nn(v_n[j, h], g_t[i, h])
                ds = (p * (dp - delta[i, h])).astype(jnp.bfloat16)
                dq_t[at] += nn(k_t[j, h], ds)
                dk_t[j, at] += nt(q_t[i, h], ds)

        sweep(i, half, seq_len, rows, visit, blocks)
        at = pl.ds(pl.multiple_of(i * rows, rows), rows)
        dq[at, :] = (dq_t[...] * scale).T.astype(dq.dtype)
        return carry

    lax.fori_loop(0, blocks, block, 0)

    def finish(b, carry):
        at = pl.ds(pl.multiple_of(b * rows, rows), rows)
        dkv[at, :width] = (dk_t[b] * scale).T.astype(dkv.dtype)
        dkv[at, width:] = dv_t[b].T.astype(dkv.dtype)
        dkv_other[at, :width] = (dk_t[blocks + b] * scale).T.astype(dkv_other.dtype)
        dkv_other[at, width:] = dv_t[blocks + b].T.astype(dkv_other.dtype)
        return carry

    lax.fori_loop(0, blocks, finish, 0)


def attend_back(info, query, kv_near, kv_other, grad, out_t, logs, blocks):
    rows_all, width = query.shape
    heads, rows = width // HD, rows_all // blocks
    bf, f32 = jnp.bfloat16, jnp.float32
    pairs = blocks * rows * rows * (blocks + 1)
    return pl.pallas_call(
        back_kernel,
        out_shape=(
            jax.ShapeDtypeStruct((rows_all, width), bf),
            jax.ShapeDtypeStruct((rows_all, 2 * width), bf),
            jax.ShapeDtypeStruct((rows_all, 2 * width), bf),
        ),
        in_specs=[pl.BlockSpec(memory_space=pltpu.SMEM)] + vmem_specs(6),
        out_specs=tuple(vmem_specs(3)),
        scratch_shapes=[
            pltpu.VMEM((blocks, heads, HD, rows), bf),
            pltpu.VMEM((blocks, heads, HD, rows), bf),
            pltpu.VMEM((2 * blocks, heads, rows, HD), bf),
            pltpu.VMEM((2 * blocks, heads, HD, rows), bf),
            pltpu.VMEM((2 * blocks, heads, rows, HD), bf),
            pltpu.VMEM((width, rows), f32),
            pltpu.VMEM((2 * blocks, width, rows), f32),
            pltpu.VMEM((2 * blocks, width, rows), f32),
            pltpu.VMEM((blocks, heads, 1, rows), f32),
        ],
        cost_estimate=pl.CostEstimate(
            flops=60 * 1024 * 1024 * 1024, transcendentals=pairs * heads, bytes_accessed=8 * 1024 * 1024
        ),
        name="attend_back",
    )(info, query, kv_near, kv_other, grad, out_t, logs)


def head_columns(groups, halves, sections, units):
    local, owned = units // groups, sections * units // (groups * halves)
    send = [[[[] for _ in range(groups)] for _ in range(halves)] for _ in range(groups)]
    take = np.zeros((groups, halves, owned, 2), np.int32)
    for u in range(sections * units):
        section, inside = divmod(u, units)
        source, offset = divmod(inside, local)
        owner, place = divmod(u, owned)
        head, ctx = divmod(owner, halves)
        slots = send[source][ctx][head]
        take[head, ctx, place] = (source, len(slots))
        slots.append(section * local + offset)
    width = max(len(x) for a in send for b in a for x in b)
    table = np.zeros((groups, halves, groups, width), np.int32)
    for a in range(groups):
        for b in range(halves):
            for c in range(groups):
                table[a, b, c, : len(send[a][b][c])] = send[a][b][c]
    return table, take


def body(
    inputs,
    dataset_ids,
    lengths,
    dataset_table,
    attn_gain,
    attn_shift,
    qkv_weight,
    query_bias,
    value_bias,
    out_weight,
    out_bias,
    mlp_gain,
    mlp_shift,
    fc_weight,
    fc_bias,
    proj_weight,
    proj_bias,
    cotangent,
):
    cell_count, row_count, model_width = inputs.shape
    cells = lax.axis_size(CELL)
    groups = lax.axis_size(HEAD)
    halves = lax.axis_size(CTX)
    parts = groups * halves
    half_index = lax.axis_index(CTX)
    head_width = HEADS // groups * HD
    token_count = cell_count * row_count
    ctx_rows = groups * row_count
    cell_steps, ctx_steps, head_steps = bits_of(CELL), bits_of(CTX), bits_of(HEAD)[::-1]
    steps_x = cell_steps + ctx_steps + head_steps
    one_hot = (
        dataset_ids[:, None] == jnp.arange(dataset_table.shape[0], dtype=jnp.int32)[None, :]
    ).astype(jnp.bfloat16)
    embedded = jnp.dot(one_hot, dataset_table, preferred_element_type=jnp.float32)
    residual = (inputs.astype(jnp.float32) + embedded[:, None, :]).reshape(token_count, model_width)
    normed = layer_norm(residual, attn_gain, attn_shift).astype(jnp.bfloat16)
    mixed_qkv = jnp.dot(normed, qkv_weight, preferred_element_type=jnp.float32)
    bias_row = jnp.concatenate([query_bias, jnp.zeros_like(query_bias), value_bias])
    mixed_qkv = (mixed_qkv + bias_row).astype(jnp.bfloat16)
    head_index = lax.axis_index(HEAD)

    def to_heads(values):
        sections = values.shape[1] // model_width
        values = values.reshape(cell_count, row_count, sections, groups, head_width)
        values = values.transpose(3, 0, 1, 2, 4).reshape(groups, cell_count, row_count, -1)
        values = lax.all_to_all(values, HEAD, split_axis=0, concat_axis=0, tiled=True)
        return values.transpose(1, 0, 2, 3).reshape(cell_count, ctx_rows, -1)

    def to_rows(values):
        sections = values.shape[-1] // head_width
        values = values.reshape(cell_count, groups, row_count, -1).transpose(1, 0, 2, 3)
        values = lax.all_to_all(values, HEAD, split_axis=0, concat_axis=0, tiled=True)
        values = values.reshape(groups, cell_count, row_count, sections, head_width)
        return values.transpose(1, 2, 3, 0, 4).reshape(token_count, sections * model_width)

    kv_near = to_heads(mixed_qkv[:, model_width:])
    mixed_query, kv_near = lax.optimization_barrier((mixed_qkv[:, :model_width], kv_near))
    kv_other = swap(kv_near, CTX, 1)
    query_heads = to_heads(mixed_query)
    normed_t = normed.T.reshape(cells, model_width // cells, token_count)
    normed_t = jnp.pad(normed_t, ((0, 0), (0, -normed_t.shape[1] % 16), (0, 0)))
    normed_t, query_heads = lax.optimization_barrier(
        (normed_t.reshape(-1, token_count), query_heads)
    )
    pieces = [normed_t]
    for p in range(1, groups):
        pieces.append(swap(normed_t, HEAD, p))
    normed_near = jnp.stack(pieces)
    normed_far = swap(normed_near, CTX, 1)
    infos = [jnp.stack([lengths[n], half_index.astype(jnp.int32)]) for n in range(cell_count)]
    runs = [attend(infos[n], query_heads[n], kv_near[n], kv_other[n], groups) for n in range(cell_count)]
    attended = jnp.stack([r[0] for r in runs])
    attended_rows = to_rows(attended)
    attn_out = jnp.dot(attended_rows, out_weight, preferred_element_type=jnp.float32) + out_bias
    middle = residual + attn_out
    mlp_normed = layer_norm(middle, mlp_gain, mlp_shift).astype(jnp.bfloat16)
    hidden = jnp.dot(mlp_normed, fc_weight, preferred_element_type=jnp.float32) + fc_bias
    active = gelu_tanh(hidden).astype(jnp.bfloat16)
    branch = jnp.dot(active, proj_weight, preferred_element_type=jnp.float32) + proj_bias
    block_out = (middle + branch).astype(jnp.bfloat16).reshape(cell_count, row_count, model_width)
    grad_low = cotangent.reshape(token_count, model_width)
    proj_kept, proj_sent = weight_blocks([(grad_low, active)], False)
    part_columns = model_width // parts
    grad_top = grad_low.astype(jnp.float32)
    proj_bias_grad = jnp.sum(grad_top, axis=0)
    low_tie = [grad_low]
    proj_total = scatter_sum(proj_kept, proj_sent, steps_x, {1: low_tie})
    proj_weight_grad = proj_total[:part_columns].T
    grad_low = low_tie[0]
    active_grad = jnp.einsum("nd,fd->nf", grad_low, proj_weight, preferred_element_type=jnp.float32)
    gelu_pull = jax.vjp(gelu_tanh, hidden)[1]
    hidden_grad = gelu_pull(active_grad)[0].astype(jnp.bfloat16)
    fc_bias_grad = jnp.sum(hidden_grad, axis=0, dtype=jnp.float32)
    normed_grad = jnp.einsum(
        "nf,df->nd", hidden_grad, fc_weight, preferred_element_type=jnp.float32
    )
    mlp_pull = jax.vjp(layer_norm, middle, mlp_gain, mlp_shift)[1]
    middle_part, mlp_gain_grad, mlp_shift_grad = mlp_pull(normed_grad)
    middle_grad = grad_top + middle_part
    middle_low = middle_grad.astype(jnp.bfloat16)
    out_bias_grad = jnp.sum(middle_low, axis=0, dtype=jnp.float32)
    attended_grad = jnp.einsum(
        "ne,de->nd", middle_low, out_weight, preferred_element_type=jnp.float32
    ).astype(jnp.bfloat16)
    grad_heads = to_heads(attended_grad)

    fc_kept, fc_sent = weight_blocks([(mlp_normed, hidden_grad), (attended_rows, middle_low)], True)
    back_tie = [grad_heads]
    fc_out_grad = scatter_sum(fc_kept, fc_sent, steps_x, {1: back_tie})
    grad_heads = back_tie[0]
    fc_out_grad = fc_out_grad[: model_width // cells]
    fc_columns = fc_weight.shape[1] // parts
    fc_weight_grad = fc_out_grad[:, :fc_columns]
    out_weight_grad = fc_out_grad[:, fc_columns:]

    backs = [
      attend_back(
        infos[n], query_heads[n], kv_near[n], kv_other[n], grad_heads[n], runs[n][1], runs[n][2], groups
      )
      for n in range(cell_count)
    ]
    dq = jnp.stack([b[0] for b in backs])
    dkv = jnp.stack([b[1] for b in backs])
    dkv_far = jnp.stack([b[2] for b in backs])

    dkv_got = swap(dkv_far, CTX, 1)
    dq_rows = to_rows(dq)
    qkv_part = qkv_blocks(normed_near, normed_far, dq[0], dkv[0], dkv_far[0])
    half_cells = cells // 2
    qkv_part = scatter_sum(qkv_part[:half_cells], qkv_part[half_cells:], cell_steps)
    qkv_part = qkv_part[: model_width // cells].astype(jnp.bfloat16)
    qkv_part = add_up(qkv_part, swap(qkv_part, CTX, 1)).astype(jnp.bfloat16)
    units = 2 * groups
    qkv_part = qkv_part.reshape(qkv_part.shape[0], 3 * units // groups, -1).transpose(1, 0, 2)
    send_table, take_table = head_columns(groups, halves, 3, units)
    sent = qkv_part[jnp.asarray(send_table)[head_index, half_index]]
    got = lax.all_to_all(sent, HEAD, split_axis=0, concat_axis=0, tiled=True)
    taken = jnp.asarray(take_table)[head_index, half_index]
    qkv_weight_grad = jnp.concatenate(
        [got[taken[n, 0], taken[n, 1]] for n in range(take_table.shape[2])], axis=-1
    ).astype(jnp.float32)

    dkv = add_up(dkv, dkv_got).astype(jnp.bfloat16)
    dkv, dq_rows = lax.optimization_barrier((dkv, dq_rows))
    dkv_rows = to_rows(dkv)
    qkv_grad = jnp.concatenate([dq_rows, dkv_rows], axis=-1)
    column_sums = jnp.sum(qkv_grad, axis=0, dtype=jnp.float32)
    query_bias_grad = column_sums[:model_width]
    value_bias_grad = column_sums[2 * model_width :]
    normed_back = jnp.einsum(
        "ne,de->nd", qkv_grad, qkv_weight, preferred_element_type=jnp.float32
    )
    attn_pull = jax.vjp(layer_norm, residual, attn_gain, attn_shift)[1]
    residual_part, attn_gain_grad, attn_shift_grad = attn_pull(normed_back)
    residual_grad = middle_grad + residual_part
    input_grad = residual_grad.astype(jnp.bfloat16).reshape(cell_count, row_count, model_width)
    cell_totals = jnp.sum(residual_grad.reshape(cell_count, row_count, model_width), axis=1)
    table_grad = jnp.dot(
        one_hot.astype(jnp.float32).T, cell_totals, precision=lax.Precision.HIGHEST
    )

    width = model_width // cells
    vectors = [
        attn_gain_grad,
        attn_shift_grad,
        query_bias_grad,
        value_bias_grad,
        out_bias_grad,
        mlp_gain_grad,
        mlp_shift_grad,
        proj_bias_grad,
    ]
    fc_rows = fc_bias_grad.shape[0] // model_width
    packed = jnp.concatenate(
        [table_grad.reshape(-1, cells, width).transpose(1, 0, 2)]
        + [v.reshape(cells, 1, width) for v in vectors]
        + [fc_bias_grad.reshape(cells, fc_rows, width)],
        axis=1,
    )
    cell_index = lax.axis_index(CELL)
    for axis, bit in cell_steps[::-1]:
        on = (cell_index // bit) % 2
        half = packed.shape[0] // 2
        kept = lax.dynamic_slice_in_dim(packed, on * half, half, 0)
        sent = lax.dynamic_slice_in_dim(packed, (1 - on) * half, half, 0)
        packed = kept + swap(sent, axis, bit)
    for axis, bit in ctx_steps + head_steps:
        packed = packed + swap(packed, axis, bit)
    packed = packed[0]
    datasets = dataset_table.shape[0]
    table_grad = packed[:datasets]
    (
        attn_gain_grad,
        attn_shift_grad,
        query_bias_grad,
        value_bias_grad,
        out_bias_grad,
        mlp_gain_grad,
        mlp_shift_grad,
        proj_bias_grad,
    ) = [packed[datasets + n] for n in range(len(vectors))]
    fc_bias_grad = packed[datasets + len(vectors) :].reshape(-1)
    return (
        block_out,
        input_grad,
        table_grad,
        attn_gain_grad,
        attn_shift_grad,
        qkv_weight_grad,
        query_bias_grad,
        value_bias_grad,
        out_weight_grad,
        out_bias_grad,
        mlp_gain_grad,
        mlp_shift_grad,
        fc_weight_grad,
        fc_bias_grad,
        proj_weight_grad,
        proj_bias_grad,
    )


def solution(mesh):
    in_specs = (
        P(CELL, (HEAD, CTX), None),
        P(CELL),
        P(CELL),
        P(),
        P(),
        P(),
        P(),
        P(),
        P(),
        P(),
        P(),
        P(),
        P(),
        P(),
        P(),
        P(),
        P(),
        P(CELL, (HEAD, CTX), None),
    )
    out_specs = (
        P(CELL, (HEAD, CTX), None),
        P(CELL, (HEAD, CTX), None),
        P(None, CELL),
        P(CELL),
        P(CELL),
        P(CELL, (HEAD, CTX)),
        P(CELL),
        P(CELL),
        P(CELL, (HEAD, CTX)),
        P(CELL),
        P(CELL),
        P(CELL),
        P(CELL, (HEAD, CTX)),
        P(CELL),
        P(CELL, (HEAD, CTX)),
        P(CELL),
    )
    return jax.shard_map(body, mesh=mesh, in_specs=in_specs, out_specs=out_specs, check_vma=False)
```

```python
import math

import jax
import jax.numpy as jnp
from jax import lax
from jax.experimental import pallas as pl
from jax.experimental.pallas import tpu as pltpu
from jax.sharding import PartitionSpec as P
import numpy as np


HEADS = 20
HD = 56


epsilon = 1e-05
MASKED = -1e30
LOG2E = math.log2(math.e)


CELL, HEAD, CTX = "cell", "head", "ctx"


def layer_norm(values, gain_row, shift_row):
    center = values - jnp.mean(values, axis=-1, keepdims=True)
    spread = jnp.mean(center * center, axis=-1, keepdims=True)
    return center * lax.rsqrt(spread + epsilon) * gain_row + shift_row


def gelu_tanh(values):
    return jax.nn.gelu(values, approximate=True)


def swap(values, axis, bit):
    return lax.ppermute(values, axis, [(i, i ^ bit) for i in range(lax.axis_size(axis))])


def bits_of(axis):
    size, bit, found = lax.axis_size(axis), 1, []
    while bit < size:
        found.append((axis, bit))
        bit *= 2
    return found


def nn(a, b):
    return jnp.dot(a, b, preferred_element_type=jnp.float32)


def nt(a, b):
    return lax.dot_general(a, b, (((1,), (1,)), ((), ())), preferred_element_type=jnp.float32)


def relative_order(count, axis_bits):
    rel = np.zeros((count,), np.int32)
    for s, bit in enumerate(axis_bits):
        rel += ((np.arange(count) >> (len(axis_bits) - 1 - s)) & 1).astype(np.int32) * bit
    return jnp.asarray(rel)


def weight_blocks(pairs, by_cell_left):
    cells, groups, halves = lax.axis_size(CELL), lax.axis_size(HEAD), lax.axis_size(CTX)
    parts, half_cells = groups * halves, cells // 2
    cell_ids = relative_order(cells, [b for _, b in bits_of(CELL)]) ^ lax.axis_index(CELL)
    places = jnp.arange(parts, dtype=jnp.int32)
    part_ids = ((places % groups) ^ lax.axis_index(HEAD)) * halves + (
        (places // groups) ^ lax.axis_index(CTX)
    )
    left_ids, right_ids = (cell_ids, part_ids) if by_cell_left else (part_ids, cell_ids)
    left_count, right_count = (cells, parts) if by_cell_left else (parts, cells)
    tokens = pairs[0][0].shape[0]
    left_rows = pairs[0][0].shape[1] // left_count
    rows = left_rows + -left_rows % 16
    widths = [right.shape[1] // right_count for _, right in pairs]
    cols = sum(widths)
    count = len(pairs)

    def kernel(left_at, right_at, *refs):
        sources, (kept, sent), scratch = refs[: 2 * count], refs[2 * count : 2 * count + 2], refs[2 * count + 2 :]
        step = pl.program_id(0)

        @pl.when(step == 0)
        def _():
            turned = scratch[-1]
            turned[...] = jnp.zeros_like(turned)
            for p in range(count):
                left_t = sources[2 * p][...].astype(jnp.float32).T.astype(jnp.bfloat16)
                for n in range(left_count):
                    turned[n, :left_rows] = left_t[n * left_rows : (n + 1) * left_rows]
                for n in range(left_count):
                    scratch[2 * p][n * rows : (n + 1) * rows, :] = turned[left_at[n]]
                width = widths[p]
                for n in range(right_count):
                    scratch[2 * p + 1][n] = sources[2 * p + 1][:, n * width : (n + 1) * width]

        index = step if by_cell_left else (step + half_cells) % cells
        offset = 0
        for p in range(count):
            block = nn(scratch[2 * p][...], scratch[2 * p + 1][right_at[index]])
            at = slice(offset, offset + widths[p])
            offset += widths[p]
            if by_cell_left:
                for n in range(cells):
                    out, place = (kept, n) if n < half_cells else (sent, n - half_cells)
                    out[place, 0, :, at] = block[n * rows : (n + 1) * rows].astype(jnp.bfloat16)
            else:

                def fill(out, block=block, at=at):
                    for n in range(parts):
                        out[0, n, :, at] = block[n * rows : (n + 1) * rows].astype(jnp.bfloat16)

                pl.when(step < half_cells)(lambda: fill(sent))
                pl.when(step >= half_cells)(lambda: fill(kept))

    last = half_cells - 1
    shape = (half_cells, parts, rows, cols)
    if by_cell_left:
        specs = [pl.BlockSpec((half_cells, 1, rows, cols), lambda i, a, b: (0, i, 0, 0))] * 2
    else:
        block_shape = (1, parts, rows, cols)
        specs = [
            pl.BlockSpec(block_shape, lambda i, a, b: (jnp.maximum(i - last - 1, 0), 0, 0, 0)),
            pl.BlockSpec(block_shape, lambda i, a, b: (jnp.minimum(i, last), 0, 0, 0)),
        ]
    scratch = []
    for width in widths:
        scratch.append(pltpu.VMEM((left_count * rows, tokens), jnp.bfloat16))
        scratch.append(pltpu.VMEM((right_count, tokens, width), jnp.bfloat16))
    scratch.append(pltpu.VMEM((left_count, rows, tokens), jnp.bfloat16))
    flat = [x for pair in pairs for x in pair]
    kept, sent = pl.pallas_call(
        kernel,
        out_shape=[jax.ShapeDtypeStruct(shape, jnp.bfloat16)] * 2,
        grid_spec=pltpu.PrefetchScalarGridSpec(
            num_scalar_prefetch=2,
            grid=(right_count,),
            in_specs=[
                pl.BlockSpec(x.shape, lambda i, a, b: (0, 0), pipeline_mode=pl.Buffered(1))
                for x in flat
            ],
            out_specs=specs,
            scratch_shapes=scratch,
        ),
        name="wb",
    )(left_ids, right_ids, *flat)
    return kept.reshape(-1, rows, cols), sent.reshape(-1, rows, cols)


def qkv_blocks(near, far, dq, dkv, dkv_far):
    cells = lax.axis_size(CELL)
    steps = [b for _, b in bits_of(CELL)]
    rel = np.zeros((cells,), np.int32)
    for s, bit in enumerate(steps):
        rel += ((np.arange(cells) >> (len(steps) - 1 - s)) & 1).astype(np.int32) * bit
    place_at = jnp.asarray(np.argsort(rel).astype(np.int32))[
        jnp.arange(cells, dtype=jnp.int32) ^ lax.axis_index(CELL)
    ]
    pieces, wide, tokens = near.shape
    rows = wide // cells
    width = dq.shape[1]
    row_at = (jnp.arange(pieces, dtype=jnp.int32) ^ lax.axis_index(HEAD)) * tokens

    def kernel(place, row, near_ref, far_ref, dq_ref, dkv_ref, far_grad, out, tall, q, kv):
        for p in range(pieces):
            at = pl.ds(pl.multiple_of(row[p], tokens), tokens)
            here, there = slice(p * tokens, (p + 1) * tokens), slice(
                (pieces + p) * tokens, (pieces + p + 1) * tokens
            )
            tall[:, here] = near_ref[p]
            tall[:, there] = far_ref[p]
            q[here, :] = dq_ref[at, :]
            kv[here, :] = dkv_ref[at, :]
            kv[there, :] = far_grad[at, :]
        for a in range(cells):
            left = tall[a * rows : (a + 1) * rows, :]
            out[place[a], :, :width] = nn(left[:, : pieces * tokens], q[...]).astype(jnp.bfloat16)
            out[place[a], :, width:] = nn(left, kv[...]).astype(jnp.bfloat16)

    smem = pl.BlockSpec(memory_space=pltpu.SMEM)
    return pl.pallas_call(
        kernel,
        out_shape=jax.ShapeDtypeStruct((cells, rows, 3 * width), jnp.bfloat16),
        in_specs=[smem, smem] + vmem_specs(5),
        out_specs=vmem_specs(1)[0],
        scratch_shapes=[
            pltpu.VMEM((wide, 2 * pieces * tokens), jnp.bfloat16),
            pltpu.VMEM((pieces * tokens, width), jnp.bfloat16),
            pltpu.VMEM((2 * pieces * tokens, 2 * width), jnp.bfloat16),
        ],
        name="qb",
    )(place_at, row_at, near, far, dq, dkv, dkv_far)


def add_up(*terms):
    total = terms[0].astype(jnp.float32)
    for term in terms[1:]:
        total = total + term.astype(jnp.float32)
    return total


def scatter_sum(kept, sent, steps, ties=None):
    ties = ties or {}
    terms = [kept]
    for s, (axis, bit) in enumerate(steps):
        if s:
            half = terms[0].shape[0] // 2
            sent = add_up(*[t[half:] for t in terms]).astype(jnp.bfloat16)
            terms = [t[:half] for t in terms]
        if s in ties:
            sent, ties[s][0] = lax.optimization_barrier((sent, ties[s][0]))
        terms.append(swap(sent, axis, bit))
    return add_up(*terms)[0]


def head_dims(query):
    width = query.shape[-1]
    return width, width // HD


def chunk_mask(start, seq_len, query_start, rows, cols):
    key_pos = start + lax.broadcasted_iota(jnp.int32, (rows, cols), 0)
    if query_start is None:
        return key_pos < seq_len
    query_pos = query_start + lax.broadcasted_iota(jnp.int32, (rows, cols), 1)
    return (key_pos < seq_len) & (key_pos <= query_pos)


def sweep(i, half, seq_len, rows, visit, blocks):
    def own(j):
        return j, (2 * j + half) * rows

    def other(j):
        return blocks + j, (2 * j + 1 - half) * rows

    def run(low, high, *kinds):
        def step(j, carry):
            visit([kind(j) for kind in kinds], False)
            return carry

        lax.fori_loop(low, high, step, 0)

    span = 2 * rows
    own_count = jnp.minimum(i, (seq_len - half * rows + span - 1) // span)
    other_count = jnp.minimum(i + half, (seq_len - (1 - half) * rows + span - 1) // span)
    both = jnp.minimum(own_count, other_count)
    run(0, both, own, other)
    run(both, other_count, other)
    run(both, own_count, own)
    visit([own(i)], True)


def attend_kernel(info, query, kv_near, kv_other, out, out_t, logs, q_t, k_n, v_t, acc, m_ref, l_ref):
    width, heads = head_dims(query)
    blocks, rows = q_t.shape[0], q_t.shape[-1]
    seq_len, half = info[0], info[1]
    factor = LOG2E / math.sqrt(HD)

    def prepare(b, carry):
        at = pl.ds(pl.multiple_of(b * rows, rows), rows)
        query_t = query[at, :].astype(jnp.float32).T
        mine = kv_near[at, :]
        mine_t = mine[:, width:].astype(jnp.float32).T
        theirs = kv_other[at, :]
        theirs_t = theirs[:, width:].astype(jnp.float32).T
        for h in range(heads):
            lo, hi = h * HD, (h + 1) * HD
            q_t[b, h] = query_t[lo:hi].astype(jnp.bfloat16)
            v_t[b, h] = mine_t[lo:hi].astype(jnp.bfloat16)
            k_n[b, h] = mine[:, lo:hi]
            v_t[blocks + b, h] = theirs_t[lo:hi].astype(jnp.bfloat16)
            k_n[blocks + b, h] = theirs[:, lo:hi]
        return carry

    lax.fori_loop(0, blocks, prepare, 0)

    def block(i, carry):
        acc[...] = jnp.zeros_like(acc)
        m_ref[...] = jnp.full_like(m_ref, MASKED)
        l_ref[...] = jnp.zeros_like(l_ref)

        def visit(chunks, diagonal):
            query_start = (2 * i + half) * rows if diagonal else None
            allowed = [chunk_mask(at, seq_len, query_start, rows, rows) for _, at in chunks]
            for h in range(heads):
                old = m_ref[h]
                new, scores = old, []
                for (j, _), mask in zip(chunks, allowed):
                    s = nn(k_n[j, h], q_t[i, h]) * factor
                    s = jnp.where(mask, s, MASKED)
                    scores.append(s)
                    new = jnp.maximum(new, jnp.max(s, axis=0, keepdims=True))
                shrink = jnp.exp2(old - new)
                total, result = l_ref[h] * shrink, acc[h] * shrink
                for (j, _), s in zip(chunks, scores):
                    p = jnp.exp2(s - new)
                    total = total + jnp.sum(p, axis=0, keepdims=True)
                    result = result + nn(v_t[j, h], p.astype(jnp.bfloat16))
                l_ref[h] = total
                acc[h] = result
                m_ref[h] = new

        sweep(i, half, seq_len, rows, visit, blocks)
        at = pl.ds(pl.multiple_of(i * rows, rows), rows)
        for h in range(heads):
            out_t[i, h * HD : (h + 1) * HD, :] = acc[h] / l_ref[h]
            logs[i, h] = m_ref[h] + jnp.log2(l_ref[h])
        out[at, :] = out_t[i].T.astype(jnp.bfloat16)
        return carry

    lax.fori_loop(0, blocks, block, 0)


def vmem_specs(count):
    return [pl.BlockSpec(memory_space=pltpu.VMEM)] * count


def attend(info, query, kv_near, kv_other, blocks):
    rows_all, width = query.shape
    heads, rows = width // HD, rows_all // blocks
    bf, f32 = jnp.bfloat16, jnp.float32
    pairs = blocks * rows * rows * (blocks + 1)
    return pl.pallas_call(
        attend_kernel,
        out_shape=(
            jax.ShapeDtypeStruct((rows_all, width), bf),
            jax.ShapeDtypeStruct((blocks, width, rows), f32),
            jax.ShapeDtypeStruct((blocks, heads, 1, rows), f32),
        ),
        in_specs=[pl.BlockSpec(memory_space=pltpu.SMEM)] + vmem_specs(3),
        out_specs=tuple(vmem_specs(3)),
        scratch_shapes=[
            pltpu.VMEM((blocks, heads, HD, rows), bf),
            pltpu.VMEM((2 * blocks, heads, rows, HD), bf),
            pltpu.VMEM((2 * blocks, heads, HD, rows), bf),
            pltpu.VMEM((heads, HD, rows), f32),
            pltpu.VMEM((heads, 1, rows), f32),
            pltpu.VMEM((heads, 1, rows), f32),
        ],
        cost_estimate=pl.CostEstimate(
            flops=20 * 1024 * 1024 * 1024, transcendentals=pairs * heads, bytes_accessed=8 * 1024 * 1024
        ),
        name="attend",
    )(info, query, kv_near, kv_other)


def back_kernel(
    info, query, kv_near, kv_other, grad, out_t, logs,
    dq, dkv, dkv_other,
    q_t, g_t, k_n, k_t, v_n, dq_t, dk_t, dv_t, delta,
):
    width, heads = head_dims(query)
    blocks, rows = q_t.shape[0], q_t.shape[-1]
    seq_len, half = info[0], info[1]
    scale = 1.0 / math.sqrt(HD)
    factor = LOG2E * scale

    def prepare(b, carry):
        at = pl.ds(pl.multiple_of(b * rows, rows), rows)
        query_t = query[at, :].astype(jnp.float32).T
        mine = kv_near[at, :]
        mine_t = mine[:, :width].astype(jnp.float32).T
        grad_t = grad[at, :].astype(jnp.float32).T
        theirs = kv_other[at, :]
        theirs_t = theirs[:, :width].astype(jnp.float32).T
        for h in range(heads):
            lo, hi = h * HD, (h + 1) * HD
            q_t[b, h] = query_t[lo:hi].astype(jnp.bfloat16)
            g_t[b, h] = grad_t[lo:hi].astype(jnp.bfloat16)
            delta[b, h] = jnp.sum(grad_t[lo:hi] * out_t[b, lo:hi], axis=0, keepdims=True)
            k_t[b, h] = mine_t[lo:hi].astype(jnp.bfloat16)
            k_n[b, h] = mine[:, lo:hi]
            v_n[b, h] = mine[:, width + lo : width + hi]
            k_t[blocks + b, h] = theirs_t[lo:hi].astype(jnp.bfloat16)
            k_n[blocks + b, h] = theirs[:, lo:hi]
            v_n[blocks + b, h] = theirs[:, width + lo : width + hi]
        return carry

    lax.fori_loop(0, blocks, prepare, 0)
    dk_t[...] = jnp.zeros_like(dk_t)
    dv_t[...] = jnp.zeros_like(dv_t)

    def block(i, carry):
        dq_t[...] = jnp.zeros_like(dq_t)

        def visit(chunks, diagonal):
            query_start = (2 * i + half) * rows if diagonal else None
            allowed = [chunk_mask(at, seq_len, query_start, rows, rows) for _, at in chunks]
            for h in range(heads):
                at = slice(h * HD, (h + 1) * HD)
                for (j, _), mask in zip(chunks, allowed):
                    s = nn(k_n[j, h], q_t[i, h]) * factor - logs[i, h]
                    p = jnp.exp2(jnp.where(mask, s, MASKED))
                    dv_t[j, at] += nt(g_t[i, h], p.astype(jnp.bfloat16))
                    dp = nn(v_n[j, h], g_t[i, h])
                    ds = (p * (dp - delta[i, h])).astype(jnp.bfloat16)
                    dq_t[at] += nn(k_t[j, h], ds)
                    dk_t[j, at] += nt(q_t[i, h], ds)

        sweep(i, half, seq_len, rows, visit, blocks)
        at = pl.ds(pl.multiple_of(i * rows, rows), rows)
        dq[at, :] = (dq_t[...] * scale).T.astype(dq.dtype)
        return carry

    lax.fori_loop(0, blocks, block, 0)

    def finish(b, carry):
        at = pl.ds(pl.multiple_of(b * rows, rows), rows)
        dkv[at, :width] = (dk_t[b] * scale).T.astype(dkv.dtype)
        dkv[at, width:] = dv_t[b].T.astype(dkv.dtype)
        dkv_other[at, :width] = (dk_t[blocks + b] * scale).T.astype(dkv_other.dtype)
        dkv_other[at, width:] = dv_t[blocks + b].T.astype(dkv_other.dtype)
        return carry

    lax.fori_loop(0, blocks, finish, 0)


def attend_back(info, query, kv_near, kv_other, grad, out_t, logs, blocks):
    rows_all, width = query.shape
    heads, rows = width // HD, rows_all // blocks
    bf, f32 = jnp.bfloat16, jnp.float32
    pairs = blocks * rows * rows * (blocks + 1)
    return pl.pallas_call(
        back_kernel,
        out_shape=(
            jax.ShapeDtypeStruct((rows_all, width), bf),
            jax.ShapeDtypeStruct((rows_all, 2 * width), bf),
            jax.ShapeDtypeStruct((rows_all, 2 * width), bf),
        ),
        in_specs=[pl.BlockSpec(memory_space=pltpu.SMEM)] + vmem_specs(6),
        out_specs=tuple(vmem_specs(3)),
        scratch_shapes=[
            pltpu.VMEM((blocks, heads, HD, rows), bf),
            pltpu.VMEM((blocks, heads, HD, rows), bf),
            pltpu.VMEM((2 * blocks, heads, rows, HD), bf),
            pltpu.VMEM((2 * blocks, heads, HD, rows), bf),
            pltpu.VMEM((2 * blocks, heads, rows, HD), bf),
            pltpu.VMEM((width, rows), f32),
            pltpu.VMEM((2 * blocks, width, rows), f32),
            pltpu.VMEM((2 * blocks, width, rows), f32),
            pltpu.VMEM((blocks, heads, 1, rows), f32),
        ],
        cost_estimate=pl.CostEstimate(
            flops=60 * 1024 * 1024 * 1024, transcendentals=pairs * heads, bytes_accessed=8 * 1024 * 1024
        ),
        name="attend_back",
    )(info, query, kv_near, kv_other, grad, out_t, logs)


def head_columns(groups, halves, sections, units):
    local, owned = units // groups, sections * units // (groups * halves)
    send = [[[[] for _ in range(groups)] for _ in range(halves)] for _ in range(groups)]
    take = np.zeros((groups, halves, owned, 2), np.int32)
    for u in range(sections * units):
        section, inside = divmod(u, units)
        source, offset = divmod(inside, local)
        owner, place = divmod(u, owned)
        head, ctx = divmod(owner, halves)
        slots = send[source][ctx][head]
        take[head, ctx, place] = (source, len(slots))
        slots.append(section * local + offset)
    width = max(len(x) for a in send for b in a for x in b)
    table = np.zeros((groups, halves, groups, width), np.int32)
    for a in range(groups):
        for b in range(halves):
            for c in range(groups):
                table[a, b, c, : len(send[a][b][c])] = send[a][b][c]
    return table, take


def body(
    inputs,
    dataset_ids,
    lengths,
    dataset_table,
    attn_gain,
    attn_shift,
    qkv_weight,
    query_bias,
    value_bias,
    out_weight,
    out_bias,
    mlp_gain,
    mlp_shift,
    fc_weight,
    fc_bias,
    proj_weight,
    proj_bias,
    cotangent,
):
    cell_count, row_count, model_width = inputs.shape
    cells = lax.axis_size(CELL)
    groups = lax.axis_size(HEAD)
    halves = lax.axis_size(CTX)
    parts = groups * halves
    half_index = lax.axis_index(CTX)
    head_width = HEADS // groups * HD
    token_count = cell_count * row_count
    ctx_rows = groups * row_count
    cell_steps, ctx_steps, head_steps = bits_of(CELL), bits_of(CTX), bits_of(HEAD)[::-1]
    steps_x = cell_steps + ctx_steps + head_steps
    one_hot = (
        dataset_ids[:, None] == jnp.arange(dataset_table.shape[0], dtype=jnp.int32)[None, :]
    ).astype(jnp.bfloat16)
    embedded = jnp.dot(one_hot, dataset_table, preferred_element_type=jnp.float32)
    residual = (inputs.astype(jnp.float32) + embedded[:, None, :]).reshape(token_count, model_width)
    normed = layer_norm(residual, attn_gain, attn_shift).astype(jnp.bfloat16)
    mixed_qkv = jnp.dot(normed, qkv_weight, preferred_element_type=jnp.float32)
    bias_row = jnp.concatenate([query_bias, jnp.zeros_like(query_bias), value_bias])
    mixed_qkv = (mixed_qkv + bias_row).astype(jnp.bfloat16)
    head_index = lax.axis_index(HEAD)

    def to_heads(values):
        sections = values.shape[1] // model_width
        values = values.reshape(cell_count, row_count, sections, groups, head_width)
        values = values.transpose(3, 0, 1, 2, 4).reshape(groups, cell_count, row_count, -1)
        values = lax.all_to_all(values, HEAD, split_axis=0, concat_axis=0, tiled=True)
        return values.transpose(1, 0, 2, 3).reshape(cell_count, ctx_rows, -1)

    def to_rows(values):
        sections = values.shape[-1] // head_width
        values = values.reshape(cell_count, groups, row_count, -1).transpose(1, 0, 2, 3)
        values = lax.all_to_all(values, HEAD, split_axis=0, concat_axis=0, tiled=True)
        values = values.reshape(groups, cell_count, row_count, sections, head_width)
        return values.transpose(1, 2, 3, 0, 4).reshape(token_count, sections * model_width)

    kv_near = to_heads(mixed_qkv[:, model_width:])
    mixed_query, kv_near = lax.optimization_barrier((mixed_qkv[:, :model_width], kv_near))
    kv_other = swap(kv_near, CTX, 1)
    query_heads = to_heads(mixed_query)
    normed_t = normed.T.reshape(cells, model_width // cells, token_count)
    normed_t = jnp.pad(normed_t, ((0, 0), (0, -normed_t.shape[1] % 16), (0, 0)))
    normed_t, query_heads = lax.optimization_barrier(
        (normed_t.reshape(-1, token_count), query_heads)
    )
    pieces = [normed_t]
    for p in range(1, groups):
        pieces.append(swap(normed_t, HEAD, p))
    infos = [jnp.stack([lengths[n], half_index.astype(jnp.int32)]) for n in range(cell_count)]
    runs = [attend(infos[n], query_heads[n], kv_near[n], kv_other[n], groups) for n in range(cell_count)]
    attended = jnp.stack([r[0] for r in runs])
    attended_rows = to_rows(attended)
    attn_out = jnp.dot(attended_rows, out_weight, preferred_element_type=jnp.float32) + out_bias
    middle = residual + attn_out
    mlp_normed = layer_norm(middle, mlp_gain, mlp_shift).astype(jnp.bfloat16)
    hidden = jnp.dot(mlp_normed, fc_weight, preferred_element_type=jnp.float32) + fc_bias
    active = gelu_tanh(hidden).astype(jnp.bfloat16)
    branch = jnp.dot(active, proj_weight, preferred_element_type=jnp.float32) + proj_bias
    block_out = (middle + branch).astype(jnp.bfloat16).reshape(cell_count, row_count, model_width)
    grad_low = cotangent.reshape(token_count, model_width)
    proj_kept, proj_sent = weight_blocks([(grad_low, active)], False)
    part_columns = model_width // parts
    grad_top = grad_low.astype(jnp.float32)
    proj_bias_grad = jnp.sum(grad_top, axis=0)
    low_tie = [grad_low]
    proj_total = scatter_sum(proj_kept, proj_sent, steps_x, {1: low_tie})
    proj_weight_grad = proj_total[:part_columns].T
    grad_low = low_tie[0]
    active_grad = jnp.einsum("nd,fd->nf", grad_low, proj_weight, preferred_element_type=jnp.float32)
    gelu_pull = jax.vjp(gelu_tanh, hidden)[1]
    hidden_grad = gelu_pull(active_grad)[0].astype(jnp.bfloat16)
    fc_bias_grad = jnp.sum(hidden_grad, axis=0, dtype=jnp.float32)
    normed_grad = jnp.einsum(
        "nf,df->nd", hidden_grad, fc_weight, preferred_element_type=jnp.float32
    )
    mlp_pull = jax.vjp(layer_norm, middle, mlp_gain, mlp_shift)[1]
    middle_part, mlp_gain_grad, mlp_shift_grad = mlp_pull(normed_grad)
    middle_grad = grad_top + middle_part
    middle_low = middle_grad.astype(jnp.bfloat16)
    out_bias_grad = jnp.sum(middle_low, axis=0, dtype=jnp.float32)
    attended_grad = jnp.einsum(
        "ne,de->nd", middle_low, out_weight, preferred_element_type=jnp.float32
    ).astype(jnp.bfloat16)
    held = lax.optimization_barrier((attended_grad, *pieces))
    attended_grad, pieces = held[0], held[1:]
    normed_near = jnp.stack(pieces)
    normed_far = swap(normed_near, CTX, 1)
    grad_heads = to_heads(attended_grad)

    fc_kept, fc_sent = weight_blocks([(mlp_normed, hidden_grad), (attended_rows, middle_low)], True)
    back_tie = [grad_heads]
    fc_out_grad = scatter_sum(fc_kept, fc_sent, steps_x, {1: back_tie})
    grad_heads = back_tie[0]
    fc_out_grad = fc_out_grad[: model_width // cells]
    fc_columns = fc_weight.shape[1] // parts
    fc_weight_grad = fc_out_grad[:, :fc_columns]
    out_weight_grad = fc_out_grad[:, fc_columns:]

    backs = [
      attend_back(
        infos[n], query_heads[n], kv_near[n], kv_other[n], grad_heads[n], runs[n][1], runs[n][2], groups
      )
      for n in range(cell_count)
    ]
    dq = jnp.stack([b[0] for b in backs])
    dkv = jnp.stack([b[1] for b in backs])
    dkv_far = jnp.stack([b[2] for b in backs])

    dkv_got = swap(dkv_far, CTX, 1)
    dq_rows = to_rows(dq)
    qkv_part = qkv_blocks(normed_near, normed_far, dq[0], dkv[0], dkv_far[0])
    half_cells = cells // 2
    qkv_part = scatter_sum(qkv_part[:half_cells], qkv_part[half_cells:], cell_steps)
    qkv_part = qkv_part[: model_width // cells].astype(jnp.bfloat16)
    qkv_part = add_up(qkv_part, swap(qkv_part, CTX, 1)).astype(jnp.bfloat16)
    units = 2 * groups
    qkv_part = qkv_part.reshape(qkv_part.shape[0], 3 * units // groups, -1).transpose(1, 0, 2)
    send_table, take_table = head_columns(groups, halves, 3, units)
    sent = qkv_part[jnp.asarray(send_table)[head_index, half_index]]
    got = lax.all_to_all(sent, HEAD, split_axis=0, concat_axis=0, tiled=True)
    taken = jnp.asarray(take_table)[head_index, half_index]
    qkv_weight_grad = jnp.concatenate(
        [got[taken[n, 0], taken[n, 1]] for n in range(take_table.shape[2])], axis=-1
    ).astype(jnp.float32)

    dkv = add_up(dkv, dkv_got).astype(jnp.bfloat16)
    dkv, dq_rows = lax.optimization_barrier((dkv, dq_rows))
    dkv_rows = to_rows(dkv)
    qkv_grad = jnp.concatenate([dq_rows, dkv_rows], axis=-1)
    column_sums = jnp.sum(qkv_grad, axis=0, dtype=jnp.float32)
    query_bias_grad = column_sums[:model_width]
    value_bias_grad = column_sums[2 * model_width :]
    normed_back = jnp.einsum(
        "ne,de->nd", qkv_grad, qkv_weight, preferred_element_type=jnp.float32
    )
    attn_pull = jax.vjp(layer_norm, residual, attn_gain, attn_shift)[1]
    residual_part, attn_gain_grad, attn_shift_grad = attn_pull(normed_back)
    residual_grad = middle_grad + residual_part
    input_grad = residual_grad.astype(jnp.bfloat16).reshape(cell_count, row_count, model_width)
    cell_totals = jnp.sum(residual_grad.reshape(cell_count, row_count, model_width), axis=1)
    table_grad = jnp.dot(
        one_hot.astype(jnp.float32).T, cell_totals, precision=lax.Precision.HIGHEST
    )

    width = model_width // cells
    vectors = [
        attn_gain_grad,
        attn_shift_grad,
        query_bias_grad,
        value_bias_grad,
        out_bias_grad,
        mlp_gain_grad,
        mlp_shift_grad,
        proj_bias_grad,
    ]
    fc_rows = fc_bias_grad.shape[0] // model_width
    packed = jnp.concatenate(
        [table_grad.reshape(-1, cells, width).transpose(1, 0, 2)]
        + [v.reshape(cells, 1, width) for v in vectors]
        + [fc_bias_grad.reshape(cells, fc_rows, width)],
        axis=1,
    )
    cell_index = lax.axis_index(CELL)
    for axis, bit in cell_steps[::-1]:
        on = (cell_index // bit) % 2
        half = packed.shape[0] // 2
        kept = lax.dynamic_slice_in_dim(packed, on * half, half, 0)
        sent = lax.dynamic_slice_in_dim(packed, (1 - on) * half, half, 0)
        packed = kept + swap(sent, axis, bit)
    for axis, bit in ctx_steps + head_steps:
        packed = packed + swap(packed, axis, bit)
    packed = packed[0]
    datasets = dataset_table.shape[0]
    table_grad = packed[:datasets]
    (
        attn_gain_grad,
        attn_shift_grad,
        query_bias_grad,
        value_bias_grad,
        out_bias_grad,
        mlp_gain_grad,
        mlp_shift_grad,
        proj_bias_grad,
    ) = [packed[datasets + n] for n in range(len(vectors))]
    fc_bias_grad = packed[datasets + len(vectors) :].reshape(-1)
    return (
        block_out,
        input_grad,
        table_grad,
        attn_gain_grad,
        attn_shift_grad,
        qkv_weight_grad,
        query_bias_grad,
        value_bias_grad,
        out_weight_grad,
        out_bias_grad,
        mlp_gain_grad,
        mlp_shift_grad,
        fc_weight_grad,
        fc_bias_grad,
        proj_weight_grad,
        proj_bias_grad,
    )


def solution(mesh):
    in_specs = (
        P(CELL, (HEAD, CTX), None),
        P(CELL),
        P(CELL),
        P(),
        P(),
        P(),
        P(),
        P(),
        P(),
        P(),
        P(),
        P(),
        P(),
        P(),
        P(),
        P(),
        P(),
        P(CELL, (HEAD, CTX), None),
    )
    out_specs = (
        P(CELL, (HEAD, CTX), None),
        P(CELL, (HEAD, CTX), None),
        P(None, CELL),
        P(CELL),
        P(CELL),
        P(CELL, (HEAD, CTX)),
        P(CELL),
        P(CELL),
        P(CELL, (HEAD, CTX)),
        P(CELL),
        P(CELL),
        P(CELL),
        P(CELL, (HEAD, CTX)),
        P(CELL),
        P(CELL, (HEAD, CTX)),
        P(CELL),
    )
    return jax.shard_map(body, mesh=mesh, in_specs=in_specs, out_specs=out_specs, check_vma=False)
```
